128 devices in a mesh: seq: 32 (over x, y, core), mp: 4 (over z).
Axes of the slice: x: 4, y: 4, z: 4, core: 2. Of those that a mesh axis runs over, the one named last changes fastest.
Arguments:
- q_in: bfloat16 [12288, 8192], P('seq', 'mp'), may hold values from -6 to 6
- k_in: bfloat16 [12288, 8192], P('seq', 'mp'), may hold values from -6 to 6
- v_in: bfloat16 [12288, 8192], P('seq', 'mp'), may hold values from -6 to 6
- dest_pos: int32 [12288], replicated, may hold values from -1 to 8191, as said below
- doc_ids: int32 [8192], replicated, may hold values from 0 to 63, never falling along the last dimension, each value on 1 to 512 neighbouring positions
- mr_filter: float32 [128, 8192], P(None, 'mp')
- norm_gain: float32 [8192], P('mp'), may hold values from 0.5 to 1.5
- residual: bfloat16 [8192, 8192], P('seq', 'mp')
- cotangent: bfloat16 [8192, 8192], P('seq', 'mp'), may hold values from -6 to 6
Outputs:
- normed: bfloat16 [8192, 8192], P('seq', 'mp')
- d_residual: bfloat16 [8192, 8192], P('seq', 'mp')
- d_q_in: bfloat16 [12288, 8192], P('seq', 'mp')
- d_k_in: bfloat16 [12288, 8192], P('seq', 'mp')
- d_v_in: bfloat16 [12288, 8192], P('seq', 'mp')
- d_filter: float32 [128, 8192], P(None, 'mp')
- d_gain: float32 [8192], P('mp')
The draws below stay inside these ranges and needn't reach their ends.
Inputs may be any that keep to these rules, and one draw needn't show every extreme that they name: `dest_pos`: every position 0 .. 8191 stands in exactly one slot; all other slots hold -1. The 384 slots of one index of seq hold at most 16 positions of the 256 positions owned by any one index of seq; that bound is reached in every draw, and some index of seq has no slot holding -1. `doc_ids`: ids never fall along the positions; every document covers 1 to 512 positions, one exactly 512.
All inputs are finite; a program needn't handle non-finite values.
Results may differ from the reference program's by a relative error of at most 0.012.
Values may be sent and summed in bfloat16 or wider, within the bound.
No kernel may reach another device: no remote copies, remote signals or barrier semaphores. Data moves between devices by JAX's collectives and lax.ppermute only.
A program may use at most 256 MiB of HBM per device.

```python
import math
import jax
import jax.numpy as jnp
import numpy as np
from jax import lax

D = 8192
L = 128
TOKEN_DEV = 256
TOKENS = 8192
ARR = 384
NDOCS = 64
N_SEQ = 32


def draw_dest_pos(key, part):
    shard_count = TOKENS // TOKEN_DEV
    half_count = shard_count // 2
    piece_rows = TOKEN_DEV // shard_count
    key_list = jax.random.split(key, 5)
    pair_perm = jax.random.permutation(key_list[0], half_count).astype(jnp.int32)
    single_perm = jax.random.permutation(key_list[1], shard_count).astype(jnp.int32)
    dest_index = jnp.arange(shard_count, dtype=jnp.int32)[:, None]
    piece_index = jnp.arange(shard_count, dtype=jnp.int32)[None, :]
    shift_by = jnp.where(dest_index % 2 == 0, 2 * pair_perm[piece_index // 2], single_perm[piece_index])
    source_table = (dest_index + shift_by) % shard_count
    local_scores = jax.random.randint(key_list[2], (shard_count, TOKEN_DEV), 0, 65536) * TOKEN_DEV + jnp.arange(TOKEN_DEV, dtype=jnp.int32)[None, :]
    local_order = jnp.argsort(local_scores, axis=1).astype(jnp.int32)
    position = (dest_index * TOKEN_DEV + local_order).reshape(-1)
    row_source = jnp.repeat(source_table, piece_rows, axis=1).reshape(-1)
    shuffle_rank = jax.random.permutation(key_list[3], TOKENS).astype(jnp.int32)
    order_index = jnp.argsort(row_source * TOKENS + shuffle_rank)
    source_sorted = row_source[order_index]
    position_sorted = position[order_index]
    source_counts = jnp.sum((row_source[:, None] == jnp.arange(shard_count, dtype=jnp.int32)[None, :]).astype(jnp.int32), axis=0)
    source_starts = jnp.cumsum(source_counts) - source_counts
    rank_within = jnp.arange(TOKENS, dtype=jnp.int32) - source_starts[source_sorted]
    slot_scores = jax.random.randint(key_list[4], (shard_count, ARR), 0, 65536) * ARR + jnp.arange(ARR, dtype=jnp.int32)[None, :]
    slot_perm = jnp.argsort(slot_scores, axis=1).astype(jnp.int32)
    slot_taken = slot_perm[source_sorted, rank_within]
    filled = jnp.full((shard_count * ARR,), -1, jnp.int32)
    return filled.at[source_sorted * ARR + slot_taken].set(position_sorted.astype(jnp.int32))


def draw_mr_filter(key, part):
    key_noise, key_span = jax.random.split(key)
    lag_pos = jnp.arange(L, dtype=jnp.float32)[:, None]
    noise_base = jnp.clip(jax.random.normal(key_noise, (L, D), jnp.float32), -5.0, 5.0)
    decay_span = jnp.exp(jax.random.uniform(key_span, (1, D), jnp.float32, math.log(16.0), math.log(400.0)))
    return noise_base * jnp.exp(-lag_pos / decay_span) * jnp.sqrt(2.0 / jnp.minimum(decay_span, float(L)))


def draw_residual(key, part):
    key_rows, key_cols, key_noise = jax.random.split(key, 3)
    rising = jnp.arange(D, dtype=jnp.float32)[None, :] / D
    col_scale = jnp.exp(math.log(0.5) + math.log(6.0) * rising + jax.random.uniform(key_cols, (1, D), jnp.float32, -0.4, 0.4))
    row_scale = jnp.exp(jax.random.uniform(key_rows, (TOKENS, 1), jnp.float32, math.log(0.3), math.log(3.0)))
    noise_base = jnp.clip(jax.random.normal(key_noise, (TOKENS, D), jnp.float32), -5.0, 5.0)
    return (noise_base * row_scale * col_scale).astype(jnp.bfloat16)


def block_levels(own_key, dims, pieces, least, largest):
    loudness, own = 1.0, jax.random.fold_in(own_key, 6)
    for axis_at, blocks in pieces:
        steps = jnp.exp(jax.random.uniform(jax.random.fold_in(own, axis_at), (blocks,), jnp.float32, least / len(pieces), largest / len(pieces)))
        loudness = loudness * jnp.repeat(steps, dims[axis_at] // blocks).reshape([-1 if axis == axis_at else 1 for axis in range(len(dims))])
    return loudness


def profile(amount, total, limit, slope):
    loads = [(1 << 20) // math.isqrt(standing ** slope) + 1 for standing in range(2, amount + 1)]
    surplus, counts = total - limit - (amount - 1), [1] * (amount - 1)
    while surplus > 0:
        free = [i for i in range(amount - 1) if counts[i] < limit]
        whole, budget = sum([loads[i] for i in free]), surplus
        for i in free:
            extra = min(limit - counts[i], max(1, budget * loads[i] // whole), surplus)
            counts[i] = counts[i] + extra
            surplus = surplus - extra
    return np.array([limit] + counts)


def uneven_parts(stream_key, amount, total, most, lean):
    if amount == 2:
        one = jax.random.randint(stream_key, (), max(1, total - most), min(most, total - 1) + 1)
        return jnp.stack([one, total - one])
    lengths = jnp.asarray(profile(amount, total, most, lean), jnp.int32)
    pairs = (amount - 1) // 2
    donor, receiver = lengths[1:1 + 2 * pairs:2], lengths[2:2 + 2 * pairs:2]
    room = jnp.minimum(donor - 1, most - receiver)
    moved = jax.random.randint(jax.random.fold_in(stream_key, 1), (pairs,), 0, 1 << 20) % (room + 1)
    lengths = lengths.at[1:1 + 2 * pairs:2].set(donor - moved).at[2:2 + 2 * pairs:2].set(receiver + moved)
    return lengths[jax.random.permutation(jax.random.fold_in(stream_key, 2), amount)]


def bell_draw(stream_key, extent, scale, limit, cuts=(), kind=jnp.bfloat16):
    entries = scale * jax.random.normal(stream_key, extent, jnp.float32)
    if cuts:
        entries = entries * block_levels(stream_key, extent, cuts, -0.22, 0.18)
    return jnp.clip(entries, -limit, limit).astype(kind)


def setup_inputs(seed: int = 0) -> dict:
    seeds = jax.random.split(jax.random.key(seed), 10)
    q_in = bell_draw(seeds[0], (N_SEQ * ARR, D), 1.0, 6.0, ((0, 32), (1, 4)))
    k_in = bell_draw(seeds[1], (N_SEQ * ARR, D), 1.0, 6.0, ((0, 32), (1, 4)))
    v_in = bell_draw(seeds[2], (N_SEQ * ARR, D), 1.0, 6.0, ((0, 32), (1, 4)))
    dest_pos = draw_dest_pos(jax.random.fold_in(seeds[9], 71), 0)
    doc_ids = jnp.searchsorted(jnp.cumsum(uneven_parts(seeds[4], NDOCS, TOKENS, 2 * TOKEN_DEV, 2)), jnp.arange(TOKENS), side="right").astype(jnp.int32)
    mr_filter = draw_mr_filter(jax.random.fold_in(seeds[9], 71), 0)
    norm_gain = jnp.clip(1.0 + 0.1 * jax.random.normal(seeds[6], (D,), jnp.float32), 0.5, 1.5)
    residual = draw_residual(jax.random.fold_in(seeds[9], 71), 0)
    cotangent = bell_draw(seeds[8], (TOKENS, D), 1.0, 6.0, ((0, 32), (1, 4)))
    return {"q_in": q_in, "k_in": k_in, "v_in": v_in, "dest_pos": dest_pos, "doc_ids": doc_ids, "mr_filter": mr_filter, "norm_gain": norm_gain, "residual": residual, "cotangent": cotangent}


NORM_EPS = 1e-06

def place_rows(arrived, dest_pos):
    target = jnp.where(dest_pos >= 0, dest_pos, TOKENS).astype(jnp.int32)
    empty = jnp.zeros((TOKENS, arrived.shape[1]), arrived.dtype)
    return empty.at[target].set(arrived, mode='drop')

def pick_rows(placed, dest_pos):
    target = jnp.where(dest_pos >= 0, dest_pos, TOKENS).astype(jnp.int32)
    return jnp.take(placed, target, axis=0, mode='fill', fill_value=0)

def forward_mix(product, mr_filter, doc_ids):
    padded = jnp.concatenate([jnp.zeros((L, D), product.dtype), product], axis=0)
    doc_pad = jnp.concatenate([jnp.full((L,), -1, jnp.int32), doc_ids.astype(jnp.int32)])

    def add_tap(offset, running):
        start = (L - offset).astype(jnp.int32)
        shifted = lax.dynamic_slice_in_dim(padded, start, TOKENS, 0)
        near_docs = lax.dynamic_slice_in_dim(doc_pad, start, TOKENS, 0)
        kept_mask = (near_docs == doc_ids)[:, None]
        tap_row = lax.dynamic_slice_in_dim(mr_filter, offset.astype(jnp.int32), 1, 0)
        return running + jnp.where(kept_mask, tap_row * shifted.astype(jnp.float32), 0.0)
    return lax.fori_loop(0, L, add_tap, jnp.zeros((TOKENS, D), jnp.float32))

def backward_mix(d_mixture, mr_filter, doc_ids):
    padded = jnp.concatenate([d_mixture, jnp.zeros((L, D), d_mixture.dtype)], axis=0)
    doc_pad = jnp.concatenate([doc_ids.astype(jnp.int32), jnp.full((L,), -2, jnp.int32)])

    def add_tap(offset, running):
        start = offset.astype(jnp.int32)
        shifted = lax.dynamic_slice_in_dim(padded, start, TOKENS, 0)
        near_docs = lax.dynamic_slice_in_dim(doc_pad, start, TOKENS, 0)
        kept_mask = (near_docs == doc_ids)[:, None]
        tap_row = lax.dynamic_slice_in_dim(mr_filter, start, 1, 0)
        return running + jnp.where(kept_mask, tap_row * shifted.astype(jnp.float32), 0.0)
    return lax.fori_loop(0, L, add_tap, jnp.zeros((TOKENS, D), jnp.float32))

def filter_grad(d_mixture, product, doc_ids):
    padded = jnp.concatenate([jnp.zeros((L, D), product.dtype), product], axis=0)
    doc_pad = jnp.concatenate([jnp.full((L,), -1, jnp.int32), doc_ids.astype(jnp.int32)])

    def one_tap(offset):
        start = (L - offset).astype(jnp.int32)
        shifted = lax.dynamic_slice_in_dim(padded, start, TOKENS, 0)
        near_docs = lax.dynamic_slice_in_dim(doc_pad, start, TOKENS, 0)
        kept_mask = (near_docs == doc_ids)[:, None]
        return lax.optimization_barrier(jnp.sum(jnp.where(kept_mask, d_mixture.astype(jnp.float32) * shifted.astype(jnp.float32), 0.0), axis=0))
    return lax.map(one_tap, jnp.arange(L, dtype=jnp.int32))

def reference(q_in, k_in, v_in, dest_pos, doc_ids, mr_filter, norm_gain, residual, cotangent):
    q_pos = place_rows(q_in, dest_pos)
    k_pos = place_rows(k_in, dest_pos)
    v_pos = place_rows(v_in, dest_pos)
    product = (k_pos.astype(jnp.float32) * v_pos.astype(jnp.float32)).astype(jnp.bfloat16)
    mixture = forward_mix(product, mr_filter, doc_ids)
    summed = residual.astype(jnp.float32) + q_pos.astype(jnp.float32) * mixture
    inv_rms = lax.rsqrt(lax.optimization_barrier(jnp.mean(summed * summed, axis=1, keepdims=True)) + NORM_EPS)
    normed = (summed * inv_rms * norm_gain[None, :]).astype(jnp.bfloat16)
    cot_value = cotangent.astype(jnp.float32)
    scaled_cot = cot_value * norm_gain[None, :]
    d_gain = lax.optimization_barrier(jnp.sum(cot_value * summed * inv_rms, axis=0))
    row_dot = lax.optimization_barrier(jnp.sum(scaled_cot * summed, axis=1, keepdims=True))
    d_summed = inv_rms * scaled_cot - summed * (inv_rms * inv_rms * inv_rms) * row_dot / D
    d_residual = d_summed.astype(jnp.bfloat16)
    d_q_pos = (d_summed * mixture).astype(jnp.bfloat16)
    d_mixture = (d_summed * q_pos.astype(jnp.float32)).astype(jnp.bfloat16)
    d_product = backward_mix(d_mixture, mr_filter, doc_ids).astype(jnp.bfloat16)
    d_filter = filter_grad(d_mixture, product, doc_ids)
    d_k_pos = (d_product.astype(jnp.float32) * v_pos.astype(jnp.float32)).astype(jnp.bfloat16)
    d_v_pos = (d_product.astype(jnp.float32) * k_pos.astype(jnp.float32)).astype(jnp.bfloat16)
    return (normed, d_residual, pick_rows(d_q_pos, dest_pos), pick_rows(d_k_pos, dest_pos), pick_rows(d_v_pos, dest_pos), d_filter, d_gain)
```

```python
import functools

import jax
import jax.numpy as jnp
from jax import lax
from jax.experimental import pallas as pl
from jax.experimental.pallas import tpu as pltpu
from jax.sharding import PartitionSpec as P

D = 8192
NORM_EPS = 1e-06
NDOCS = 64
BF = jnp.bfloat16
F32 = jnp.float32
I32 = jnp.int32

ROWS = 256
SLOTS = 384
TAPS = 128
SHARDS = 32
PAIR = 16
SENT = SHARDS * PAIR
WIN = TAPS + ROWS
FREQ = 320
CB = 512


def dot(a, b):
    return jnp.dot(a, b, preferred_element_type=F32)


def iota(shape, dim):
    return lax.broadcasted_iota(I32, shape, dim)


def onehot(match):
    return jnp.where(match, 1.0, 0.0).astype(BF)


def params():
    return pltpu.CompilerParams(
        dimension_semantics=("arbitrary",), vmem_limit_bytes=48 * 1024 * 1024
    )


def cols(rows, width=CB, last=None):
    if last is None:
        return pl.BlockSpec((rows, width), lambda j: (0, j))
    return pl.BlockSpec((rows, width), lambda j: (0, jnp.minimum(j, last)))


def whole(shape):
    return pl.BlockSpec(shape, lambda j: (0,) * len(shape))


def cost(flops, nbytes):
    return pl.CostEstimate(flops=int(flops), transcendentals=0, bytes_accessed=int(nbytes))


def sds(shape, dtype):
    return jax.ShapeDtypeStruct(shape, dtype)


def build_pack(owner_col, owner_row, pack):
    same = (owner_col == owner_row) & (iota((SLOTS, SLOTS), 0) < iota((SLOTS, SLOTS), 1))
    rank = jnp.sum(jnp.where(same, 1, 0), axis=0, keepdims=True)
    slot = jnp.where(owner_row >= 0, owner_row * PAIR + rank, -1)
    pack[...] = onehot(iota((SENT, SLOTS), 0) == slot)


def pack_product_kernel(owner_col, owner_row, k_ref, v_ref, out_ref, pack):
    @pl.when(pl.program_id(0) == 0)
    def _():
        build_pack(owner_col[...], owner_row[...], pack)

    product = (k_ref[...].astype(F32) * v_ref[...].astype(F32)).astype(BF)
    out_ref[...] = dot(pack[...], product).astype(BF)


def pack_rows_kernel(owner_col, owner_row, q_ref, out_ref, pack):
    @pl.when(pl.program_id(0) == 0)
    def _():
        build_pack(owner_col[...], owner_row[...], pack)

    out_ref[...] = dot(pack[...], q_ref[...]).astype(BF)


def pack_arrivals(kernel, owner_col, owner_row, blocks, width):
    return pl.pallas_call(
        kernel,
        grid=(width // CB,),
        in_specs=[whole((SLOTS, 1)), whole((1, SLOTS))] + [cols(SLOTS)] * len(blocks),
        out_specs=cols(SENT),
        out_shape=sds((SENT, width), BF),
        scratch_shapes=[pltpu.VMEM((SENT, SLOTS), BF)],
        compiler_params=params(),
        cost_estimate=cost(
            2 * SENT * SLOTS * width, 2 * width * (SENT + SLOTS * len(blocks))
        ),
    )(owner_col, owner_row, *blocks)


def place_product_kernel(pos_row, recv_ref, out_ref, tail_ref, place):
    @pl.when(pl.program_id(0) == 0)
    def _():
        place[...] = onehot(iota((ROWS, SENT), 0) == pos_row[...])

    rows = dot(place[...], recv_ref[...]).astype(BF)
    out_ref[...] = rows
    tail_ref[...] = rows[ROWS - TAPS :]


def place_product(pos_row, received):
    width = received.shape[1]
    return pl.pallas_call(
        place_product_kernel,
        grid=(width // CB,),
        in_specs=[whole((1, SENT)), cols(SENT)],
        out_specs=[cols(ROWS), cols(TAPS)],
        out_shape=[sds((ROWS, width), BF), sds((TAPS, width), BF)],
        scratch_shapes=[pltpu.VMEM((ROWS, SENT), BF)],
        compiler_params=params(),
        cost_estimate=cost(2 * SENT * ROWS * width, 2 * width * (SENT + ROWS + TAPS)),
    )(pos_row, received)


def segment_dft(docs_window):
    place = jnp.arange(WIN, dtype=I32)
    docs = jnp.where(place >= 1, docs_window, -1)
    ids = jnp.arange(NDOCS, dtype=I32)
    inside = docs[None, :] == ids[:, None]
    span = jnp.sum(inside.astype(I32), axis=1)
    own = jnp.sum((inside & (place >= TAPS)[None, :]).astype(I32), axis=1)
    first = jnp.min(jnp.where(inside, place[None, :], 2 * WIN), axis=1)
    taps = jnp.minimum(TAPS, span)
    length = jnp.maximum(span, own + taps - 1)
    length = length + 1 - length % 2
    slots = jnp.where(own > 0, (length + 1) // 2, 0)
    start = jnp.sum(jnp.where(ids[None, :] < ids[:, None], slots[None, :], 0), axis=1)
    slot = jnp.arange(FREQ, dtype=I32)[:, None]
    member = (slot >= start[None, :]) & (slot < (start + slots)[None, :])

    def pick(value):
        return jnp.sum(jnp.where(member, value[None, :], 0), axis=1, keepdims=True)

    live = pick(jnp.ones_like(ids)) > 0
    doc = jnp.where(live, pick(ids), -9)
    wave = slot - pick(start)
    size = jnp.where(live, pick(length), 1)
    size_f = size.astype(F32)
    inverse = 1.0 / size_f

    def angles(steps):
        turns = (wave * steps).astype(F32)
        turns = turns - jnp.floor(turns * inverse) * size_f
        return turns * (inverse * (2.0 * jnp.pi))

    turn = angles(place[None, :] - pick(first))
    mask = docs[None, :] == doc
    spectrum = jnp.concatenate(
        [jnp.where(mask, jnp.cos(turn), 0.0), jnp.where(mask, -jnp.sin(turn), 0.0)], axis=0
    ).astype(BF)
    lag = jnp.arange(TAPS, dtype=I32)[None, :]
    turn = angles(lag)
    weight = jnp.where(
        live & (lag < pick(taps)), jnp.where(wave == 0, inverse, 2.0 * inverse), 0.0
    )
    taps_spectrum = jnp.concatenate(
        [weight * jnp.cos(turn), -weight * jnp.sin(turn)], axis=0
    ).astype(BF)
    return spectrum, taps_spectrum


def mixture_kernel(cc, cc_own_t, bb, product, halo, filt, mix_ref, x_ref, f_ref):
    window = jnp.concatenate([halo[...], product[...]], axis=0)
    x = dot(cc[...], window)
    f = dot(bb[...], filt[...].astype(BF))
    xr, xi, fr, fi = x[:FREQ], x[FREQ:], f[:FREQ], f[FREQ:]
    y = jnp.concatenate(
        [(xr * fr - xi * fi).astype(BF), (xr * fi + xi * fr).astype(BF)], axis=0
    )
    mix_ref[...] = dot(cc_own_t[...], y)
    x_ref[...] = x.astype(BF)
    f_ref[...] = f.astype(BF)


def forward_mixture(spectrum, spectrum_t, taps_spectrum, product, halo, filt):
    width = product.shape[1]
    return pl.pallas_call(
        mixture_kernel,
        grid=(width // CB,),
        in_specs=[
            whole((2 * FREQ, WIN)),
            whole((ROWS, 2 * FREQ)),
            whole((2 * FREQ, TAPS)),
            cols(ROWS),
            cols(TAPS),
            cols(TAPS),
        ],
        out_specs=[cols(ROWS), cols(2 * FREQ), cols(2 * FREQ)],
        out_shape=[
            sds((ROWS, width), F32),
            sds((2 * FREQ, width), BF),
            sds((2 * FREQ, width), BF),
        ],
        compiler_params=params(),
        cost_estimate=cost(2 * 2 * FREQ * (WIN + TAPS + ROWS) * width, width * 8000),
    )(spectrum, spectrum_t[TAPS:], taps_spectrum, product, halo, filt)


def row_sums_kernel(pos_row, recv, mix, residual, cot, gain, q_ref, sums_ref, place, acc):
    step = pl.program_id(0)

    @pl.when(step == 0)
    def _():
        place[...] = onehot(iota((ROWS, SENT), 0) == pos_row[...])
        acc[...] = jnp.zeros_like(acc)

    q = dot(place[...], recv[...])
    q_ref[...] = q.astype(BF)
    summed = residual[...].astype(F32) + q * mix[...]
    scaled = cot[...].astype(F32) * gain[...]
    squares = jnp.sum(summed * summed, axis=1, keepdims=True)
    dots = jnp.sum(scaled * summed, axis=1, keepdims=True)
    lane = iota((ROWS, 128), 1)
    acc[...] += jnp.where(lane == 0, squares, jnp.where(lane == 1, dots, 0.0))

    @pl.when(step == pl.num_programs(0) - 1)
    def _():
        sums_ref[...] = jnp.transpose(acc[...])[:8]


def row_sums(pos_row, received, mix, residual, cot, gain):
    width = mix.shape[1]
    return pl.pallas_call(
        row_sums_kernel,
        grid=(width // CB,),
        in_specs=[whole((1, SENT)), cols(SENT), cols(ROWS), cols(ROWS), cols(ROWS), cols(1)],
        out_specs=[cols(ROWS), whole((8, ROWS))],
        out_shape=[sds((ROWS, width), BF), sds((8, ROWS), F32)],
        scratch_shapes=[pltpu.VMEM((ROWS, SENT), BF), pltpu.VMEM((ROWS, 128), F32)],
        compiler_params=params(),
        cost_estimate=cost(2 * SENT * ROWS * width, width * 4000),
    )(pos_row, received, mix, residual, cot, gain)


def tap_rows(shape, tap_dim, step):
    tap = iota(shape, tap_dim)
    return (tap // 4) * PAIR + tap % 4 + 4 * step


def backward_kernel(
    blocks,
    s0, s1, s2, s3, pos_col, cc_own, bb_t, q_ref, mix_ref, res_ref, cot_ref, gain_ref, x_ref, f_ref,
    normed_ref, dres_ref, z_ref, out_ref,
    give, stats, taps_acc, gain_acc,
):
    step = pl.program_id(0)

    @pl.when(step == 0)
    def _():
        give[...] = onehot(pos_col[...] == iota((SENT, ROWS), 1))
        sums = s0[...] + s1[...] + s2[...] + s3[...]
        tall = jnp.concatenate([sums, jnp.zeros((120, ROWS), F32)], axis=0)
        sums = jnp.transpose(tall)
        inv = lax.rsqrt(sums[:, 0:1] / D + NORM_EPS)
        lane = iota((ROWS, 128), 1)
        stats[...] = jnp.where(lane == 0, inv, sums)
        taps_acc[...] = jnp.zeros_like(taps_acc)
        gain_acc[...] = jnp.zeros_like(gain_acc)

    @pl.when(step < blocks)
    def _():
        inv = stats[:, 0:1]
        row_dot = stats[:, 1:2]
        gain = gain_ref[...]
        q = q_ref[...].astype(F32)
        mix = mix_ref[...]
        summed = res_ref[...].astype(F32) + q * mix
        cot = cot_ref[...].astype(F32)
        scaled = cot * gain
        unit = summed * inv
        normed_ref[...] = (unit * gain).astype(BF)
        gain_part = jnp.sum(cot * unit, axis=0, keepdims=True)
        d_summed = inv * scaled - summed * (inv * inv * inv) * row_dot / D
        dres_ref[...] = d_summed.astype(BF)
        out_ref[...] = dot(give[...], (d_summed * mix).astype(BF)).astype(BF)
        g = dot(cc_own[...], (d_summed * q).astype(BF))
        gr, gi = g[:FREQ], g[FREQ:]
        xr, xi = x_ref[:FREQ].astype(F32), x_ref[FREQ:].astype(F32)
        v = jnp.concatenate(
            [(gr * xr + gi * xi).astype(BF), (gi * xr - gr * xi).astype(BF)], axis=0
        )
        taps = dot(bb_t[...], v)
        fr, fi = f_ref[:FREQ].astype(F32), f_ref[FREQ:].astype(F32)
        z_ref[:FREQ] = (gr * fr + gi * fi).astype(BF)
        z_ref[FREQ:] = (gi * fr - gr * fi).astype(BF)
        spread = onehot(iota((SENT, TAPS), 0) == tap_rows((SENT, TAPS), 1, step))
        taps_acc[...] += dot(spread, taps.astype(BF))
        for i in range(CB // 128):
            row = iota((PAIR, 128), 0) == step * (CB // 128) + i
            gain_acc[...] += jnp.where(row, gain_part[:, 128 * i : 128 * (i + 1)], 0.0)

    @pl.when(step == blocks)
    def _():
        out_ref[...] = taps_acc[...].astype(BF)

    @pl.when(step == blocks + 1)
    def _():
        rows = jnp.broadcast_to(gain_acc[...][None], (SHARDS, PAIR, 128)).reshape(SENT, 128)
        out_ref[:, :128] = rows.astype(BF)


def backward(sums, pos_col, cc_own, bb_t, q, mix, residual, cot, gain, x, f):
    width = q.shape[1]
    blocks = width // CB
    last = blocks - 1
    return pl.pallas_call(
        functools.partial(backward_kernel, blocks),
        grid=(blocks + 2,),
        in_specs=[whole((8, ROWS))] * 4
        + [
            whole((SENT, 1)),
            whole((2 * FREQ, ROWS)),
            whole((TAPS, 2 * FREQ)),
            cols(ROWS, last=last),
            cols(ROWS, last=last),
            cols(ROWS, last=last),
            cols(ROWS, last=last),
            cols(1, last=last),
            cols(2 * FREQ, last=last),
            cols(2 * FREQ, last=last),
        ],
        out_specs=[
            cols(ROWS, last=last),
            cols(ROWS, last=last),
            cols(2 * FREQ, last=last),
            cols(SENT),
        ],
        out_shape=[
            sds((ROWS, width), BF),
            sds((ROWS, width), BF),
            sds((2 * FREQ, width), BF),
            sds((SENT, width + CB + 128), BF),
        ],
        scratch_shapes=[
            pltpu.VMEM((SENT, ROWS), BF),
            pltpu.VMEM((ROWS, 128), F32),
            pltpu.VMEM((SENT, CB), F32),
            pltpu.VMEM((PAIR, 128), F32),
        ],
        compiler_params=params(),
        cost_estimate=cost(3e9, width * 9000),
    )(*sums, pos_col, cc_own, bb_t, q, mix, residual, cot, gain, x, f)


def product_grad_kernel(cc_t, z_ref, own_ref, head_ref):
    grad = dot(cc_t[...], z_ref[...])
    head_ref[...] = grad[:TAPS].astype(BF)
    own_ref[...] = grad[TAPS:]


def product_grad(spectrum_t, z):
    width = z.shape[1]
    return pl.pallas_call(
        product_grad_kernel,
        grid=(width // CB,),
        in_specs=[whole((WIN, 2 * FREQ)), cols(2 * FREQ)],
        out_specs=[cols(ROWS), cols(TAPS)],
        out_shape=[sds((ROWS, width), F32), sds((TAPS, width), BF)],
        compiler_params=params(),
        cost_estimate=cost(2 * WIN * 2 * FREQ * width, width * 2600),
    )(spectrum_t, z)


def give_back_kernel(blocks, pos_col, own_ref, next_ref, out_ref, give):
    step = pl.program_id(0)

    @pl.when(step == 0)
    def _():
        give[...] = onehot(pos_col[...] == iota((SENT, ROWS), 1))

    own = own_ref[...]
    grad = jnp.concatenate(
        [own[: ROWS - TAPS], own[ROWS - TAPS :] + next_ref[...].astype(F32)], axis=0
    )
    out_ref[...] = dot(give[...], grad.astype(BF)).astype(BF)


def give_back(pos_col, own, from_next):
    width = own.shape[1]
    blocks = width // CB
    return pl.pallas_call(
        functools.partial(give_back_kernel, blocks),
        grid=(blocks,),
        in_specs=[whole((SENT, 1)), cols(ROWS), cols(TAPS)],
        out_specs=cols(SENT),
        out_shape=sds((SENT, width + CB), BF),
        scratch_shapes=[pltpu.VMEM((SENT, ROWS), BF)],
        compiler_params=params(),
        cost_estimate=cost(2 * SENT * ROWS * width, width * 2400),
    )(pos_col, own, from_next)


def reduce_kernel(taps_ref, gain_ref, rows_ref, out_ref, d_gain_ref):
    total = jnp.sum(taps_ref[...].astype(F32).reshape(SHARDS, PAIR, CB), axis=0)
    out_ref[...] = (
        jnp.broadcast_to(total[None], (SHARDS, PAIR, CB)).reshape(SENT, CB).astype(BF)
    )
    d_gain_ref[...] = jnp.sum(gain_ref[...].astype(F32).reshape(SHARDS, PAIR, 128), axis=0)


def reduce_parts(received, rows):
    width = rows.shape[1] - CB
    blocks = width // CB
    return pl.pallas_call(
        reduce_kernel,
        grid=(1,),
        in_specs=[
            pl.BlockSpec((SENT, CB), lambda j: (0, blocks)),
            pl.BlockSpec((SENT, 128), lambda j: (0, (width + CB) // 128)),
            pl.BlockSpec(memory_space=pl.ANY),
        ],
        out_specs=[
            pl.BlockSpec((SENT, CB), lambda j: (0, blocks)),
            whole((PAIR, 128)),
        ],
        out_shape=[sds(rows.shape, BF), sds((PAIR, 128), F32)],
        input_output_aliases={2: 0},
        compiler_params=params(),
        cost_estimate=cost(SENT * CB, SENT * CB * 4),
    )(received, received, rows)


def build_home(owner_col, owner_row, home):
    same = (owner_col == owner_row) & (iota((SLOTS, SLOTS), 1) < iota((SLOTS, SLOTS), 0))
    rank = jnp.sum(jnp.where(same, 1, 0), axis=1, keepdims=True)
    slot = jnp.where(owner_col >= 0, owner_col * PAIR + rank, -1)
    home[...] = onehot(iota((SLOTS, SENT), 1) == slot)


def home_rows_kernel(owner_col, owner_row, back_ref, out_ref, home):
    @pl.when(pl.program_id(0) == 0)
    def _():
        build_home(owner_col[...], owner_row[...], home)

    out_ref[...] = dot(home[...], back_ref[...]).astype(BF)


def home_rows(owner_col, owner_row, back, width):
    return pl.pallas_call(
        home_rows_kernel,
        grid=(width // CB,),
        in_specs=[whole((SLOTS, 1)), whole((1, SLOTS)), cols(SENT)],
        out_specs=cols(SLOTS),
        out_shape=sds((SLOTS, width), BF),
        scratch_shapes=[pltpu.VMEM((SLOTS, SENT), BF)],
        compiler_params=params(),
        cost_estimate=cost(2 * SENT * SLOTS * width, 2 * width * (SENT + SLOTS)),
    )(owner_col, owner_row, back)


def home_product_kernel(
    owner_col, owner_row, back_ref, taps_ref, k_ref, v_ref, dk_ref, dv_ref, filt_ref, home
):
    step = pl.program_id(0)

    @pl.when(step == 0)
    def _():
        build_home(owner_col[...], owner_row[...], home)

    grad = dot(home[...], back_ref[...])
    dk_ref[...] = (grad * v_ref[...].astype(F32)).astype(BF)
    dv_ref[...] = (grad * k_ref[...].astype(F32)).astype(BF)
    gather = onehot(iota((TAPS, SENT), 1) == tap_rows((TAPS, SENT), 0, step))
    filt_ref[...] = dot(gather, taps_ref[...])


def home_product(owner_col, owner_row, back, k, v):
    width = k.shape[1]
    blocks = width // CB
    return pl.pallas_call(
        home_product_kernel,
        grid=(blocks,),
        in_specs=[
            whole((SLOTS, 1)),
            whole((1, SLOTS)),
            cols(SENT),
            pl.BlockSpec((SENT, CB), lambda j: (0, blocks)),
            cols(SLOTS),
            cols(SLOTS),
        ],
        out_specs=[cols(SLOTS), cols(SLOTS), cols(TAPS)],
        out_shape=[sds((SLOTS, width), BF), sds((SLOTS, width), BF), sds((TAPS, width), F32)],
        scratch_shapes=[pltpu.VMEM((SLOTS, SENT), BF)],
        compiler_params=params(),
        cost_estimate=cost(2 * SENT * SLOTS * width, 2 * width * (SENT + 5 * SLOTS)),
    )(owner_col, owner_row, back, back, k, v)


def exchange(rows):
    shards = rows.reshape(SHARDS, PAIR, rows.shape[1])
    return lax.all_to_all(shards, "seq", split_axis=0, concat_axis=0, tiled=True).reshape(
        rows.shape
    )


def shift(value, steps):
    pairs = [(i, i + steps) for i in range(SHARDS) if 0 <= i + steps < SHARDS]
    return lax.ppermute(value, "seq", pairs)


def slot_positions(dest_table, my_index):
    arriving = (dest_table >= 0) & (dest_table // ROWS == my_index)
    before = (jnp.arange(SLOTS)[:, None] < jnp.arange(SLOTS)[None, :]).astype(BF)
    rank = jnp.dot(arriving.astype(BF), before, preferred_element_type=F32).astype(I32)
    rank = jnp.where(arriving, rank, -1)
    target = dest_table - my_index * ROWS + 1
    hit = rank[:, None, :] == jnp.arange(PAIR, dtype=I32)[None, :, None]
    return (jnp.sum(jnp.where(hit, target[:, None, :], 0), axis=2) - 1).reshape(SENT)


def body(q_in, k_in, v_in, dest_pos, doc_ids, mr_filter, norm_gain, residual, cotangent):
    my_index = lax.axis_index("seq")
    width = q_in.shape[1]
    gain = norm_gain[None, :]

    own_plan = lax.dynamic_slice_in_dim(dest_pos, my_index * SLOTS, SLOTS)
    own_owner = jnp.where(own_plan >= 0, own_plan // ROWS, -1)
    owner_col, owner_row = own_owner[:, None], own_owner[None, :]

    sent_product = pack_arrivals(pack_product_kernel, owner_col, owner_row, [k_in, v_in], width)
    sent_product, dest_later, docs_later, owner_col, owner_row = lax.optimization_barrier(
        (sent_product, dest_pos, doc_ids, owner_col, owner_row)
    )
    recv_product = exchange(sent_product)
    sent_q = pack_arrivals(pack_rows_kernel, owner_col, owner_row, [q_in], width)

    pos = slot_positions(dest_later.reshape(SHARDS, SLOTS), my_index)
    pos_row, pos_col = pos[None, :], pos[:, None]
    docs_all = jnp.concatenate([jnp.full((TAPS,), -1, I32), docs_later])
    docs_window = lax.dynamic_slice_in_dim(docs_all, my_index * ROWS, WIN)
    spectrum, taps_spectrum = segment_dft(docs_window)
    spectrum_t = spectrum.T
    taps_spectrum_t = taps_spectrum.T

    sent_q, recv_product, pos_row, pos_col, spectrum, spectrum_t, taps_spectrum, taps_spectrum_t = (
        lax.optimization_barrier(
            (sent_q, recv_product, pos_row, pos_col, spectrum, spectrum_t, taps_spectrum, taps_spectrum_t)
        )
    )
    recv_q = exchange(sent_q)
    product, tail = place_product(pos_row, recv_product)
    halo = shift(tail, 1)
    mix, x, f = forward_mixture(
        spectrum, spectrum_t, taps_spectrum, product, halo, mr_filter
    )
    recv_q, mix = lax.optimization_barrier((recv_q, mix))
    q_pos, sums = row_sums(pos_row, recv_q, mix, residual, cotangent, gain)
    all_sums = [sums] + [
        lax.ppermute(sums, "mp", [(i, (i + k) % 4) for i in range(4)]) for k in (1, 2, 3)
    ]
    normed, d_residual, z, sent_dq = backward(
        all_sums, pos_col, spectrum[:, TAPS:], taps_spectrum_t,
        q_pos, mix, residual, cotangent, gain, x, f,
    )
    back_q = exchange(sent_dq)
    own_grad, head_grad = product_grad(spectrum_t, z)
    from_next = shift(head_grad, -1)
    rows = give_back(pos_col, own_grad, from_next)
    sent_dp, d_gain = reduce_parts(back_q, rows)
    back_p = exchange(sent_dp)
    d_q_in = home_rows(owner_col, owner_row, back_q, width)
    d_k_in, d_v_in, d_filter = home_product(owner_col, owner_row, back_p, k_in, v_in)
    return (normed, d_residual, d_q_in, d_k_in, d_v_in, d_filter, d_gain.reshape(width))


def solution(mesh):
    return jax.shard_map(
        body,
        mesh=mesh,
        in_specs=(
            P("seq", "mp"),
            P("seq", "mp"),
            P("seq", "mp"),
            P(),
            P(),
            P(None, "mp"),
            P("mp"),
            P("seq", "mp"),
            P("seq", "mp"),
        ),
        out_specs=(
            P("seq", "mp"),
            P("seq", "mp"),
            P("seq", "mp"),
            P("seq", "mp"),
            P("seq", "mp"),
            P(None, "mp"),
            P("mp"),
        ),
        check_vma=False,
    )
```

```python
import functools

import jax
import jax.numpy as jnp
from jax import lax
from jax.experimental import pallas as pl
from jax.experimental.pallas import tpu as pltpu
from jax.sharding import PartitionSpec as P

D = 8192
NORM_EPS = 1e-06
NDOCS = 64
BF = jnp.bfloat16
F32 = jnp.float32
I32 = jnp.int32

ROWS = 256
SLOTS = 384
TAPS = 128
SHARDS = 32
PAIR = 16
WIN = TAPS + ROWS
FREQ = 320
CB = 512


def dot(a, b):
    return jnp.dot(a, b, preferred_element_type=F32)


def iota(shape, dim):
    return lax.broadcasted_iota(I32, shape, dim)


def onehot(match):
    return jnp.where(match, 1.0, 0.0).astype(BF)


def params():
    return pltpu.CompilerParams(
        dimension_semantics=("arbitrary",), vmem_limit_bytes=24 * 1024 * 1024
    )


def cols(rows, width=CB, last=None):
    if last is None:
        return pl.BlockSpec((rows, width), lambda j: (0, j))
    return pl.BlockSpec((rows, width), lambda j: (0, jnp.minimum(j, last)))


def whole(shape):
    return pl.BlockSpec(shape, lambda j: (0,) * len(shape))


def cost(flops, nbytes):
    return pl.CostEstimate(flops=int(flops), transcendentals=0, bytes_accessed=int(nbytes))


def hbm(*values):
    return [pltpu.with_memory_space_constraint(v, pltpu.HBM) for v in values]


def sds(shape, dtype):
    return pltpu.HBM(shape, dtype)


def owners_of(table_ref, index):
    rows = [table_ref[pl.ds(3 * index + i, 1), :] for i in range(3)]
    plan = jnp.concatenate(rows, axis=1)
    return jnp.where(plan >= 0, plan // ROWS, -1)


def as_column(row):
    return jnp.transpose(jnp.broadcast_to(row, (128, SLOTS)))[:, 0:1]


def slots_of(pair, core, half, owner, owner_col, sibling_col):
    early = iota((SLOTS, SLOTS), 0) < iota((SLOTS, SLOTS), 1)
    same = jnp.where((owner_col == owner) & early, 1, 0)
    rank = jnp.sum(same, axis=0, keepdims=True)
    if pair == PAIR:
        return jnp.where(owner >= 0, owner * pair + rank, -1)
    before = jnp.sum(jnp.where(sibling_col == owner, 1, 0), axis=0, keepdims=True)
    mine = core if half == 0 else 1 - core
    rank = rank + mine * before
    return jnp.where((owner >= 0) & (rank % 2 == core), owner * pair + rank // 2, -1)


def plan_kernel(pair, index_ref, table_ref, slots_ref):
    index = index_ref[0]
    core = index % 2
    own = owners_of(table_ref, index)
    own_col = as_column(own)
    if pair == PAIR:
        slots_ref[...] = jnp.broadcast_to(
            slots_of(pair, core, 0, own, own_col, None), (8, SLOTS)
        )
        return
    other = owners_of(table_ref, index + 1 - 2 * core)
    other_col = as_column(other)
    first = slots_of(pair, core, 0, own, own_col, other_col)
    second = slots_of(pair, core, 1, other, other_col, own_col)
    theirs = slots_of(pair, 1 - core, 1, own, own_col, other_col)
    slots_ref[...] = jnp.concatenate(
        [first, second, theirs, jnp.full((5, SLOTS), -1, I32)], axis=0
    )


def send_plan(pair, my_index, dest_pos):
    return pl.pallas_call(
        functools.partial(plan_kernel, pair),
        grid_spec=pltpu.PrefetchScalarGridSpec(
            num_scalar_prefetch=1,
            grid=(1,),
            in_specs=[pl.BlockSpec((SHARDS * SLOTS // 128, 128), lambda j, ref: (0, 0))],
            out_specs=pl.BlockSpec((8, SLOTS), lambda j, ref: (0, 0)),
        ),
        out_shape=jax.ShapeDtypeStruct((8, SLOTS), I32),
        compiler_params=params(),
    )(my_index.reshape(1), dest_pos.reshape(SHARDS * SLOTS // 128, 128))


def build_pack(slots_ref, packs):
    for half, pack in enumerate(packs):
        pack[...] = onehot(iota(pack.shape, 0) == slots_ref[half : half + 1, :])


def pack_product_kernel(slots_ref, k_ref, v_ref, out_ref, pack):
    @pl.when(pl.program_id(0) == 0)
    def _():
        build_pack(slots_ref, [pack])

    product = (k_ref[...].astype(F32) * v_ref[...].astype(F32)).astype(BF)
    out_ref[...] = dot(pack[...], product).astype(BF)


def pack_rows_kernel(halves, slots_ref, *refs):
    blocks, out_ref, packs = refs[:halves], refs[halves], refs[halves + 1 :]

    @pl.when(pl.program_id(0) == 0)
    def _():
        build_pack(slots_ref, packs)

    total = dot(packs[0][...], blocks[0][...])
    for half in range(1, halves):
        total = total + dot(packs[half][...], blocks[half][...])
    out_ref[...] = total.astype(BF)


def pack_arrivals(kernel, pair, slots, blocks, halves):
    width = blocks[0].shape[1]
    sent = SHARDS * pair
    return pl.pallas_call(
        kernel,
        grid=(width // CB,),
        in_specs=[whole((8, SLOTS))] + [cols(SLOTS)] * len(blocks),
        out_specs=cols(sent),
        out_shape=sds((sent, width), BF),
        scratch_shapes=[pltpu.VMEM((sent, SLOTS), BF)] * halves,
        compiler_params=params(),
        cost_estimate=cost(
            2 * sent * SLOTS * width * halves, 2 * width * (sent + SLOTS * len(blocks))
        ),
    )(slots, *blocks)


def product_kernel(k_ref, v_ref, out_ref):
    out_ref[...] = (k_ref[...].astype(F32) * v_ref[...].astype(F32)).astype(BF)


def slot_product(k, v):
    width = k.shape[1]
    return pl.pallas_call(
        product_kernel,
        grid=(width // CB,),
        in_specs=[cols(SLOTS)] * 2,
        out_specs=cols(SLOTS),
        out_shape=sds((SLOTS, width), BF),
        compiler_params=params(),
        cost_estimate=cost(SLOTS * width, 6 * width * SLOTS),
    )(*hbm(k, v))


def place_product_kernel(pos_row, recv_ref, out_ref, tail_ref, place):
    @pl.when(pl.program_id(0) == 0)
    def _():
        place[...] = onehot(iota(place.shape, 0) == pos_row[...])

    rows = dot(place[...], recv_ref[...]).astype(BF)
    out_ref[...] = rows
    tail_ref[...] = rows[ROWS - TAPS :]


def place_product(pos_row, received):
    sent, width = received.shape
    return pl.pallas_call(
        place_product_kernel,
        grid=(width // CB,),
        in_specs=[whole((1, sent)), cols(sent)],
        out_specs=[cols(ROWS), cols(TAPS)],
        out_shape=[sds((ROWS, width), BF), sds((TAPS, width), BF)],
        scratch_shapes=[pltpu.VMEM((ROWS, sent), BF)],
        compiler_params=params(),
        cost_estimate=cost(2 * sent * ROWS * width, 2 * width * (sent + ROWS + TAPS)),
    )(pos_row, received)


def segment_dft(docs_window):
    place = jnp.arange(WIN, dtype=I32)
    docs = jnp.where(place >= 1, docs_window, -1)
    ids = jnp.arange(NDOCS, dtype=I32)
    inside = docs[None, :] == ids[:, None]
    span = jnp.sum(inside.astype(I32), axis=1)
    own = jnp.sum((inside & (place >= TAPS)[None, :]).astype(I32), axis=1)
    first = jnp.min(jnp.where(inside, place[None, :], 2 * WIN), axis=1)
    taps = jnp.minimum(TAPS, span)
    length = jnp.maximum(span, own + taps - 1)
    length = length + 1 - length % 2
    slots = jnp.where(own > 0, (length + 1) // 2, 0)
    start = jnp.sum(jnp.where(ids[None, :] < ids[:, None], slots[None, :], 0), axis=1)
    slot = jnp.arange(FREQ, dtype=I32)[:, None]
    member = (slot >= start[None, :]) & (slot < (start + slots)[None, :])

    def pick(value):
        return jnp.sum(jnp.where(member, value[None, :], 0), axis=1, keepdims=True)

    live = pick(jnp.ones_like(ids)) > 0
    doc = jnp.where(live, pick(ids), -9)
    wave = slot - pick(start)
    size = jnp.where(live, pick(length), 1)
    size_f = size.astype(F32)
    inverse = 1.0 / size_f

    def angles(steps):
        turns = (wave * steps).astype(F32)
        turns = turns - jnp.floor(turns * inverse) * size_f
        return turns * (inverse * (2.0 * jnp.pi))

    turn = angles(place[None, :] - pick(first))
    mask = docs[None, :] == doc
    spectrum = jnp.concatenate(
        [jnp.where(mask, jnp.cos(turn), 0.0), jnp.where(mask, -jnp.sin(turn), 0.0)], axis=0
    ).astype(BF)
    lag = jnp.arange(TAPS, dtype=I32)[None, :]
    turn = angles(lag)
    weight = jnp.where(
        live & (lag < pick(taps)), jnp.where(wave == 0, inverse, 2.0 * inverse), 0.0
    )
    taps_spectrum = jnp.concatenate(
        [weight * jnp.cos(turn), -weight * jnp.sin(turn)], axis=0
    ).astype(BF)
    return spectrum, taps_spectrum


CROSS = TAPS + ROWS - 1
CROSS_FREQ = (CROSS + 1) // 2


def crossing_dft(own_docs, next_docs):
    wave = jnp.arange(CROSS_FREQ, dtype=I32)[:, None]
    place = jnp.arange(TAPS, dtype=I32)[None, :]

    def waves(steps):
        turn = ((wave * steps) % CROSS).astype(F32) * (2.0 * jnp.pi / CROSS)
        return jnp.concatenate([jnp.cos(turn), -jnp.sin(turn)], axis=0)

    document = own_docs[ROWS - 1]
    head = jnp.where((next_docs == document)[None, :], waves(place + TAPS), 0.0)
    tail = jnp.where((own_docs[ROWS - TAPS :] == document)[None, :], waves(place), 0.0)
    weight = jnp.where(wave == 0, 1.0, 2.0) / CROSS
    taps = jnp.concatenate([weight, weight], axis=0) * waves(place)
    return head.astype(BF), tail.T.astype(BF), taps.astype(BF)


def mixture_kernel(cc, cc_own_t, bb, product, halo, filt, mix_ref, x_ref, f_ref):
    window = jnp.concatenate([halo[...], product[...]], axis=0)
    x = dot(cc[...], window)
    f = dot(bb[...], filt[...].astype(BF))
    xr, xi, fr, fi = x[:FREQ], x[FREQ:], f[:FREQ], f[FREQ:]
    y = jnp.concatenate(
        [(xr * fr - xi * fi).astype(BF), (xr * fi + xi * fr).astype(BF)], axis=0
    )
    mix_ref[...] = dot(cc_own_t[...], y)
    x_ref[...] = x.astype(BF)
    f_ref[...] = f.astype(BF)


def forward_mixture(spectrum, cc_own_t, taps_spectrum, product, halo, filt):
    width = product.shape[1]
    return pl.pallas_call(
        mixture_kernel,
        grid=(width // CB,),
        in_specs=[
            whole((2 * FREQ, WIN)),
            whole((ROWS, 2 * FREQ)),
            whole((2 * FREQ, TAPS)),
            cols(ROWS),
            cols(TAPS),
            cols(TAPS),
        ],
        out_specs=[cols(ROWS), cols(2 * FREQ), cols(2 * FREQ)],
        out_shape=[
            sds((ROWS, width), F32),
            sds((2 * FREQ, width), BF),
            sds((2 * FREQ, width), BF),
        ],
        compiler_params=params(),
        cost_estimate=cost(2 * 2 * FREQ * (WIN + TAPS + ROWS) * width, width * 8000),
    )(spectrum, cc_own_t, taps_spectrum, *hbm(product), halo, *hbm(filt))


def row_sums_kernel(pos_row, recv, mix, residual, cot, gain, q_ref, sums_ref, place, acc):
    step = pl.program_id(0)

    @pl.when(step == 0)
    def _():
        place[...] = onehot(iota(place.shape, 0) == pos_row[...])
        acc[...] = jnp.zeros_like(acc)

    q = dot(place[...], recv[...])
    q_ref[...] = q.astype(BF)
    summed = residual[...].astype(F32) + q * mix[...]
    scaled = cot[...].astype(F32) * gain[...]
    squares = jnp.sum(summed * summed, axis=1, keepdims=True)
    dots = jnp.sum(scaled * summed, axis=1, keepdims=True)
    lane = iota((ROWS, 128), 1)
    acc[...] += jnp.where(lane == 0, squares, jnp.where(lane == 1, dots, 0.0))

    @pl.when(step == pl.num_programs(0) - 1)
    def _():
        sums_ref[...] = jnp.transpose(acc[...])[:8]


def row_sums(pos_row, received, mix, residual, cot, gain):
    sent = received.shape[0]
    width = mix.shape[1]
    return pl.pallas_call(
        row_sums_kernel,
        grid=(width // CB,),
        in_specs=[whole((1, sent)), cols(sent), cols(ROWS), cols(ROWS), cols(ROWS), cols(1)],
        out_specs=[cols(ROWS), whole((8, ROWS))],
        out_shape=[sds((ROWS, width), BF), jax.ShapeDtypeStruct((8, ROWS), F32)],
        scratch_shapes=[pltpu.VMEM((ROWS, sent), BF), pltpu.VMEM((ROWS, 128), F32)],
        compiler_params=params(),
        cost_estimate=cost(2 * sent * ROWS * width, width * 4000),
    )(pos_row, received, *hbm(mix, residual, cot), gain)


def tap_rows(pair, shape, tap_dim, step):
    tap = iota(shape, tap_dim)
    return (tap // 4) * pair + tap % 4 + 4 * (step % (pair // 4))


def extra_cols(pair, width):
    return (width // CB) * 4 // pair * CB, width // pair


def row_stats(s0, s1, s2, s3, stats):
    sums = s0[...] + s1[...] + s2[...] + s3[...]
    sums = jnp.transpose(jnp.concatenate([sums, jnp.zeros((120, ROWS), F32)], axis=0))
    inv = lax.rsqrt(sums[:, 0:1] / D + NORM_EPS)
    stats[...] = jnp.where(iota((ROWS, 128), 1) == 0, inv, sums)


def d_summed_of(stats, summed, scaled):
    inv = stats[:, 0:1]
    return inv * scaled - summed * (inv * inv * inv) * stats[:, 1:2] / D


def backward_kernel(
    pair, blocks,
    s0, s1, s2, s3, pos_col, cc_own, bb_t, q_ref, mix_ref, res_ref, cot_ref, gain_ref, x_ref,
    dmix_ref, head_ref, out_ref,
    give, stats, taps_acc, gain_acc,
):
    step = pl.program_id(0)
    per = pair // 4
    parts = blocks // per
    sent = SHARDS * pair

    @pl.when(step == 0)
    def _():
        give[...] = onehot(pos_col[...] == iota(give.shape, 1))
        row_stats(s0, s1, s2, s3, stats)
        taps_acc[...] = jnp.zeros_like(taps_acc)
        gain_acc[...] = jnp.zeros_like(gain_acc)

    @pl.when(step < blocks)
    def _():
        q = q_ref[...].astype(F32)
        mix = mix_ref[...]
        summed = res_ref[...].astype(F32) + q * mix
        cot = cot_ref[...].astype(F32)
        gain_part = jnp.sum(cot * summed * stats[:, 0:1], axis=0, keepdims=True)
        d_summed = d_summed_of(stats, summed, cot * gain_ref[...])
        out_ref[...] = dot(give[...], (d_summed * mix).astype(BF)).astype(BF)
        d_mix = (d_summed * q).astype(BF)
        dmix_ref[...] = d_mix
        head_ref[...] = d_mix[:TAPS]
        g = dot(cc_own[...], d_mix)
        gr, gi = g[:FREQ], g[FREQ:]
        xr, xi = x_ref[:FREQ].astype(F32), x_ref[FREQ:].astype(F32)
        v = jnp.concatenate(
            [(gr * xr + gi * xi).astype(BF), (gi * xr - gr * xi).astype(BF)], axis=0
        )
        taps = dot(bb_t[...], v).astype(BF)
        spread = onehot(iota((sent, TAPS), 0) == tap_rows(pair, (sent, TAPS), 1, step))
        taps_acc[step // per] += dot(spread, taps)
        wide = gain_acc.shape[1]
        for i in range(CB // wide):
            row = iota(gain_acc.shape, 0) == step * (CB // wide) + i
            gain_acc[...] += jnp.where(row, gain_part[:, wide * i : wide * (i + 1)], 0.0)

    @pl.when((step >= blocks) & (step < blocks + parts))
    def _():
        out_ref[...] = taps_acc[jnp.minimum(step - blocks, parts - 1)].astype(BF)

    @pl.when(step == blocks + parts)
    def _():
        wide = gain_acc.shape[1]
        rows = jnp.broadcast_to(gain_acc[...][None], (SHARDS, pair, wide)).reshape(sent, wide)
        out_ref[:, :wide] = rows.astype(BF)


def backward(pair, sums, pos_col, cc_own, bb_t, q, mix, residual, cot, gain, x):
    width = q.shape[1]
    blocks = width // CB
    last = blocks - 1
    sent = SHARDS * pair
    part_cols, gain_cols = extra_cols(pair, width)
    parts = part_cols // CB
    row_block = cols(ROWS, last=last)
    return pl.pallas_call(
        functools.partial(backward_kernel, pair, blocks),
        grid=(blocks + parts + 1,),
        in_specs=[whole((8, ROWS))] * 4
        + [
            whole((sent, 1)),
            whole((2 * FREQ, ROWS)),
            whole((TAPS, 2 * FREQ)),
            row_block,
            row_block,
            row_block,
            row_block,
            cols(1, last=last),
            cols(2 * FREQ, last=last),
        ],
        out_specs=[row_block, cols(TAPS, last=last), cols(sent)],
        out_shape=[
            sds((ROWS, width), BF),
            sds((TAPS, width), BF),
            sds((sent, width + part_cols + gain_cols), BF),
        ],
        scratch_shapes=[
            pltpu.VMEM((sent, ROWS), BF),
            pltpu.VMEM((ROWS, 128), F32),
            pltpu.VMEM((parts, sent, CB), F32),
            pltpu.VMEM((pair, gain_cols), F32),
        ],
        compiler_params=params(),
        cost_estimate=cost(2e9, width * 6000),
    )(*sums, *hbm(pos_col, cc_own, bb_t, q, mix, residual, cot), gain, *hbm(x))


def finish_kernel(
    s0, s1, s2, s3, cc_own, cc_own_t, q_ref, mix_ref, res_ref, cot_ref, gain_ref, f_ref, dmix_ref,
    normed_ref, dres_ref, own_ref,
    stats,
):
    @pl.when(pl.program_id(0) == 0)
    def _():
        row_stats(s0, s1, s2, s3, stats)

    gain = gain_ref[...]
    summed = res_ref[...].astype(F32) + q_ref[...].astype(F32) * mix_ref[...]
    normed_ref[...] = (summed * stats[:, 0:1] * gain).astype(BF)
    dres_ref[...] = d_summed_of(stats, summed, cot_ref[...].astype(F32) * gain).astype(BF)
    g = dot(cc_own[...], dmix_ref[...])
    gr, gi = g[:FREQ], g[FREQ:]
    fr, fi = f_ref[:FREQ].astype(F32), f_ref[FREQ:].astype(F32)
    z = jnp.concatenate(
        [(gr * fr + gi * fi).astype(BF), (gi * fr - gr * fi).astype(BF)], axis=0
    )
    own_ref[...] = dot(cc_own_t[...], z)


def finish(sums, cc_own, cc_own_t, q, mix, residual, cot, gain, f, d_mix):
    width = q.shape[1]
    return pl.pallas_call(
        finish_kernel,
        grid=(width // CB,),
        in_specs=[whole((8, ROWS))] * 4
        + [whole((2 * FREQ, ROWS)), whole((ROWS, 2 * FREQ))]
        + [cols(ROWS)] * 4
        + [cols(1), cols(2 * FREQ), cols(ROWS)],
        out_specs=[cols(ROWS)] * 3,
        out_shape=[sds((ROWS, width), BF), sds((ROWS, width), BF), sds((ROWS, width), F32)],
        scratch_shapes=[pltpu.VMEM((ROWS, 128), F32)],
        compiler_params=params(),
        cost_estimate=cost(2 * 2 * 2 * FREQ * ROWS * width, width * 6000),
    )(*sums, *hbm(cc_own, cc_own_t, q, mix, residual, cot), gain, *hbm(f, d_mix))


def give_back_kernel(pos_col, head, tail_t, taps, own_ref, next_ref, filt, out_ref, give):
    @pl.when(pl.program_id(0) == 0)
    def _():
        give[...] = onehot(pos_col[...] == iota(give.shape, 1))

    g = dot(head[...], next_ref[...])
    f = dot(taps[...], filt[...].astype(BF))
    gr, gi, fr, fi = g[:CROSS_FREQ], g[CROSS_FREQ:], f[:CROSS_FREQ], f[CROSS_FREQ:]
    z = jnp.concatenate(
        [(gr * fr + gi * fi).astype(BF), (gi * fr - gr * fi).astype(BF)], axis=0
    )
    own = own_ref[...]
    grad = jnp.concatenate(
        [own[: ROWS - TAPS], own[ROWS - TAPS :] + dot(tail_t[...], z)], axis=0
    )
    out_ref[...] = dot(give[...], grad.astype(BF)).astype(BF)


def give_back(pair, pos_col, crossing, own, from_next, filt):
    width = own.shape[1]
    sent = SHARDS * pair
    return pl.pallas_call(
        give_back_kernel,
        grid=(width // CB,),
        in_specs=[
            whole((sent, 1)),
            whole((2 * CROSS_FREQ, TAPS)),
            whole((TAPS, 2 * CROSS_FREQ)),
            whole((2 * CROSS_FREQ, TAPS)),
            cols(ROWS),
            cols(TAPS),
            cols(TAPS),
        ],
        out_specs=cols(sent),
        out_shape=sds((sent, width + extra_cols(pair, width)[0]), BF),
        scratch_shapes=[pltpu.VMEM((sent, ROWS), BF)],
        compiler_params=params(),
        cost_estimate=cost(2 * sent * ROWS * width, width * 2400),
    )(*hbm(pos_col, *crossing, own), from_next, *hbm(filt))


def reduce_kernel(pair, taps_ref, gain_ref, rows_ref, out_ref, d_gain_ref):
    def over_sources(ref):
        value = ref[...].astype(F32)
        return jnp.sum(value.reshape(SHARDS, pair, value.shape[1]), axis=0)

    total = over_sources(taps_ref)
    out_ref[...] = (
        jnp.broadcast_to(total[None], (SHARDS, pair, CB)).reshape(SHARDS * pair, CB).astype(BF)
    )
    d_gain_ref[...] = over_sources(gain_ref)


def reduce_parts(pair, received, rows, width):
    part_cols, gain_cols = extra_cols(pair, width)
    blocks = width // CB
    sent = SHARDS * pair
    return pl.pallas_call(
        functools.partial(reduce_kernel, pair),
        grid=(part_cols // CB,),
        in_specs=[
            pl.BlockSpec((sent, CB), lambda j: (0, blocks + j)),
            pl.BlockSpec((sent, gain_cols), lambda j: (0, (width + part_cols) // gain_cols)),
            pl.BlockSpec(memory_space=pl.ANY),
        ],
        out_specs=[
            pl.BlockSpec((sent, CB), lambda j: (0, blocks + j)),
            whole((pair, gain_cols)),
        ],
        out_shape=[sds(rows.shape, BF), jax.ShapeDtypeStruct((pair, gain_cols), F32)],
        input_output_aliases={2: 0},
        compiler_params=params(),
        cost_estimate=cost(sent * part_cols, sent * part_cols * 4),
    )(received, received, *hbm(rows))


def build_home(pair, slots_ref, homes):
    for half, home in enumerate(homes):
        slot = as_column(slots_ref[2 * half : 2 * half + 1, :])
        home[...] = onehot(iota(home.shape, 1) == slot)


def homecoming(backs, homes):
    total = dot(homes[0][...], backs[0][...])
    for back, home in zip(backs[1:], homes[1:]):
        total = total + dot(home[...], back[...])
    return total


def home_rows_kernel(pair, halves, slots_ref, *refs):
    backs, out_ref, homes = refs[:halves], refs[halves], refs[halves + 1 :]

    @pl.when(pl.program_id(0) == 0)
    def _():
        build_home(pair, slots_ref, homes)

    out_ref[...] = homecoming(backs, homes).astype(BF)


def home_rows(pair, slots, backs, width):
    sent = SHARDS * pair
    halves = len(backs)
    return pl.pallas_call(
        functools.partial(home_rows_kernel, pair, halves),
        grid=(width // CB,),
        in_specs=[whole((8, SLOTS))] + [cols(sent)] * halves,
        out_specs=cols(SLOTS),
        out_shape=sds((SLOTS, width), BF),
        scratch_shapes=[pltpu.VMEM((SLOTS, sent), BF)] * halves,
        compiler_params=params(),
        cost_estimate=cost(
            2 * sent * SLOTS * width * halves, 2 * width * (sent * halves + SLOTS)
        ),
    )(slots, *backs)


def home_product_kernel(pair, halves, slots_ref, taps_ref, k_ref, v_ref, *refs):
    backs, (dk_ref, dv_ref, filt_ref), homes = refs[:halves], refs[halves : halves + 3], refs[halves + 3 :]
    step = pl.program_id(0)

    @pl.when(step == 0)
    def _():
        build_home(pair, slots_ref, homes)

    grad = homecoming(backs, homes)
    dk_ref[...] = (grad * v_ref[...].astype(F32)).astype(BF)
    dv_ref[...] = (grad * k_ref[...].astype(F32)).astype(BF)
    shape = (TAPS, SHARDS * pair)
    filt_ref[...] = dot(onehot(iota(shape, 1) == tap_rows(pair, shape, 0, step)), taps_ref[...])


def home_product(pair, slots, back, backs, k, v):
    width = k.shape[1]
    blocks = width // CB
    sent = SHARDS * pair
    halves = len(backs)
    per = pair // 4
    return pl.pallas_call(
        functools.partial(home_product_kernel, pair, halves),
        grid=(blocks,),
        in_specs=[
            whole((8, SLOTS)),
            pl.BlockSpec((sent, CB), lambda j: (0, blocks + j // per)),
            cols(SLOTS),
            cols(SLOTS),
        ]
        + [cols(sent)] * halves,
        out_specs=[cols(SLOTS), cols(SLOTS), cols(TAPS)],
        out_shape=[sds((SLOTS, width), BF), sds((SLOTS, width), BF), sds((TAPS, width), F32)],
        scratch_shapes=[pltpu.VMEM((SLOTS, sent), BF)] * halves,
        compiler_params=params(),
        cost_estimate=cost(2 * sent * SLOTS * width, 2 * width * (sent + 5 * SLOTS)),
    )(slots, back, *hbm(k, v), *backs)


def exchange(pair, rows):
    shards = rows.reshape(SHARDS, pair, rows.shape[1])
    return lax.all_to_all(shards, "seq", split_axis=0, concat_axis=0, tiled=True).reshape(
        rows.shape
    )


def shift(value, steps):
    pairs = [(i, i + steps) for i in range(SHARDS) if 0 <= i + steps < SHARDS]
    return lax.ppermute(value, "seq", pairs)


def swap(value):
    return lax.ppermute(value, "seq", [(i, i ^ 1) for i in range(SHARDS)])


def slot_positions(pair, dest_pos, my_index):
    holders = SHARDS * pair // PAIR
    table = dest_pos.reshape(holders, -1)
    arriving = (table >= 0) & (table // ROWS == my_index)
    row = jnp.arange(table.shape[1], dtype=I32)
    before = (row[:, None] < row[None, :]).astype(BF)
    rank = jnp.dot(arriving.astype(BF), before, preferred_element_type=F32).astype(I32)
    rank = jnp.where(arriving, rank, -1)
    target = table - my_index * ROWS + 1
    order = jnp.arange(PAIR, dtype=I32)
    if pair != PAIR:
        order = (order % pair) * 2 + order // pair
    hit = rank[:, None, :] == order[None, :, None]
    return (jnp.sum(jnp.where(hit, target[:, None, :], 0), axis=2) - 1).reshape(SHARDS * pair)


def layer(pair, q_in, k_in, v_in, dest_pos, doc_ids, mr_filter, norm_gain, residual, cotangent):
    my_index = lax.axis_index("seq")
    width = q_in.shape[1]
    gain = norm_gain[None, :]
    shared = pair != PAIR

    if shared:
        product_in = slot_product(k_in, v_in)
        product_other = swap(product_in)
        slots = send_plan(pair, my_index, dest_pos)
        q_other = swap(q_in)
        sent_product = pack_arrivals(
            functools.partial(pack_rows_kernel, 2), pair, slots, [product_in, product_other], 2
        )
        q_blocks = [q_in, q_other]
    else:
        slots = send_plan(pair, my_index, dest_pos)
        sent_product = pack_arrivals(pack_product_kernel, pair, slots, hbm(k_in, v_in), 1)
        q_blocks = hbm(q_in)
    sent_product, dest_later, docs_later, slots = lax.optimization_barrier(
        (sent_product, dest_pos, doc_ids, slots)
    )
    recv_product = exchange(pair, sent_product)
    halves = len(q_blocks)
    sent_q = pack_arrivals(
        functools.partial(pack_rows_kernel, halves), pair, slots, q_blocks, halves
    )

    pos = slot_positions(pair, dest_later, my_index)
    pos_row, pos_col = pos[None, :], pos[:, None]
    docs_all = jnp.concatenate(
        [jnp.full((TAPS,), -1, I32), docs_later, jnp.full((TAPS,), -2, I32)]
    )
    docs = lax.dynamic_slice_in_dim(docs_all, my_index * ROWS, WIN + TAPS)
    spectrum, taps_spectrum = segment_dft(docs[:WIN])
    spectrum_t = spectrum.T
    prepared = (
        pos_row,
        pos_col,
        spectrum,
        spectrum[:, TAPS:],
        spectrum_t[TAPS:],
        taps_spectrum,
        taps_spectrum.T,
        crossing_dft(docs[TAPS:WIN], docs[WIN:]),
    )
    sent_q, recv_product, prepared = lax.optimization_barrier((sent_q, recv_product, prepared))
    pos_row, pos_col, cc, cc_own, cc_own_t, bb, bb_t, crossing = prepared

    product, tail = place_product(pos_row, recv_product)
    sent_q, halo = lax.optimization_barrier((sent_q, shift(tail, 1)))
    recv_q = exchange(pair, sent_q)
    mix, x, f = forward_mixture(cc, cc_own_t, bb, product, halo, mr_filter)
    q_pos, sums = row_sums(pos_row, recv_q, mix, residual, cotangent, gain)
    all_sums = [sums] + [
        lax.ppermute(sums, "mp", [(i, (i + k) % 4) for i in range(4)]) for k in (1, 2, 3)
    ]
    d_mix, head, sent_dq = backward(
        pair, all_sums, pos_col, cc_own, bb_t, q_pos, mix, residual, cotangent, gain, x
    )
    from_next = shift(head, -1)
    back_q = exchange(pair, sent_dq)
    normed, d_residual, own_grad = finish(
        all_sums, cc_own, cc_own_t, q_pos, mix, residual, cotangent, gain, f, d_mix
    )
    rows = give_back(pair, pos_col, crossing, own_grad, from_next, mr_filter)
    sent_dp, d_gain = reduce_parts(pair, back_q, rows, width)
    back_p = exchange(pair, sent_dp)
    backs_q, backs_p = [back_q], [back_p]
    if shared:
        backs_q.append(swap(back_q[:, :width]))
        backs_p.append(swap(back_p[:, :width]))
    d_q_in = home_rows(pair, slots, backs_q, width)
    d_k_in, d_v_in, d_filter = home_product(pair, slots, back_p, backs_p, k_in, v_in)
    return (normed, d_residual, d_q_in, d_k_in, d_v_in, d_filter, d_gain.reshape(width))


def body(*args):
    return layer(PAIR, *args)


def solution(mesh):
    return jax.shard_map(
        body,
        mesh=mesh,
        in_specs=(
            P("seq", "mp"),
            P("seq", "mp"),
            P("seq", "mp"),
            P(),
            P(),
            P(None, "mp"),
            P("mp"),
            P("seq", "mp"),
            P("seq", "mp"),
        ),
        out_specs=(
            P("seq", "mp"),
            P("seq", "mp"),
            P("seq", "mp"),
            P("seq", "mp"),
            P("seq", "mp"),
            P(None, "mp"),
            P("mp"),
        ),
        check_vma=False,
    )
```

```python
import functools

import jax
import jax.numpy as jnp
from jax import lax
from jax.experimental import pallas as pl
from jax.experimental.pallas import tpu as pltpu
from jax.sharding import PartitionSpec as P

D = 8192
NORM_EPS = 1e-06
NDOCS = 64
BF = jnp.bfloat16
F32 = jnp.float32
I32 = jnp.int32

ROWS = 256
SLOTS = 384
TAPS = 128
SHARDS = 32
PAIR = 16
WIN = TAPS + ROWS
FREQ = 320
CB = 512


def dot(a, b):
    return jnp.dot(a, b, preferred_element_type=F32)


def iota(shape, dim):
    return lax.broadcasted_iota(I32, shape, dim)


def onehot(match):
    return jnp.where(match, 1.0, 0.0).astype(BF)


def params(grid=True):
    return pltpu.CompilerParams(
        dimension_semantics=("arbitrary",) if grid else None, vmem_limit_bytes=24 * 1024 * 1024
    )


def cols(rows, width=CB, last=None):
    if last is None:
        return pl.BlockSpec((rows, width), lambda j: (0, j))
    return pl.BlockSpec((rows, width), lambda j: (0, jnp.minimum(j, last)))


RESIDENT = pl.BlockSpec(memory_space=pltpu.VMEM)


def block_of(step):
    return pl.ds(pl.multiple_of(step * CB, CB), CB)


def whole(shape):
    return pl.BlockSpec(shape, lambda j: (0,) * len(shape))


def cost(flops, nbytes):
    return pl.CostEstimate(flops=int(flops), transcendentals=0, bytes_accessed=int(nbytes))


def hbm(*values):
    return [pltpu.with_memory_space_constraint(v, pltpu.HBM) for v in values]


def kept(*values):
    return [pltpu.with_memory_space_constraint(v, pltpu.VMEM) for v in values]


def sds(shape, dtype):
    return pltpu.HBM(shape, dtype)


def owners_of(table_ref, index):
    rows = [table_ref[pl.ds(3 * index + i, 1), :] for i in range(3)]
    plan = jnp.concatenate(rows, axis=1)
    return jnp.where(plan >= 0, plan // ROWS, -1)


def as_column(row):
    return jnp.transpose(jnp.broadcast_to(row, (128, row.shape[1])))[:, 0:1]


def slots_of(pair, core, half, owner, owner_col, sibling_col):
    early = iota((SLOTS, SLOTS), 0) < iota((SLOTS, SLOTS), 1)
    same = jnp.where((owner_col == owner) & early, 1, 0)
    rank = jnp.sum(same, axis=0, keepdims=True)
    if pair == PAIR:
        return jnp.where(owner >= 0, owner * pair + rank, -1)
    before = jnp.sum(jnp.where(sibling_col == owner, 1, 0), axis=0, keepdims=True)
    mine = core if half == 0 else 1 - core
    rank = rank + mine * before
    return jnp.where((owner >= 0) & (rank % 2 == core), owner * pair + rank // 2, -1)


def plan_kernel(pair, index_ref, table_ref, slots_ref):
    index = index_ref[0]
    core = index % 2
    own = owners_of(table_ref, index)
    own_col = as_column(own)
    if pair == PAIR:
        slots_ref[...] = jnp.broadcast_to(
            slots_of(pair, core, 0, own, own_col, None), (8, SLOTS)
        )
        return
    other = owners_of(table_ref, index + 1 - 2 * core)
    other_col = as_column(other)
    first = slots_of(pair, core, 0, own, own_col, other_col)
    second = slots_of(pair, core, 1, other, other_col, own_col)
    theirs = slots_of(pair, 1 - core, 1, own, own_col, other_col)
    slots_ref[...] = jnp.concatenate(
        [first, second, theirs, jnp.full((5, SLOTS), -1, I32)], axis=0
    )


def send_plan(pair, my_index, dest_pos):
    return pl.pallas_call(
        functools.partial(plan_kernel, pair),
        grid_spec=pltpu.PrefetchScalarGridSpec(
            num_scalar_prefetch=1,
            grid=(1,),
            in_specs=[pl.BlockSpec((SHARDS * SLOTS // 128, 128), lambda j, ref: (0, 0))],
            out_specs=pl.BlockSpec((8, SLOTS), lambda j, ref: (0, 0)),
        ),
        out_shape=jax.ShapeDtypeStruct((8, SLOTS), I32),
        compiler_params=params(),
    )(my_index.reshape(1), dest_pos.reshape(SHARDS * SLOTS // 128, 128))


def build_pack(slots_ref, packs):
    for half, pack in enumerate(packs):
        pack[...] = onehot(iota(pack.shape, 0) == slots_ref[half : half + 1, :])


def pack_kernel(halves, blocks, slots_ref, *refs):
    first, second = refs[: 2 * halves : 2], refs[1 : 2 * halves : 2]
    q_refs, out_ref, packs = refs[2:3], refs[3], refs[4:]
    if halves == 2:
        first, second, q_refs, out_ref, packs = None, refs[:2], refs[2:4], refs[4], refs[5:]
    step = pl.program_id(0)

    @pl.when(step == 0)
    def _():
        build_pack(slots_ref, packs)

    def packed(values):
        total = dot(packs[0][...], values[0])
        for value, pack in zip(values[1:], packs[1:]):
            total = total + dot(pack[...], value)
        return total.astype(BF)

    @pl.when(step < blocks)
    def _():
        if first is None:
            out_ref[...] = packed([ref[...] for ref in second])
        else:
            product = first[0][...].astype(F32) * second[0][...].astype(F32)
            out_ref[...] = packed([product.astype(BF)])

    @pl.when(step >= blocks)
    def _():
        out_ref[...] = packed([ref[...] for ref in q_refs])


def pack_arrivals(pair, slots, early, late):
    width = early[0].shape[1]
    blocks = width // CB
    halves = len(late)
    sent = SHARDS * pair
    return pl.pallas_call(
        functools.partial(pack_kernel, halves, blocks),
        grid=(2 * blocks,),
        in_specs=[whole((8, SLOTS))]
        + [cols(SLOTS, last=blocks - 1)] * len(early)
        + [pl.BlockSpec((SLOTS, CB), lambda j: (0, jnp.maximum(j - blocks, 0)))] * halves,
        out_specs=cols(sent),
        out_shape=sds((sent, 2 * width), BF),
        scratch_shapes=[pltpu.VMEM((sent, SLOTS), BF)] * halves,
        compiler_params=params(),
        cost_estimate=cost(4 * sent * SLOTS * width * halves, 4 * width * (sent + SLOTS * 2)),
    )(slots, *early, *late)


def product_kernel(k_ref, v_ref, out_ref):
    out_ref[...] = (k_ref[...].astype(F32) * v_ref[...].astype(F32)).astype(BF)


def slot_product(k, v):
    width = k.shape[1]
    return pl.pallas_call(
        product_kernel,
        grid=(width // CB,),
        in_specs=[cols(SLOTS)] * 2,
        out_specs=cols(SLOTS),
        out_shape=sds((SLOTS, width), BF),
        compiler_params=params(),
        cost_estimate=cost(SLOTS * width, 6 * width * SLOTS),
    )(*hbm(k, v))


def place_tail_kernel(pos_row, recv_ref, tail_ref, place):
    @pl.when(pl.program_id(0) == 0)
    def _():
        place[...] = onehot(iota(place.shape, 0) + (ROWS - TAPS) == pos_row[...])

    tail_ref[...] = dot(place[...], recv_ref[...]).astype(BF)


def place_tail(pos_row, received, width):
    sent = received.shape[0]
    return pl.pallas_call(
        place_tail_kernel,
        grid=(width // CB,),
        in_specs=[whole((1, sent)), cols(sent)],
        out_specs=cols(TAPS),
        out_shape=sds((TAPS, width), BF),
        scratch_shapes=[pltpu.VMEM((TAPS, sent), BF)],
        compiler_params=params(),
        cost_estimate=cost(2 * sent * TAPS * width, 2 * width * (sent + TAPS)),
    )(pos_row, received)


def segment_dft(docs_window):
    place = jnp.arange(WIN, dtype=I32)
    docs = jnp.where(place >= 1, docs_window, -1)
    ids = jnp.arange(NDOCS, dtype=I32)
    inside = docs[None, :] == ids[:, None]
    span = jnp.sum(inside.astype(I32), axis=1)
    own = jnp.sum((inside & (place >= TAPS)[None, :]).astype(I32), axis=1)
    first = jnp.min(jnp.where(inside, place[None, :], 2 * WIN), axis=1)
    taps = jnp.minimum(TAPS, span)
    length = jnp.maximum(span, own + taps - 1)
    length = length + 1 - length % 2
    slots = jnp.where(own > 0, (length + 1) // 2, 0)
    start = jnp.sum(jnp.where(ids[None, :] < ids[:, None], slots[None, :], 0), axis=1)
    slot = jnp.arange(FREQ, dtype=I32)[:, None]
    member = (slot >= start[None, :]) & (slot < (start + slots)[None, :])

    def pick(value):
        return jnp.sum(jnp.where(member, value[None, :], 0), axis=1, keepdims=True)

    live = pick(jnp.ones_like(ids)) > 0
    doc = jnp.where(live, pick(ids), -9)
    wave = slot - pick(start)
    size = jnp.where(live, pick(length), 1)
    size_f = size.astype(F32)
    inverse = 1.0 / size_f

    def angles(steps):
        turns = (wave * steps).astype(F32)
        turns = turns - jnp.floor(turns * inverse) * size_f
        return turns * (inverse * (2.0 * jnp.pi))

    turn = angles(place[None, :] - pick(first))
    mask = docs[None, :] == doc
    spectrum = jnp.concatenate(
        [jnp.where(mask, jnp.cos(turn), 0.0), jnp.where(mask, -jnp.sin(turn), 0.0)], axis=0
    )
    lag = jnp.arange(TAPS, dtype=I32)[None, :]
    turn = angles(lag)
    weight = jnp.where(
        live & (lag < pick(taps)), jnp.where(wave == 0, inverse, 2.0 * inverse), 0.0
    )
    taps_spectrum = jnp.concatenate(
        [weight * jnp.cos(turn), -weight * jnp.sin(turn)], axis=0
    )
    return spectrum, taps_spectrum


CROSS = TAPS + ROWS - 1
CROSS_FREQ = (CROSS + 1) // 2


def crossing_dft(own_docs, next_docs):
    wave = jnp.arange(CROSS_FREQ, dtype=I32)[:, None]
    place = jnp.arange(TAPS, dtype=I32)[None, :]

    def waves(steps):
        turn = ((wave * steps) % CROSS).astype(F32) * (2.0 * jnp.pi / CROSS)
        return jnp.concatenate([jnp.cos(turn), -jnp.sin(turn)], axis=0)

    document = own_docs[ROWS - 1]
    head = jnp.where((next_docs == document)[None, :], waves(place + TAPS), 0.0)
    tail = jnp.where((own_docs[ROWS - TAPS :] == document)[None, :], waves(place), 0.0)
    weight = jnp.where(wave == 0, 1.0, 2.0) / CROSS
    taps = jnp.concatenate([weight, weight], axis=0) * waves(place)
    return head, tail, taps


def spectra_product(xr, xi, fr, fi):
    return jnp.concatenate(
        [(xr * fr - xi * fi).astype(BF), (xr * fi + xi * fr).astype(BF)], axis=0
    )


def conj_product(gr, gi, fr, fi):
    return jnp.concatenate(
        [(gr * fr + gi * fi).astype(BF), (gi * fr - gr * fi).astype(BF)], axis=0
    )


def sums_of(summed, scaled):
    squares = jnp.sum(summed * summed, axis=1, keepdims=True)
    dots = jnp.sum(scaled * summed, axis=1, keepdims=True)
    lane = iota((summed.shape[0], 128), 1)
    return jnp.where(lane == 0, squares, jnp.where(lane == 1, dots, 0.0))


def conv_kernel(
    pos_row, cc_own, cc_own_t, bb, recv_p, recv_q, filt, residual, cot, gain,
    q_ref, mix_ref, x_ref, f_ref, sums_ref,
    place, acc,
):
    step = pl.program_id(0)

    @pl.when(step == 0)
    def _():
        place[...] = onehot(iota(place.shape, 0) == pos_row[...])
        acc[...] = jnp.zeros_like(acc)

    at = block_of(step)
    product = dot(place[...], recv_p[...]).astype(BF)
    q = dot(place[...], recv_q[...])
    q_ref[:, at] = q.astype(BF)
    x = dot(cc_own[...], product)
    f = dot(bb[...], filt[...].astype(BF))
    x_ref[:, at] = x.astype(BF)
    f_ref[:, at] = f.astype(BF)
    mix = dot(cc_own_t[...], spectra_product(x[:FREQ], x[FREQ:], f[:FREQ], f[FREQ:]))
    mix_ref[:, at] = mix
    late = slice(TAPS, ROWS)
    summed = residual[late].astype(F32) + q[late] * mix[late]
    acc[...] += sums_of(summed, cot[late].astype(F32) * gain[...])

    @pl.when(step == pl.num_programs(0) - 1)
    def _():
        sums_ref[...] = jnp.transpose(acc[...])[:8]


def forward(pos_row, cc_own, cc_own_t, bb, received, filt, residual, cot, gain):
    sent = received.shape[0]
    width = received.shape[1] // 2
    blocks = width // CB
    return pl.pallas_call(
        conv_kernel,
        grid=(blocks,),
        in_specs=[
            whole((1, sent)),
            whole((2 * FREQ, ROWS)),
            whole((ROWS, 2 * FREQ)),
            whole((2 * FREQ, TAPS)),
            cols(sent),
            pl.BlockSpec((sent, CB), lambda j: (0, blocks + j)),
            cols(TAPS),
            cols(ROWS),
            cols(ROWS),
            cols(1),
        ],
        out_specs=[RESIDENT] * 4 + [whole((8, TAPS))],
        out_shape=[
            pltpu.VMEM((ROWS, width), BF),
            pltpu.VMEM((ROWS, width), F32),
            pltpu.VMEM((2 * FREQ, width), BF),
            pltpu.VMEM((2 * FREQ, width), BF),
            jax.ShapeDtypeStruct((8, TAPS), F32),
        ],
        scratch_shapes=[pltpu.VMEM((ROWS, sent), BF), pltpu.VMEM((TAPS, 128), F32)],
        compiler_params=params(),
        cost_estimate=cost(4e9, width * 6000),
    )(pos_row, *hbm(cc_own, cc_own_t, bb), received, received, *hbm(filt, residual, cot), gain)


def crossing(value):
    return value[:CROSS_FREQ], value[FREQ : FREQ + CROSS_FREQ]


def head_kernel(
    cc_halo, cc_head_t, halo, f_ref, q_ref, mix_ref, residual, cot, gain, sums_ref,
    mix_head_ref, out_sums_ref,
    acc,
):
    step = pl.program_id(0)

    @pl.when(step == 0)
    def _():
        acc[...] = jnp.zeros_like(acc)

    at = block_of(step)
    x = dot(cc_halo[...], halo[...])
    fr, fi = crossing(f_ref[:, at].astype(F32))
    y = spectra_product(x[:CROSS_FREQ], x[CROSS_FREQ:], fr, fi)
    mix = mix_ref[:TAPS, at] + dot(cc_head_t[...], y)
    mix_head_ref[:, at] = mix
    summed = residual[...].astype(F32) + q_ref[:TAPS, at].astype(F32) * mix
    acc[...] += sums_of(summed, cot[...].astype(F32) * gain[...])

    @pl.when(step == pl.num_programs(0) - 1)
    def _():
        out_sums_ref[:, :TAPS] = jnp.transpose(acc[...])[:8]
        out_sums_ref[:, TAPS:] = sums_ref[...]


def forward_head(cc_halo, cc_head_t, halo, f, q, mix, residual, cot, gain, sums):
    width = q.shape[1]
    return pl.pallas_call(
        head_kernel,
        grid=(width // CB,),
        in_specs=[
            whole((2 * CROSS_FREQ, TAPS)),
            whole((TAPS, 2 * CROSS_FREQ)),
            cols(TAPS),
            RESIDENT,
            RESIDENT,
            RESIDENT,
            cols(TAPS),
            cols(TAPS),
            cols(1),
            whole((8, TAPS)),
        ],
        out_specs=[RESIDENT, whole((8, ROWS))],
        out_shape=[pltpu.VMEM((TAPS, width), F32), jax.ShapeDtypeStruct((8, ROWS), F32)],
        scratch_shapes=[pltpu.VMEM((TAPS, 128), F32)],
        compiler_params=params(),
        cost_estimate=cost(6e8, width * 3000),
    )(*hbm(cc_halo, cc_head_t), halo, *kept(f, q, mix), *hbm(residual, cot), gain, sums)


def prepare_kernel(
    cc_ref, bb_ref, head_ref, tail_ref, taps_ref,
    own, own_t, halo, head_t, bb, bb_t, onward_head, onward_tail_t, onward_taps,
):
    own[...] = cc_ref[:, TAPS:].astype(BF)
    own_t[...] = jnp.transpose(cc_ref[:, TAPS:]).astype(BF)
    bb[...] = bb_ref[...].astype(BF)
    bb_t[...] = jnp.transpose(bb_ref[...]).astype(BF)
    real, imag = crossing(cc_ref)
    halo[:CROSS_FREQ] = real[:, :TAPS].astype(BF)
    halo[CROSS_FREQ:] = imag[:, :TAPS].astype(BF)
    head = jnp.concatenate([real[:, TAPS : 2 * TAPS], imag[:, TAPS : 2 * TAPS]], axis=0)
    head_t[...] = jnp.transpose(head).astype(BF)
    onward_head[...] = head_ref[...].astype(BF)
    onward_tail_t[...] = jnp.transpose(tail_ref[...]).astype(BF)
    onward_taps[...] = taps_ref[...].astype(BF)


def prepare(cc, bb, head, tail, taps):
    shapes = [
        (2 * FREQ, ROWS),
        (ROWS, 2 * FREQ),
        (2 * CROSS_FREQ, TAPS),
        (TAPS, 2 * CROSS_FREQ),
        (2 * FREQ, TAPS),
        (TAPS, 2 * FREQ),
        (2 * CROSS_FREQ, TAPS),
        (TAPS, 2 * CROSS_FREQ),
        (2 * CROSS_FREQ, TAPS),
    ]
    return pl.pallas_call(
        prepare_kernel, out_shape=[sds(shape, BF) for shape in shapes], compiler_params=params(False)
    )(cc, bb, head, tail, taps)


def tap_rows(pair, shape, tap_dim, step):
    tap = iota(shape, tap_dim)
    return (tap // 4) * pair + tap % 4 + 4 * (step % (pair // 4))


def extra_cols(pair, width):
    return (width // CB) * 4 // pair * CB, width // pair


def row_stats(s0, s1, s2, s3, stats):
    sums = s0[...] + s1[...] + s2[...] + s3[...]
    sums = jnp.transpose(jnp.concatenate([sums, jnp.zeros((120, ROWS), F32)], axis=0))
    inv = lax.rsqrt(sums[:, 0:1] / D + NORM_EPS)
    stats[...] = jnp.where(iota((ROWS, 128), 1) == 0, inv, sums)


def d_summed_of(stats, summed, scaled):
    inv = stats[:, 0:1]
    return inv * scaled - summed * (inv * inv * inv) * stats[:, 1:2] / D


def head_grad_kernel(
    s0, s1, s2, s3, q_ref, mix_head_ref, res_ref, cot_ref, gain_ref, head_ref, stats
):
    step = pl.program_id(0)

    @pl.when(step == 0)
    def _():
        row_stats(s0, s1, s2, s3, stats)

    at = block_of(step)
    q = q_ref[:TAPS, at].astype(F32)
    summed = res_ref[...].astype(F32) + q * mix_head_ref[:, at]
    d_summed = d_summed_of(stats[:TAPS], summed, cot_ref[...].astype(F32) * gain_ref[...])
    head_ref[...] = (d_summed * q).astype(BF)


def head_grad(sums, q, mix_head, residual, cot, gain):
    width = q.shape[1]
    return pl.pallas_call(
        head_grad_kernel,
        grid=(width // CB,),
        in_specs=[whole((8, ROWS))] * 4
        + [RESIDENT, RESIDENT, cols(TAPS), cols(TAPS), cols(1)],
        out_specs=cols(TAPS),
        out_shape=sds((TAPS, width), BF),
        scratch_shapes=[pltpu.VMEM((ROWS, 128), F32)],
        compiler_params=params(),
        cost_estimate=cost(width * TAPS * 10, width * TAPS * 6),
    )(*sums, *kept(q, mix_head), *hbm(residual, cot), gain)


def mixture_block(mix_ref, mix_head_ref, at):
    return jnp.concatenate([mix_head_ref[:, at], mix_ref[TAPS:, at]], axis=0)


def backward_kernel(
    pair, blocks,
    s0, s1, s2, s3, pos_row, cc_own, cc_halo, bb_t, q_ref, mix_ref, mix_head_ref, x_ref,
    halo_ref, res_ref, cot_ref, gain_ref,
    dmix_ref, out_ref,
    give, stats, taps_acc, gain_acc,
):
    step = pl.program_id(0)
    per = pair // 4
    parts = blocks // per
    sent = SHARDS * pair

    @pl.when(step == 0)
    def _():
        give[...] = onehot(as_column(pos_row[...]) == iota(give.shape, 1))
        row_stats(s0, s1, s2, s3, stats)
        taps_acc[...] = jnp.zeros_like(taps_acc)
        gain_acc[...] = jnp.zeros_like(gain_acc)

    @pl.when(step < blocks)
    def _():
        at = block_of(jnp.minimum(step, blocks - 1))
        q = q_ref[:, at].astype(F32)
        mix = mixture_block(mix_ref, mix_head_ref, at)
        summed = res_ref[...].astype(F32) + q * mix
        cot = cot_ref[...].astype(F32)
        gain_part = jnp.sum(cot * summed * stats[:, 0:1], axis=0, keepdims=True)
        d_summed = d_summed_of(stats, summed, cot * gain_ref[...])
        out_ref[...] = dot(give[...], (d_summed * mix).astype(BF)).astype(BF)
        d_mix = (d_summed * q).astype(BF)
        dmix_ref[...] = d_mix
        g = dot(cc_own[...], d_mix)
        x = x_ref[:, at].astype(F32)
        reach = dot(cc_halo[...], halo_ref[...])
        xr = jnp.concatenate([x[:CROSS_FREQ] + reach[:CROSS_FREQ], x[CROSS_FREQ:FREQ]], axis=0)
        xi = jnp.concatenate(
            [x[FREQ : FREQ + CROSS_FREQ] + reach[CROSS_FREQ:], x[FREQ + CROSS_FREQ :]], axis=0
        )
        taps = dot(bb_t[...], conj_product(g[:FREQ], g[FREQ:], xr, xi)).astype(BF)
        spread = onehot(iota((sent, TAPS), 0) == tap_rows(pair, (sent, TAPS), 1, step))
        part = jnp.minimum(step // per, parts - 1)
        taps_acc[part] += dot(spread, taps)
        wide = gain_acc.shape[1]
        for i in range(CB // wide):
            row = iota(gain_acc.shape, 0) == step * (CB // wide) + i
            gain_acc[...] += jnp.where(row, gain_part[:, wide * i : wide * (i + 1)], 0.0)

    @pl.when((step >= blocks) & (step < blocks + parts))
    def _():
        out_ref[...] = taps_acc[jnp.clip(step - blocks, 0, parts - 1)].astype(BF)

    @pl.when(step == blocks + parts)
    def _():
        wide = gain_acc.shape[1]
        rows = jnp.broadcast_to(gain_acc[...][None], (SHARDS, pair, wide)).reshape(sent, wide)
        out_ref[:, :wide] = rows.astype(BF)


def backward(pair, sums, pos_row, cc_own, cc_halo, bb_t, q, mix, mix_head, x, halo, residual, cot, gain):
    width = q.shape[1]
    blocks = width // CB
    last = blocks - 1
    sent = SHARDS * pair
    part_cols, gain_cols = extra_cols(pair, width)
    parts = part_cols // CB
    return pl.pallas_call(
        functools.partial(backward_kernel, pair, blocks),
        grid=(blocks + parts + 1,),
        in_specs=[whole((8, ROWS))] * 4
        + [
            whole((1, sent)),
            whole((2 * FREQ, ROWS)),
            whole((2 * CROSS_FREQ, TAPS)),
            whole((TAPS, 2 * FREQ)),
        ]
        + [RESIDENT] * 4
        + [
            cols(TAPS, last=last),
            cols(ROWS, last=last),
            cols(ROWS, last=last),
            cols(1, last=last),
        ],
        out_specs=[cols(ROWS, last=last), cols(sent)],
        out_shape=[
            sds((ROWS, width), BF),
            sds((sent, width + part_cols + gain_cols), BF),
        ],
        scratch_shapes=[
            pltpu.VMEM((sent, ROWS), BF),
            pltpu.VMEM((ROWS, 128), F32),
            pltpu.VMEM((parts, sent, CB), F32),
            pltpu.VMEM((pair, gain_cols), F32),
        ],
        compiler_params=params(),
        cost_estimate=cost(2e9, width * 6000),
    )(
        *sums, *hbm(pos_row, cc_own, cc_halo, bb_t), *kept(q, mix, mix_head, x), halo,
        *hbm(residual, cot), gain,
    )


def finish_kernel(
    s0, s1, s2, s3, cc_own, cc_own_t, q_ref, mix_ref, mix_head_ref, f_ref, res_ref, cot_ref,
    gain_ref, dmix_ref,
    normed_ref, dres_ref, own_ref,
    stats,
):
    step = pl.program_id(0)

    @pl.when(step == 0)
    def _():
        row_stats(s0, s1, s2, s3, stats)

    at = block_of(step)
    gain = gain_ref[...]
    mix = mixture_block(mix_ref, mix_head_ref, at)
    summed = res_ref[...].astype(F32) + q_ref[:, at].astype(F32) * mix
    normed_ref[...] = (summed * stats[:, 0:1] * gain).astype(BF)
    dres_ref[...] = d_summed_of(stats, summed, cot_ref[...].astype(F32) * gain).astype(BF)
    g = dot(cc_own[...], dmix_ref[...])
    f = f_ref[:, at].astype(F32)
    own_ref[...] = dot(cc_own_t[...], conj_product(g[:FREQ], g[FREQ:], f[:FREQ], f[FREQ:]))


def finish(sums, cc_own, cc_own_t, q, mix, mix_head, f, residual, cot, gain, d_mix):
    width = q.shape[1]
    return pl.pallas_call(
        finish_kernel,
        grid=(width // CB,),
        in_specs=[whole((8, ROWS))] * 4
        + [whole((2 * FREQ, ROWS)), whole((ROWS, 2 * FREQ))]
        + [RESIDENT] * 4
        + [cols(ROWS), cols(ROWS), cols(1), cols(ROWS)],
        out_specs=[cols(ROWS)] * 3,
        out_shape=[sds((ROWS, width), BF), sds((ROWS, width), BF), sds((ROWS, width), F32)],
        scratch_shapes=[pltpu.VMEM((ROWS, 128), F32)],
        compiler_params=params(),
        cost_estimate=cost(2 * 2 * 2 * FREQ * ROWS * width, width * 6000),
    )(
        *sums, *hbm(cc_own, cc_own_t), *kept(q, mix, mix_head, f), *hbm(residual, cot), gain,
        *hbm(d_mix),
    )


def give_back_kernel(pos_row, head, tail_t, taps, own_ref, next_ref, filt, out_ref, give):
    @pl.when(pl.program_id(0) == 0)
    def _():
        give[...] = onehot(as_column(pos_row[...]) == iota(give.shape, 1))

    g = dot(head[...], next_ref[...])
    f = dot(taps[...], filt[...].astype(BF))
    gr, gi, fr, fi = g[:CROSS_FREQ], g[CROSS_FREQ:], f[:CROSS_FREQ], f[CROSS_FREQ:]
    z = conj_product(gr, gi, fr, fi)
    own = own_ref[...]
    grad = jnp.concatenate(
        [own[: ROWS - TAPS], own[ROWS - TAPS :] + dot(tail_t[...], z)], axis=0
    )
    out_ref[...] = dot(give[...], grad.astype(BF)).astype(BF)


def give_back(pair, pos_row, onward, own, from_next, filt):
    width = own.shape[1]
    sent = SHARDS * pair
    return pl.pallas_call(
        give_back_kernel,
        grid=(width // CB,),
        in_specs=[
            whole((1, sent)),
            whole((2 * CROSS_FREQ, TAPS)),
            whole((TAPS, 2 * CROSS_FREQ)),
            whole((2 * CROSS_FREQ, TAPS)),
            cols(ROWS),
            cols(TAPS),
            cols(TAPS),
        ],
        out_specs=cols(sent),
        out_shape=sds((sent, width + extra_cols(pair, width)[0]), BF),
        scratch_shapes=[pltpu.VMEM((sent, ROWS), BF)],
        compiler_params=params(),
        cost_estimate=cost(2 * sent * ROWS * width, width * 2400),
    )(*hbm(pos_row, *onward, own), from_next, *hbm(filt))


def reduce_kernel(pair, taps_ref, gain_ref, rows_ref, out_ref, d_gain_ref):
    def over_sources(ref):
        value = ref[...].astype(F32)
        return jnp.sum(value.reshape(SHARDS, pair, value.shape[1]), axis=0)

    total = over_sources(taps_ref)
    out_ref[...] = (
        jnp.broadcast_to(total[None], (SHARDS, pair, CB)).reshape(SHARDS * pair, CB).astype(BF)
    )
    d_gain_ref[...] = over_sources(gain_ref)


def reduce_parts(pair, received, rows, width):
    part_cols, gain_cols = extra_cols(pair, width)
    blocks = width // CB
    sent = SHARDS * pair
    return pl.pallas_call(
        functools.partial(reduce_kernel, pair),
        grid=(part_cols // CB,),
        in_specs=[
            pl.BlockSpec((sent, CB), lambda j: (0, blocks + j)),
            pl.BlockSpec((sent, gain_cols), lambda j: (0, (width + part_cols) // gain_cols)),
            pl.BlockSpec(memory_space=pl.ANY),
        ],
        out_specs=[
            pl.BlockSpec((sent, CB), lambda j: (0, blocks + j)),
            whole((pair, gain_cols)),
        ],
        out_shape=[sds(rows.shape, BF), jax.ShapeDtypeStruct((pair, gain_cols), F32)],
        input_output_aliases={2: 0},
        compiler_params=params(),
        cost_estimate=cost(sent * part_cols, sent * part_cols * 4),
    )(received, received, *hbm(rows))


def build_home(pair, slots_ref, homes):
    for half, home in enumerate(homes):
        slot = as_column(slots_ref[2 * half : 2 * half + 1, :])
        home[...] = onehot(iota(home.shape, 1) == slot)


def homecoming(backs, homes):
    total = dot(homes[0][...], backs[0][...])
    for back, home in zip(backs[1:], homes[1:]):
        total = total + dot(home[...], back[...])
    return total


def home_rows_kernel(pair, halves, slots_ref, *refs):
    backs, out_ref, homes = refs[:halves], refs[halves], refs[halves + 1 :]

    @pl.when(pl.program_id(0) == 0)
    def _():
        build_home(pair, slots_ref, homes)

    out_ref[...] = homecoming(backs, homes).astype(BF)


def home_rows(pair, slots, backs, width):
    sent = SHARDS * pair
    halves = len(backs)
    return pl.pallas_call(
        functools.partial(home_rows_kernel, pair, halves),
        grid=(width // CB,),
        in_specs=[whole((8, SLOTS))] + [cols(sent)] * halves,
        out_specs=cols(SLOTS),
        out_shape=sds((SLOTS, width), BF),
        scratch_shapes=[pltpu.VMEM((SLOTS, sent), BF)] * halves,
        compiler_params=params(),
        cost_estimate=cost(
            2 * sent * SLOTS * width * halves, 2 * width * (sent * halves + SLOTS)
        ),
    )(slots, *backs)


def home_product_kernel(pair, halves, slots_ref, taps_ref, k_ref, v_ref, *refs):
    backs, (dk_ref, dv_ref, filt_ref), homes = refs[:halves], refs[halves : halves + 3], refs[halves + 3 :]
    step = pl.program_id(0)

    @pl.when(step == 0)
    def _():
        build_home(pair, slots_ref, homes)

    grad = homecoming(backs, homes)
    dk_ref[...] = (grad * v_ref[...].astype(F32)).astype(BF)
    dv_ref[...] = (grad * k_ref[...].astype(F32)).astype(BF)
    shape = (TAPS, SHARDS * pair)
    filt_ref[...] = dot(onehot(iota(shape, 1) == tap_rows(pair, shape, 0, step)), taps_ref[...])


def home_product(pair, slots, back, backs, k, v):
    width = k.shape[1]
    blocks = width // CB
    sent = SHARDS * pair
    halves = len(backs)
    per = pair // 4
    return pl.pallas_call(
        functools.partial(home_product_kernel, pair, halves),
        grid=(blocks,),
        in_specs=[
            whole((8, SLOTS)),
            pl.BlockSpec((sent, CB), lambda j: (0, blocks + j // per)),
            cols(SLOTS),
            cols(SLOTS),
        ]
        + [cols(sent)] * halves,
        out_specs=[cols(SLOTS), cols(SLOTS), cols(TAPS)],
        out_shape=[sds((SLOTS, width), BF), sds((SLOTS, width), BF), sds((TAPS, width), F32)],
        scratch_shapes=[pltpu.VMEM((SLOTS, sent), BF)] * halves,
        compiler_params=params(),
        cost_estimate=cost(2 * sent * SLOTS * width, 2 * width * (sent + 5 * SLOTS)),
    )(slots, back, *hbm(k, v), *backs)


def exchange(pair, rows):
    shards = rows.reshape(SHARDS, pair, rows.shape[1])
    return lax.all_to_all(shards, "seq", split_axis=0, concat_axis=0, tiled=True).reshape(
        rows.shape
    )


def shift(value, steps):
    pairs = [(i, i + steps) for i in range(SHARDS) if 0 <= i + steps < SHARDS]
    return lax.ppermute(value, "seq", pairs)


def swap(value):
    return lax.ppermute(value, "seq", [(i, i ^ 1) for i in range(SHARDS)])


def slot_positions(pair, dest_pos, my_index):
    holders = SHARDS * pair // PAIR
    table = dest_pos.reshape(holders, -1)
    arriving = (table >= 0) & (table // ROWS == my_index)
    row = jnp.arange(table.shape[1], dtype=I32)
    before = (row[:, None] < row[None, :]).astype(BF)
    rank = jnp.dot(arriving.astype(BF), before, preferred_element_type=F32).astype(I32)
    rank = jnp.where(arriving, rank, -1)
    target = table - my_index * ROWS + 1
    order = jnp.arange(PAIR, dtype=I32)
    if pair != PAIR:
        order = (order % pair) * 2 + order // pair
    hit = rank[:, None, :] == order[None, :, None]
    return (jnp.sum(jnp.where(hit, target[:, None, :], 0), axis=2) - 1).reshape(SHARDS * pair)


def layer(pair, q_in, k_in, v_in, dest_pos, doc_ids, mr_filter, norm_gain, residual, cotangent):
    my_index = lax.axis_index("seq")
    width = q_in.shape[1]
    gain = norm_gain[None, :]
    shared = pair != PAIR

    if shared:
        product_in = slot_product(k_in, v_in)
        product_other = swap(product_in)
        q_other = swap(q_in)
        slots = send_plan(pair, my_index, dest_pos)
        sent_rows = pack_arrivals(
            pair, slots, [*hbm(product_in), product_other], [*hbm(q_in), q_other]
        )
    else:
        slots = send_plan(pair, my_index, dest_pos)
        sent_rows = pack_arrivals(pair, slots, hbm(k_in, v_in), hbm(q_in))
    sent_rows, dest_later, docs_later, slots = lax.optimization_barrier(
        (sent_rows, dest_pos, doc_ids, slots)
    )
    received = exchange(pair, sent_rows)

    pos = slot_positions(pair, dest_later, my_index)
    pos_row = pos[None, :]
    docs_all = jnp.concatenate(
        [jnp.full((TAPS,), -1, I32), docs_later, jnp.full((TAPS,), -2, I32)]
    )
    docs = lax.dynamic_slice_in_dim(docs_all, my_index * ROWS, WIN + TAPS)
    cc, bb = segment_dft(docs[:WIN])
    onward = crossing_dft(docs[TAPS:WIN], docs[WIN:])
    prepared = prepare(cc, bb, *onward)
    received, pos_row, prepared = lax.optimization_barrier((received, pos_row, prepared))
    cc_own, cc_own_t, cc_halo, cc_head_t, bb, bb_t, *onward = prepared

    halo = shift(place_tail(pos_row, received, width), 1)
    q, mix, x, f, sums = forward(
        pos_row, cc_own, cc_own_t, bb, received, mr_filter, residual, cotangent, gain
    )
    mix_head, sums = forward_head(
        cc_halo, cc_head_t, halo, f, q, mix, residual, cotangent, gain, sums
    )
    all_sums = [sums] + [
        lax.ppermute(sums, "mp", [(i, (i + k) % 4) for i in range(4)]) for k in (1, 2, 3)
    ]
    head = head_grad(all_sums, q, mix_head, residual, cotangent, gain)
    d_mix, sent_dq = backward(
        pair, all_sums, pos_row, cc_own, cc_halo, bb_t, q, mix, mix_head, x, halo,
        residual, cotangent, gain,
    )
    sent_dq, from_next = lax.optimization_barrier((sent_dq, shift(head, -1)))
    back_q = exchange(pair, sent_dq)
    normed, d_residual, own_grad = finish(
        all_sums, cc_own, cc_own_t, q, mix, mix_head, f, residual, cotangent, gain, d_mix
    )
    rows = give_back(pair, pos_row, onward, own_grad, from_next, mr_filter)
    sent_dp, d_gain = reduce_parts(pair, back_q, rows, width)
    back_p = exchange(pair, sent_dp)
    backs_q, backs_p = [back_q], [back_p]
    if shared:
        backs_q.append(swap(back_q[:, :width]))
        backs_p.append(swap(back_p[:, :width]))
    d_q_in = home_rows(pair, slots, backs_q, width)
    d_k_in, d_v_in, d_filter = home_product(pair, slots, back_p, backs_p, k_in, v_in)
    return (normed, d_residual, d_q_in, d_k_in, d_v_in, d_filter, d_gain.reshape(width))


def body(*args):
    return layer(PAIR, *args)


def solution(mesh):
    return jax.shard_map(
        body,
        mesh=mesh,
        in_specs=(
            P("seq", "mp"),
            P("seq", "mp"),
            P("seq", "mp"),
            P(),
            P(),
            P(None, "mp"),
            P("mp"),
            P("seq", "mp"),
            P("seq", "mp"),
        ),
        out_specs=(
            P("seq", "mp"),
            P("seq", "mp"),
            P("seq", "mp"),
            P("seq", "mp"),
            P("seq", "mp"),
            P(None, "mp"),
            P("mp"),
        ),
        check_vma=False,
    )
```

```python
import functools

import jax
import jax.numpy as jnp
from jax import lax
from jax.experimental import pallas as pl
from jax.experimental.pallas import tpu as pltpu
from jax.sharding import PartitionSpec as P

D = 8192
NORM_EPS = 1e-06
NDOCS = 64
BF = jnp.bfloat16
F32 = jnp.float32
I32 = jnp.int32

ROWS = 256
SLOTS = 384
TAPS = 128
SHARDS = 32
PAIR = 16
WIN = TAPS + ROWS
FREQ = 320
CB = 512
PACK, PRODUCT, TAIL, CONV, HEAD = 1024, 1024, 2048, 1024, 1024
HEAD_GRAD, BACK, FINISH, GIVE, HOME, HOME_P = 1024, 1024, 1024, 1024, 1024, 1024


def dot(a, b):
    return jnp.dot(a, b, preferred_element_type=F32)


def iota(shape, dim):
    return lax.broadcasted_iota(I32, shape, dim)


def onehot(match):
    return jnp.where(match, 1.0, 0.0).astype(BF)


def params(grid=True):
    return pltpu.CompilerParams(
        dimension_semantics=("arbitrary",) if grid else None, vmem_limit_bytes=36 * 1024 * 1024
    )


def cols(rows, width=CB, last=None):
    if last is None:
        return pl.BlockSpec((rows, width), lambda j: (0, j))
    return pl.BlockSpec((rows, width), lambda j: (0, jnp.minimum(j, last)))


RESIDENT = pl.BlockSpec(memory_space=pltpu.VMEM)


def block_of(step, width=CB):
    return pl.ds(pl.multiple_of(step * width, width), width)


def whole(shape):
    return pl.BlockSpec(shape, lambda j: (0,) * len(shape))


def cost(flops, nbytes):
    return pl.CostEstimate(flops=int(flops), transcendentals=0, bytes_accessed=int(nbytes))


def hbm(*values):
    return [pltpu.with_memory_space_constraint(v, pltpu.HBM) for v in values]


def kept(*values):
    return [pltpu.with_memory_space_constraint(v, pltpu.VMEM) for v in values]


def sds(shape, dtype):
    return pltpu.HBM(shape, dtype)


def owners_of(table_ref, index):
    rows = [table_ref[pl.ds(3 * index + i, 1), :] for i in range(3)]
    plan = jnp.concatenate(rows, axis=1)
    return jnp.where(plan >= 0, plan // ROWS, -1)


def as_column(row):
    return jnp.transpose(jnp.broadcast_to(row, (128, row.shape[1])))[:, 0:1]


def slots_of(pair, core, half, owner, owner_col, sibling_col):
    early = iota((SLOTS, SLOTS), 0) < iota((SLOTS, SLOTS), 1)
    same = jnp.where((owner_col == owner) & early, 1, 0)
    rank = jnp.sum(same, axis=0, keepdims=True)
    if pair == PAIR:
        return jnp.where(owner >= 0, owner * pair + rank, -1)
    before = jnp.sum(jnp.where(sibling_col == owner, 1, 0), axis=0, keepdims=True)
    mine = core if half == 0 else 1 - core
    rank = rank + mine * before
    return jnp.where((owner >= 0) & (rank % 2 == core), owner * pair + rank // 2, -1)


def plan_kernel(pair, index_ref, table_ref, slots_ref):
    index = index_ref[0]
    core = index % 2
    own = owners_of(table_ref, index)
    own_col = as_column(own)
    if pair == PAIR:
        slots_ref[...] = jnp.broadcast_to(
            slots_of(pair, core, 0, own, own_col, None), (8, SLOTS)
        )
        return
    other = owners_of(table_ref, index + 1 - 2 * core)
    other_col = as_column(other)
    first = slots_of(pair, core, 0, own, own_col, other_col)
    second = slots_of(pair, core, 1, other, other_col, own_col)
    theirs = slots_of(pair, 1 - core, 1, own, own_col, other_col)
    slots_ref[...] = jnp.concatenate(
        [first, second, theirs, jnp.full((5, SLOTS), -1, I32)], axis=0
    )


def send_plan(pair, my_index, dest_pos):
    return pl.pallas_call(
        functools.partial(plan_kernel, pair),
        grid_spec=pltpu.PrefetchScalarGridSpec(
            num_scalar_prefetch=1,
            grid=(1,),
            in_specs=[pl.BlockSpec((SHARDS * SLOTS // 128, 128), lambda j, ref: (0, 0))],
            out_specs=pl.BlockSpec((8, SLOTS), lambda j, ref: (0, 0)),
        ),
        out_shape=jax.ShapeDtypeStruct((8, SLOTS), I32),
        compiler_params=params(),
    )(my_index.reshape(1), dest_pos.reshape(SHARDS * SLOTS // 128, 128))


def build_pack(slots_ref, packs):
    for half, pack in enumerate(packs):
        pack[...] = onehot(iota(pack.shape, 0) == slots_ref[half : half + 1, :])


def pack_kernel(halves, blocks, slots_ref, *refs):
    first, second = refs[: 2 * halves : 2], refs[1 : 2 * halves : 2]
    q_refs, out_ref, packs = refs[2:3], refs[3], refs[4:]
    if halves == 2:
        first, second, q_refs, out_ref, packs = None, refs[:2], refs[2:4], refs[4], refs[5:]
    step = pl.program_id(0)

    @pl.when(step == 0)
    def _():
        build_pack(slots_ref, packs)

    def packed(values):
        total = dot(packs[0][...], values[0])
        for value, pack in zip(values[1:], packs[1:]):
            total = total + dot(pack[...], value)
        return total.astype(BF)

    @pl.when(step < blocks)
    def _():
        if first is None:
            out_ref[...] = packed([ref[...] for ref in second])
        else:
            product = first[0][...].astype(F32) * second[0][...].astype(F32)
            out_ref[...] = packed([product.astype(BF)])

    @pl.when(step >= blocks)
    def _():
        out_ref[...] = packed([ref[...] for ref in q_refs])


def pack_arrivals(pair, slots, early, late):
    width = early[0].shape[1]
    blocks = width // PACK
    halves = len(late)
    sent = SHARDS * pair
    return pl.pallas_call(
        functools.partial(pack_kernel, halves, blocks),
        grid=(2 * blocks,),
        in_specs=[RESIDENT]
        + [cols(SLOTS, PACK, last=blocks - 1)] * len(early)
        + [pl.BlockSpec((SLOTS, PACK), lambda j: (0, jnp.maximum(j - blocks, 0)))] * halves,
        out_specs=cols(sent, PACK),
        out_shape=sds((sent, 2 * width), BF),
        scratch_shapes=[pltpu.VMEM((sent, SLOTS), BF)] * halves,
        compiler_params=params(),
        cost_estimate=cost(4 * sent * SLOTS * width * halves, 4 * width * (sent + SLOTS * 2)),
    )(*kept(slots), *early, *late)


def product_kernel(k_ref, v_ref, out_ref):
    out_ref[...] = (k_ref[...].astype(F32) * v_ref[...].astype(F32)).astype(BF)


def slot_product(k, v):
    width = k.shape[1]
    return pl.pallas_call(
        product_kernel,
        grid=(width // PRODUCT,),
        in_specs=[cols(SLOTS, PRODUCT)] * 2,
        out_specs=cols(SLOTS, PRODUCT),
        out_shape=sds((SLOTS, width), BF),
        compiler_params=params(),
        cost_estimate=cost(SLOTS * width, 6 * width * SLOTS),
    )(*hbm(k, v))


def place_tail_kernel(pos_row, recv_ref, tail_ref, place):
    @pl.when(pl.program_id(0) == 0)
    def _():
        place[...] = onehot(iota(place.shape, 0) + (ROWS - TAPS) == pos_row[...])

    tail_ref[...] = dot(place[...], recv_ref[...]).astype(BF)


def place_tail(pos_row, received, width):
    sent = received.shape[0]
    return pl.pallas_call(
        place_tail_kernel,
        grid=(width // TAIL,),
        in_specs=[RESIDENT, cols(sent, TAIL)],
        out_specs=cols(TAPS, TAIL),
        out_shape=sds((TAPS, width), BF),
        scratch_shapes=[pltpu.VMEM((TAPS, sent), BF)],
        compiler_params=params(),
        cost_estimate=cost(2 * sent * TAPS * width, 2 * width * (sent + TAPS)),
    )(*kept(pos_row), received)


def segment_dft(docs_window):
    place = jnp.arange(WIN, dtype=I32)
    docs = jnp.where(place >= 1, docs_window, -1)
    ids = jnp.arange(NDOCS, dtype=I32)
    inside = docs[None, :] == ids[:, None]
    span = jnp.sum(inside.astype(I32), axis=1)
    own = jnp.sum((inside & (place >= TAPS)[None, :]).astype(I32), axis=1)
    first = jnp.min(jnp.where(inside, place[None, :], 2 * WIN), axis=1)
    taps = jnp.minimum(TAPS, span)
    length = jnp.maximum(span, own + taps - 1)
    length = length + 1 - length % 2
    slots = jnp.where(own > 0, (length + 1) // 2, 0)
    start = jnp.sum(jnp.where(ids[None, :] < ids[:, None], slots[None, :], 0), axis=1)
    slot = jnp.arange(FREQ, dtype=I32)[:, None]
    member = (slot >= start[None, :]) & (slot < (start + slots)[None, :])

    def pick(value):
        return jnp.sum(jnp.where(member, value[None, :], 0), axis=1, keepdims=True)

    live = pick(jnp.ones_like(ids)) > 0
    doc = jnp.where(live, pick(ids), -9)
    wave = slot - pick(start)
    size = jnp.where(live, pick(length), 1)
    size_f = size.astype(F32)
    inverse = 1.0 / size_f

    def angles(steps):
        turns = (wave * steps).astype(F32)
        turns = turns - jnp.floor(turns * inverse) * size_f
        return turns * (inverse * (2.0 * jnp.pi))

    turn = angles(place[None, :] - pick(first))
    mask = docs[None, :] == doc
    spectrum = jnp.concatenate(
        [jnp.where(mask, jnp.cos(turn), 0.0), jnp.where(mask, -jnp.sin(turn), 0.0)], axis=0
    )
    lag = jnp.arange(TAPS, dtype=I32)[None, :]
    turn = angles(lag)
    weight = jnp.where(
        live & (lag < pick(taps)), jnp.where(wave == 0, inverse, 2.0 * inverse), 0.0
    )
    taps_spectrum = jnp.concatenate(
        [weight * jnp.cos(turn), -weight * jnp.sin(turn)], axis=0
    )
    return spectrum, taps_spectrum


CROSS = TAPS + ROWS - 1
CROSS_FREQ = (CROSS + 1) // 2


def crossing_dft(own_docs, next_docs):
    wave = jnp.arange(CROSS_FREQ, dtype=I32)[:, None]
    place = jnp.arange(TAPS, dtype=I32)[None, :]

    def waves(steps):
        turn = ((wave * steps) % CROSS).astype(F32) * (2.0 * jnp.pi / CROSS)
        return jnp.concatenate([jnp.cos(turn), -jnp.sin(turn)], axis=0)

    document = own_docs[ROWS - 1]
    head = jnp.where((next_docs == document)[None, :], waves(place + TAPS), 0.0)
    tail = jnp.where((own_docs[ROWS - TAPS :] == document)[None, :], waves(place), 0.0)
    weight = jnp.where(wave == 0, 1.0, 2.0) / CROSS
    taps = jnp.concatenate([weight, weight], axis=0) * waves(place)
    return head, tail, taps


def spectra_product(xr, xi, fr, fi):
    return jnp.concatenate(
        [(xr * fr - xi * fi).astype(BF), (xr * fi + xi * fr).astype(BF)], axis=0
    )


def conj_product(gr, gi, fr, fi):
    return jnp.concatenate(
        [(gr * fr + gi * fi).astype(BF), (gi * fr - gr * fi).astype(BF)], axis=0
    )


def sums_of(summed, scaled):
    squares = jnp.sum(summed * summed, axis=1, keepdims=True)
    dots = jnp.sum(scaled * summed, axis=1, keepdims=True)
    lane = iota((summed.shape[0], 128), 1)
    return jnp.where(lane == 0, squares, jnp.where(lane == 1, dots, 0.0))


def conv_kernel(
    pos_row, cc_own, cc_own_t, bb, recv_p, recv_q, filt, residual, cot, gain,
    q_ref, mix_ref, x_ref, f_ref, sums_ref,
    place, acc,
):
    step = pl.program_id(0)

    @pl.when(step == 0)
    def _():
        place[...] = onehot(iota(place.shape, 0) == pos_row[...])
        acc[...] = jnp.zeros_like(acc)

    at = block_of(step, CONV)
    product = dot(place[...], recv_p[...]).astype(BF)
    q = dot(place[...], recv_q[...])
    q_ref[:, at] = q.astype(BF)
    x = dot(cc_own[...], product)
    f = dot(bb[...], filt[...].astype(BF))
    x_ref[:, at] = x.astype(BF)
    f_ref[:, at] = f.astype(BF)
    mix = dot(cc_own_t[...], spectra_product(x[:FREQ], x[FREQ:], f[:FREQ], f[FREQ:]))
    mix_ref[:, at] = mix
    late = slice(TAPS, ROWS)
    summed = residual[late].astype(F32) + q[late] * mix[late]
    acc[...] += sums_of(summed, cot[late].astype(F32) * gain[...])

    @pl.when(step == pl.num_programs(0) - 1)
    def _():
        sums_ref[...] = jnp.transpose(acc[...])[:8]


def forward(pos_row, cc_own, cc_own_t, bb, received, filt, residual, cot, gain):
    sent = received.shape[0]
    width = received.shape[1] // 2
    blocks = width // CONV
    return pl.pallas_call(
        conv_kernel,
        grid=(blocks,),
        in_specs=[
            RESIDENT,
            RESIDENT,
            RESIDENT,
            RESIDENT,
            cols(sent, CONV),
            pl.BlockSpec((sent, CONV), lambda j: (0, blocks + j)),
            cols(TAPS, CONV),
            cols(ROWS, CONV),
            cols(ROWS, CONV),
            cols(1, CONV),
        ],
        out_specs=[RESIDENT] * 4 + [whole((8, TAPS))],
        out_shape=[
            pltpu.VMEM((ROWS, width), BF),
            pltpu.VMEM((ROWS, width), F32),
            pltpu.VMEM((2 * FREQ, width), BF),
            pltpu.VMEM((2 * FREQ, width), BF),
            jax.ShapeDtypeStruct((8, TAPS), F32),
        ],
        scratch_shapes=[pltpu.VMEM((ROWS, sent), BF), pltpu.VMEM((TAPS, 128), F32)],
        compiler_params=params(),
        cost_estimate=cost(4e9, width * 6000),
    )(*kept(pos_row, cc_own, cc_own_t, bb), received, received, *hbm(filt, residual, cot), gain)


def crossing(value):
    return value[:CROSS_FREQ], value[FREQ : FREQ + CROSS_FREQ]


def head_kernel(
    cc_halo, cc_head_t, halo, f_ref, q_ref, mix_ref, residual, cot, gain, sums_ref,
    mix_head_ref, out_sums_ref,
    acc,
):
    step = pl.program_id(0)

    @pl.when(step == 0)
    def _():
        acc[...] = jnp.zeros_like(acc)

    at = block_of(step, HEAD)
    x = dot(cc_halo[...], halo[...])
    fr, fi = crossing(f_ref[:, at].astype(F32))
    y = spectra_product(x[:CROSS_FREQ], x[CROSS_FREQ:], fr, fi)
    mix = mix_ref[:TAPS, at] + dot(cc_head_t[...], y)
    mix_head_ref[:, at] = mix
    summed = residual[...].astype(F32) + q_ref[:TAPS, at].astype(F32) * mix
    acc[...] += sums_of(summed, cot[...].astype(F32) * gain[...])

    @pl.when(step == pl.num_programs(0) - 1)
    def _():
        out_sums_ref[:, :TAPS] = jnp.transpose(acc[...])[:8]
        out_sums_ref[:, TAPS:] = sums_ref[...]


def forward_head(cc_halo, cc_head_t, halo, f, q, mix, residual, cot, gain, sums):
    width = q.shape[1]
    return pl.pallas_call(
        head_kernel,
        grid=(width // HEAD,),
        in_specs=[
            RESIDENT,
            RESIDENT,
            cols(TAPS, HEAD),
            RESIDENT,
            RESIDENT,
            RESIDENT,
            cols(TAPS, HEAD),
            cols(TAPS, HEAD),
            cols(1, HEAD),
            RESIDENT,
        ],
        out_specs=[RESIDENT, whole((8, ROWS))],
        out_shape=[pltpu.VMEM((TAPS, width), F32), jax.ShapeDtypeStruct((8, ROWS), F32)],
        scratch_shapes=[pltpu.VMEM((TAPS, 128), F32)],
        compiler_params=params(),
        cost_estimate=cost(6e8, width * 3000),
    )(*kept(cc_halo, cc_head_t), halo, *kept(f, q, mix), *hbm(residual, cot), gain, *kept(sums))


def prepare_kernel(
    cc_ref, bb_ref, head_ref, tail_ref, taps_ref,
    own, own_t, halo, head_t, bb, bb_t, onward_head, onward_tail_t, onward_taps,
):
    own[...] = cc_ref[:, TAPS:].astype(BF)
    own_t[...] = jnp.transpose(cc_ref[:, TAPS:]).astype(BF)
    bb[...] = bb_ref[...].astype(BF)
    bb_t[...] = jnp.transpose(bb_ref[...]).astype(BF)
    real, imag = crossing(cc_ref)
    halo[:CROSS_FREQ] = real[:, :TAPS].astype(BF)
    halo[CROSS_FREQ:] = imag[:, :TAPS].astype(BF)
    head = jnp.concatenate([real[:, TAPS : 2 * TAPS], imag[:, TAPS : 2 * TAPS]], axis=0)
    head_t[...] = jnp.transpose(head).astype(BF)
    onward_head[...] = head_ref[...].astype(BF)
    onward_tail_t[...] = jnp.transpose(tail_ref[...]).astype(BF)
    onward_taps[...] = taps_ref[...].astype(BF)


def prepare(cc, bb, head, tail, taps):
    shapes = [
        (2 * FREQ, ROWS),
        (ROWS, 2 * FREQ),
        (2 * CROSS_FREQ, TAPS),
        (TAPS, 2 * CROSS_FREQ),
        (2 * FREQ, TAPS),
        (TAPS, 2 * FREQ),
        (2 * CROSS_FREQ, TAPS),
        (TAPS, 2 * CROSS_FREQ),
        (2 * CROSS_FREQ, TAPS),
    ]
    return pl.pallas_call(
        prepare_kernel, out_shape=[pltpu.VMEM(shape, BF) for shape in shapes], compiler_params=params(False)
    )(cc, bb, head, tail, taps)


def tap_rows(pair, shape, tap_dim, step):
    tap = iota(shape, tap_dim)
    return (tap // 4) * pair + tap % 4 + 4 * (step % (pair // 4))


def extra_cols(pair, width):
    return (width // CB) * 4 // pair * CB, width // pair


def row_stats(s0, s1, s2, s3, stats):
    sums = s0[...] + s1[...] + s2[...] + s3[...]
    sums = jnp.transpose(jnp.concatenate([sums, jnp.zeros((120, ROWS), F32)], axis=0))
    inv = lax.rsqrt(sums[:, 0:1] / D + NORM_EPS)
    stats[...] = jnp.where(iota((ROWS, 128), 1) == 0, inv, sums)


def d_summed_of(stats, summed, scaled):
    inv = stats[:, 0:1]
    return inv * scaled - summed * (inv * inv * inv) * stats[:, 1:2] / D


def head_grad_kernel(
    s0, s1, s2, s3, q_ref, mix_head_ref, res_ref, cot_ref, gain_ref, head_ref, stats
):
    step = pl.program_id(0)

    @pl.when(step == 0)
    def _():
        row_stats(s0, s1, s2, s3, stats)

    at = block_of(step, HEAD_GRAD)
    q = q_ref[:TAPS, at].astype(F32)
    summed = res_ref[...].astype(F32) + q * mix_head_ref[:, at]
    d_summed = d_summed_of(stats[:TAPS], summed, cot_ref[...].astype(F32) * gain_ref[...])
    head_ref[...] = (d_summed * q).astype(BF)


def head_grad(sums, q, mix_head, residual, cot, gain):
    width = q.shape[1]
    return pl.pallas_call(
        head_grad_kernel,
        grid=(width // HEAD_GRAD,),
        in_specs=[RESIDENT] * 4
        + [RESIDENT, RESIDENT, cols(TAPS, HEAD_GRAD), cols(TAPS, HEAD_GRAD), cols(1, HEAD_GRAD)],
        out_specs=cols(TAPS, HEAD_GRAD),
        out_shape=sds((TAPS, width), BF),
        scratch_shapes=[pltpu.VMEM((ROWS, 128), F32)],
        compiler_params=params(),
        cost_estimate=cost(width * TAPS * 10, width * TAPS * 6),
    )(*kept(*sums, q, mix_head), *hbm(residual, cot), gain)


def mixture_block(mix_ref, mix_head_ref, at):
    return jnp.concatenate([mix_head_ref[:, at], mix_ref[TAPS:, at]], axis=0)


def backward_kernel(
    pair, blocks,
    s0, s1, s2, s3, pos_row, cc_own, cc_halo, bb_t, q_ref, mix_ref, mix_head_ref, x_ref,
    halo_ref, res_ref, cot_ref, gain_ref,
    dmix_ref, out_ref,
    give, stats, taps_acc, gain_acc,
):
    step = pl.program_id(0)
    per = pair // 4
    parts = taps_acc.shape[0]
    sent = SHARDS * pair

    @pl.when(step == 0)
    def _():
        give[...] = onehot(as_column(pos_row[...]) == iota(give.shape, 1))
        row_stats(s0, s1, s2, s3, stats)
        taps_acc[...] = jnp.zeros_like(taps_acc)
        gain_acc[...] = jnp.zeros_like(gain_acc)

    @pl.when(step < blocks)
    def _():
        at = block_of(jnp.minimum(step, blocks - 1), BACK)
        q = q_ref[:, at].astype(F32)
        mix = mixture_block(mix_ref, mix_head_ref, at)
        summed = res_ref[...].astype(F32) + q * mix
        cot = cot_ref[...].astype(F32)
        gain_part = jnp.sum(cot * summed * stats[:, 0:1], axis=0, keepdims=True)
        d_summed = d_summed_of(stats, summed, cot * gain_ref[...])
        out_ref[...] = dot(give[...], (d_summed * mix).astype(BF)).astype(BF)
        d_mix = (d_summed * q).astype(BF)
        dmix_ref[...] = d_mix
        g = dot(cc_own[...], d_mix)
        x = x_ref[:, at].astype(F32)
        reach = dot(cc_halo[...], halo_ref[...])
        xr = jnp.concatenate([x[:CROSS_FREQ] + reach[:CROSS_FREQ], x[CROSS_FREQ:FREQ]], axis=0)
        xi = jnp.concatenate(
            [x[FREQ : FREQ + CROSS_FREQ] + reach[CROSS_FREQ:], x[FREQ + CROSS_FREQ :]], axis=0
        )
        taps = dot(bb_t[...], conj_product(g[:FREQ], g[FREQ:], xr, xi)).astype(BF)
        for i in range(BACK // CB):
            block = jnp.minimum(step, blocks - 1) * (BACK // CB) + i
            spread = onehot(iota((sent, TAPS), 0) == tap_rows(pair, (sent, TAPS), 1, block))
            taps_acc[block // per] += dot(spread, taps[:, CB * i : CB * (i + 1)])
        wide = gain_acc.shape[1]
        for i in range(BACK // wide):
            row = iota(gain_acc.shape, 0) == step * (BACK // wide) + i
            gain_acc[...] += jnp.where(row, gain_part[:, wide * i : wide * (i + 1)], 0.0)

    def extra(at):
        if at < CB * parts:
            return taps_acc[at // CB]
        wide = gain_acc.shape[1]
        return jnp.broadcast_to(gain_acc[...][None], (SHARDS, pair, wide)).reshape(sent, wide)

    starts = [CB * part for part in range(parts + 1)]
    for late in range(pl.cdiv(starts[-1] + 1, BACK)):

        @pl.when(step == blocks + late)
        def _(late=late):
            for at in starts:
                if at // BACK == late:
                    value = extra(at).astype(BF)
                    out_ref[:, at % BACK : at % BACK + value.shape[1]] = value


def backward(pair, sums, pos_row, cc_own, cc_halo, bb_t, q, mix, mix_head, x, halo, residual, cot, gain):
    width = q.shape[1]
    blocks = width // BACK
    last = blocks - 1
    sent = SHARDS * pair
    part_cols, gain_cols = extra_cols(pair, width)
    parts = part_cols // CB
    return pl.pallas_call(
        functools.partial(backward_kernel, pair, blocks),
        grid=(blocks + pl.cdiv(part_cols + gain_cols, BACK),),
        in_specs=[RESIDENT] * 4
        + [
            RESIDENT,
            RESIDENT,
            RESIDENT,
            RESIDENT,
        ]
        + [RESIDENT] * 4
        + [
            cols(TAPS, BACK, last=last),
            cols(ROWS, BACK, last=last),
            cols(ROWS, BACK, last=last),
            cols(1, BACK, last=last),
        ],
        out_specs=[cols(ROWS, BACK, last=last), cols(sent, BACK)],
        out_shape=[
            sds((ROWS, width), BF),
            sds((sent, width + part_cols + gain_cols), BF),
        ],
        scratch_shapes=[
            pltpu.VMEM((sent, ROWS), BF),
            pltpu.VMEM((ROWS, 128), F32),
            pltpu.VMEM((parts, sent, CB), F32),
            pltpu.VMEM((pair, gain_cols), F32),
        ],
        compiler_params=params(),
        cost_estimate=cost(2e9, width * 6000),
    )(
        *kept(*sums, pos_row, cc_own, cc_halo, bb_t, q, mix, mix_head, x), halo,
        *hbm(residual, cot), gain,
    )


def finish_kernel(
    s0, s1, s2, s3, cc_own, cc_own_t, q_ref, mix_ref, mix_head_ref, f_ref, res_ref, cot_ref,
    gain_ref, dmix_ref,
    normed_ref, dres_ref, own_ref,
    stats,
):
    step = pl.program_id(0)

    @pl.when(step == 0)
    def _():
        row_stats(s0, s1, s2, s3, stats)

    at = block_of(step, FINISH)
    gain = gain_ref[...]
    mix = mixture_block(mix_ref, mix_head_ref, at)
    summed = res_ref[...].astype(F32) + q_ref[:, at].astype(F32) * mix
    normed_ref[...] = (summed * stats[:, 0:1] * gain).astype(BF)
    dres_ref[...] = d_summed_of(stats, summed, cot_ref[...].astype(F32) * gain).astype(BF)
    g = dot(cc_own[...], dmix_ref[...])
    f = f_ref[:, at].astype(F32)
    own_ref[...] = dot(cc_own_t[...], conj_product(g[:FREQ], g[FREQ:], f[:FREQ], f[FREQ:]))


def finish(sums, cc_own, cc_own_t, q, mix, mix_head, f, residual, cot, gain, d_mix):
    width = q.shape[1]
    return pl.pallas_call(
        finish_kernel,
        grid=(width // FINISH,),
        in_specs=[RESIDENT] * 4
        + [RESIDENT, RESIDENT]
        + [RESIDENT] * 4
        + [cols(ROWS, FINISH), cols(ROWS, FINISH), cols(1, FINISH), cols(ROWS, FINISH)],
        out_specs=[cols(ROWS, FINISH)] * 3,
        out_shape=[sds((ROWS, width), BF), sds((ROWS, width), BF), sds((ROWS, width), F32)],
        scratch_shapes=[pltpu.VMEM((ROWS, 128), F32)],
        compiler_params=params(),
        cost_estimate=cost(2 * 2 * 2 * FREQ * ROWS * width, width * 6000),
    )(
        *kept(*sums, cc_own, cc_own_t, q, mix, mix_head, f), *hbm(residual, cot), gain,
        *hbm(d_mix),
    )


def give_back_kernel(pos_row, head, tail_t, taps, own_ref, next_ref, filt, out_ref, give):
    @pl.when(pl.program_id(0) == 0)
    def _():
        give[...] = onehot(as_column(pos_row[...]) == iota(give.shape, 1))

    g = dot(head[...], next_ref[...])
    f = dot(taps[...], filt[...].astype(BF))
    gr, gi, fr, fi = g[:CROSS_FREQ], g[CROSS_FREQ:], f[:CROSS_FREQ], f[CROSS_FREQ:]
    z = conj_product(gr, gi, fr, fi)
    own = own_ref[...]
    grad = jnp.concatenate(
        [own[: ROWS - TAPS], own[ROWS - TAPS :] + dot(tail_t[...], z)], axis=0
    )
    out_ref[...] = dot(give[...], grad.astype(BF)).astype(BF)


def give_back(pair, pos_row, onward, own, from_next, filt):
    width = own.shape[1]
    sent = SHARDS * pair
    return pl.pallas_call(
        give_back_kernel,
        grid=(width // GIVE,),
        in_specs=[
            RESIDENT,
            RESIDENT,
            RESIDENT,
            RESIDENT,
            cols(ROWS, GIVE),
            cols(TAPS, GIVE),
            cols(TAPS, GIVE),
        ],
        out_specs=cols(sent, GIVE),
        out_shape=sds((sent, width + extra_cols(pair, width)[0]), BF),
        scratch_shapes=[pltpu.VMEM((sent, ROWS), BF)],
        compiler_params=params(),
        cost_estimate=cost(2 * sent * ROWS * width, width * 2400),
    )(*kept(pos_row, *onward), *hbm(own), from_next, *hbm(filt))


def reduce_kernel(pair, taps_ref, gain_ref, rows_ref, out_ref, d_gain_ref):
    def over_sources(ref):
        value = ref[...].astype(F32)
        return jnp.sum(value.reshape(SHARDS, pair, value.shape[1]), axis=0)

    total = over_sources(taps_ref)
    out_ref[...] = (
        jnp.broadcast_to(total[None], (SHARDS, pair, CB)).reshape(SHARDS * pair, CB).astype(BF)
    )
    d_gain_ref[...] = over_sources(gain_ref)


def reduce_parts(pair, received, rows, width):
    part_cols, gain_cols = extra_cols(pair, width)
    blocks = width // CB
    sent = SHARDS * pair
    return pl.pallas_call(
        functools.partial(reduce_kernel, pair),
        grid=(part_cols // CB,),
        in_specs=[
            pl.BlockSpec((sent, CB), lambda j: (0, blocks + j)),
            pl.BlockSpec((sent, gain_cols), lambda j: (0, (width + part_cols) // gain_cols)),
            pl.BlockSpec(memory_space=pl.ANY),
        ],
        out_specs=[
            pl.BlockSpec((sent, CB), lambda j: (0, blocks + j)),
            whole((pair, gain_cols)),
        ],
        out_shape=[sds(rows.shape, BF), jax.ShapeDtypeStruct((pair, gain_cols), F32)],
        input_output_aliases={2: 0},
        compiler_params=params(),
        cost_estimate=cost(sent * part_cols, sent * part_cols * 4),
    )(received, received, *hbm(rows))


def build_home(pair, slots_ref, homes):
    for half, home in enumerate(homes):
        slot = as_column(slots_ref[2 * half : 2 * half + 1, :])
        home[...] = onehot(iota(home.shape, 1) == slot)


def homecoming(backs, homes):
    total = dot(homes[0][...], backs[0][...])
    for back, home in zip(backs[1:], homes[1:]):
        total = total + dot(home[...], back[...])
    return total


def home_rows_kernel(pair, halves, slots_ref, *refs):
    backs, out_ref, homes = refs[:halves], refs[halves], refs[halves + 1 :]

    @pl.when(pl.program_id(0) == 0)
    def _():
        build_home(pair, slots_ref, homes)

    out_ref[...] = homecoming(backs, homes).astype(BF)


def home_rows(pair, slots, backs, width):
    sent = SHARDS * pair
    halves = len(backs)
    return pl.pallas_call(
        functools.partial(home_rows_kernel, pair, halves),
        grid=(width // HOME,),
        in_specs=[RESIDENT] + [cols(sent, HOME)] * halves,
        out_specs=cols(SLOTS, HOME),
        out_shape=sds((SLOTS, width), BF),
        scratch_shapes=[pltpu.VMEM((SLOTS, sent), BF)] * halves,
        compiler_params=params(),
        cost_estimate=cost(
            2 * sent * SLOTS * width * halves, 2 * width * (sent * halves + SLOTS)
        ),
    )(*kept(slots), *backs)


def home_product_kernel(pair, halves, slots_ref, taps_ref, k_ref, v_ref, *refs):
    backs, (dk_ref, dv_ref, filt_ref), homes = refs[:halves], refs[halves : halves + 3], refs[halves + 3 :]
    step = pl.program_id(0)

    @pl.when(step == 0)
    def _():
        build_home(pair, slots_ref, homes)

    grad = homecoming(backs, homes)
    dk_ref[...] = (grad * v_ref[...].astype(F32)).astype(BF)
    dv_ref[...] = (grad * k_ref[...].astype(F32)).astype(BF)
    shape = (TAPS, SHARDS * pair)
    for i in range(HOME_P // CB):
        block = step * (HOME_P // CB) + i
        gather = onehot(iota(shape, 1) == tap_rows(pair, shape, 0, block))
        part = taps_ref[:, block_of(block // (pair // 4))]
        filt_ref[:, CB * i : CB * (i + 1)] = dot(gather, part)


def home_product(pair, slots, back, backs, k, v):
    width = k.shape[1]
    part_cols = extra_cols(pair, width)[0]
    sent = SHARDS * pair
    halves = len(backs)
    return pl.pallas_call(
        functools.partial(home_product_kernel, pair, halves),
        grid=(width // HOME_P,),
        in_specs=[
            RESIDENT,
            pl.BlockSpec((sent, part_cols), lambda j: (0, width // part_cols)),
            cols(SLOTS, HOME_P),
            cols(SLOTS, HOME_P),
        ]
        + [cols(sent, HOME_P)] * halves,
        out_specs=[cols(SLOTS, HOME_P), cols(SLOTS, HOME_P), cols(TAPS, HOME_P)],
        out_shape=[sds((SLOTS, width), BF), sds((SLOTS, width), BF), sds((TAPS, width), F32)],
        scratch_shapes=[pltpu.VMEM((SLOTS, sent), BF)] * halves,
        compiler_params=params(),
        cost_estimate=cost(2 * sent * SLOTS * width, 2 * width * (sent + 5 * SLOTS)),
    )(*kept(slots), back, *hbm(k, v), *backs)


def exchange(pair, rows):
    shards = rows.reshape(SHARDS, pair, rows.shape[1])
    return lax.all_to_all(shards, "seq", split_axis=0, concat_axis=0, tiled=True).reshape(
        rows.shape
    )


def shift(value, steps):
    pairs = [(i, i + steps) for i in range(SHARDS) if 0 <= i + steps < SHARDS]
    return lax.ppermute(value, "seq", pairs)


def swap(value):
    return lax.ppermute(value, "seq", [(i, i ^ 1) for i in range(SHARDS)])


def slot_positions(pair, dest_pos, my_index):
    holders = SHARDS * pair // PAIR
    table = dest_pos.reshape(holders, -1)
    arriving = (table >= 0) & (table // ROWS == my_index)
    row = jnp.arange(table.shape[1], dtype=I32)
    before = (row[:, None] < row[None, :]).astype(BF)
    rank = jnp.dot(arriving.astype(BF), before, preferred_element_type=F32).astype(I32)
    rank = jnp.where(arriving, rank, -1)
    target = table - my_index * ROWS + 1
    order = jnp.arange(PAIR, dtype=I32)
    if pair != PAIR:
        order = (order % pair) * 2 + order // pair
    hit = rank[:, None, :] == order[None, :, None]
    return (jnp.sum(jnp.where(hit, target[:, None, :], 0), axis=2) - 1).reshape(SHARDS * pair)


def layer(pair, q_in, k_in, v_in, dest_pos, doc_ids, mr_filter, norm_gain, residual, cotangent):
    my_index = lax.axis_index("seq")
    width = q_in.shape[1]
    gain = norm_gain[None, :]
    shared = pair != PAIR

    if shared:
        product_in = slot_product(k_in, v_in)
        product_other = swap(product_in)
        q_other = swap(q_in)
        slots = send_plan(pair, my_index, dest_pos)
        sent_rows = pack_arrivals(
            pair, slots, [*hbm(product_in), product_other], [*hbm(q_in), q_other]
        )
    else:
        slots = send_plan(pair, my_index, dest_pos)
        sent_rows = pack_arrivals(pair, slots, hbm(k_in, v_in), hbm(q_in))
    sent_rows, dest_later, docs_later, slots = lax.optimization_barrier(
        (sent_rows, dest_pos, doc_ids, slots)
    )
    received = exchange(pair, sent_rows)

    pos = slot_positions(pair, dest_later, my_index)
    pos_row = pos[None, :]
    docs_all = jnp.concatenate(
        [jnp.full((TAPS,), -1, I32), docs_later, jnp.full((TAPS,), -2, I32)]
    )
    docs = lax.dynamic_slice_in_dim(docs_all, my_index * ROWS, WIN + TAPS)
    cc, bb = segment_dft(docs[:WIN])
    onward = crossing_dft(docs[TAPS:WIN], docs[WIN:])
    prepared = prepare(cc, bb, *onward)
    received, pos_row, prepared = lax.optimization_barrier((received, pos_row, prepared))
    cc_own, cc_own_t, cc_halo, cc_head_t, bb, bb_t, *onward = prepared

    halo = shift(place_tail(pos_row, received, width), 1)
    q, mix, x, f, sums = forward(
        pos_row, cc_own, cc_own_t, bb, received, mr_filter, residual, cotangent, gain
    )
    mix_head, sums = forward_head(
        cc_halo, cc_head_t, halo, f, q, mix, residual, cotangent, gain, sums
    )
    all_sums = [sums] + [
        lax.ppermute(sums, "mp", [(i, (i + k) % 4) for i in range(4)]) for k in (1, 2, 3)
    ]
    head = head_grad(all_sums, q, mix_head, residual, cotangent, gain)
    d_mix, sent_dq = backward(
        pair, all_sums, pos_row, cc_own, cc_halo, bb_t, q, mix, mix_head, x, halo,
        residual, cotangent, gain,
    )
    sent_dq, from_next = lax.optimization_barrier((sent_dq, shift(head, -1)))
    back_q = exchange(pair, sent_dq)
    normed, d_residual, own_grad = finish(
        all_sums, cc_own, cc_own_t, q, mix, mix_head, f, residual, cotangent, gain, d_mix
    )
    rows = give_back(pair, pos_row, onward, own_grad, from_next, mr_filter)
    sent_dp, d_gain = reduce_parts(pair, back_q, rows, width)
    back_p = exchange(pair, sent_dp)
    backs_q, backs_p = [back_q], [back_p]
    if shared:
        backs_q.append(swap(back_q[:, :width]))
        backs_p.append(swap(back_p[:, :width]))
    d_q_in = home_rows(pair, slots, backs_q, width)
    d_k_in, d_v_in, d_filter = home_product(pair, slots, back_p, backs_p, k_in, v_in)
    return (normed, d_residual, d_q_in, d_k_in, d_v_in, d_filter, d_gain.reshape(width))


def body(*args):
    return layer(PAIR, *args)


def solution(mesh):
    return jax.shard_map(
        body,
        mesh=mesh,
        in_specs=(
            P("seq", "mp"),
            P("seq", "mp"),
            P("seq", "mp"),
            P(),
            P(),
            P(None, "mp"),
            P("mp"),
            P("seq", "mp"),
            P("seq", "mp"),
        ),
        out_specs=(
            P("seq", "mp"),
            P("seq", "mp"),
            P("seq", "mp"),
            P("seq", "mp"),
            P("seq", "mp"),
            P(None, "mp"),
            P("mp"),
        ),
        check_vma=False,
    )
```

```python
import functools
import math

import jax
import jax.numpy as jnp
from jax import lax
from jax.experimental import pallas as pl
from jax.experimental.pallas import tpu as pltpu
from jax.sharding import PartitionSpec as P

D = 8192
NORM_EPS = 1e-06
NDOCS = 64
BF = jnp.bfloat16
F32 = jnp.float32
I32 = jnp.int32

ROWS = 256
SLOTS = 384
TAPS = 128
SHARDS = 32
PAIR = 16
WIN = TAPS + ROWS
FREQ = 320
CB = 512
WIDE, NARROW = 1024, 256


def step_width(pair):
    return NARROW if pair == PAIR else WIDE


def dot(a, b):
    return jnp.dot(a, b, preferred_element_type=F32)


def iota(shape, dim):
    return lax.broadcasted_iota(I32, shape, dim)


def onehot(match):
    return jnp.where(match, 1.0, 0.0).astype(BF)


def params(grid=True):
    return pltpu.CompilerParams(
        dimension_semantics=("arbitrary",) if grid else None, vmem_limit_bytes=36 * 1024 * 1024
    )


def cols(rows, width=CB, last=None):
    if last is None:
        return pl.BlockSpec((rows, width), lambda j: (0, j))
    return pl.BlockSpec((rows, width), lambda j: (0, jnp.minimum(j, last)))


RESIDENT = pl.BlockSpec(memory_space=pltpu.VMEM)


def block_of(step, width=CB):
    return pl.ds(pl.multiple_of(step * width, width), width)


def whole(shape):
    return pl.BlockSpec(shape, lambda j: (0,) * len(shape))


def cost(flops, nbytes):
    return pl.CostEstimate(flops=int(flops), transcendentals=0, bytes_accessed=int(nbytes))


def hbm(*values):
    return [pltpu.with_memory_space_constraint(v, pltpu.HBM) for v in values]


def kept(*values):
    return [pltpu.with_memory_space_constraint(v, pltpu.VMEM) for v in values]


def sds(shape, dtype):
    return pltpu.HBM(shape, dtype)


def owners_of(table_ref, index):
    rows = [table_ref[pl.ds(3 * index + i, 1), :] for i in range(3)]
    plan = jnp.concatenate(rows, axis=1)
    return jnp.where(plan >= 0, plan // ROWS, -1)


def as_column(row):
    return jnp.transpose(jnp.broadcast_to(row, (128, row.shape[1])))[:, 0:1]


def slots_of(pair, core, half, owner, owner_col, sibling_col):
    early = iota((SLOTS, SLOTS), 0) < iota((SLOTS, SLOTS), 1)
    same = jnp.where((owner_col == owner) & early, 1, 0)
    rank = jnp.sum(same, axis=0, keepdims=True)
    if pair == PAIR:
        return jnp.where(owner >= 0, owner * pair + rank, -1)
    before = jnp.sum(jnp.where(sibling_col == owner, 1, 0), axis=0, keepdims=True)
    mine = core if half == 0 else 1 - core
    rank = rank + mine * before
    return jnp.where((owner >= 0) & (rank % 2 == core), owner * pair + rank // 2, -1)


def plan_kernel(pair, index_ref, table_ref, slots_ref):
    index = index_ref[0]
    core = index % 2
    own = owners_of(table_ref, index)
    own_col = as_column(own)
    if pair == PAIR:
        slots_ref[...] = jnp.broadcast_to(
            slots_of(pair, core, 0, own, own_col, None), (8, SLOTS)
        )
        return
    other = owners_of(table_ref, index + 1 - 2 * core)
    other_col = as_column(other)
    first = slots_of(pair, core, 0, own, own_col, other_col)
    second = slots_of(pair, core, 1, other, other_col, own_col)
    theirs = slots_of(pair, 1 - core, 1, own, own_col, other_col)
    slots_ref[...] = jnp.concatenate(
        [first, second, theirs, jnp.full((5, SLOTS), -1, I32)], axis=0
    )


def send_plan(pair, my_index, dest_pos):
    return pl.pallas_call(
        functools.partial(plan_kernel, pair),
        grid_spec=pltpu.PrefetchScalarGridSpec(
            num_scalar_prefetch=1,
            grid=(1,),
            in_specs=[pl.BlockSpec((SHARDS * SLOTS // 128, 128), lambda j, ref: (0, 0))],
            out_specs=pl.BlockSpec((8, SLOTS), lambda j, ref: (0, 0)),
        ),
        out_shape=jax.ShapeDtypeStruct((8, SLOTS), I32),
        compiler_params=params(),
    )(my_index.reshape(1), dest_pos.reshape(SHARDS * SLOTS // 128, 128))


def build_pack(slots_ref, packs):
    for half, pack in enumerate(packs):
        pack[...] = onehot(iota(pack.shape, 0) == slots_ref[half : half + 1, :])


def pack_kernel(halves, blocks, slots_ref, *refs):
    first, second = refs[: 2 * halves : 2], refs[1 : 2 * halves : 2]
    q_refs, out_ref, packs = refs[2:3], refs[3], refs[4:]
    if halves == 2:
        first, second, q_refs, out_ref, packs = None, refs[:2], refs[2:4], refs[4], refs[5:]
    step = pl.program_id(0)

    @pl.when(step == 0)
    def _():
        build_pack(slots_ref, packs)

    def packed(values):
        total = dot(packs[0][...], values[0])
        for value, pack in zip(values[1:], packs[1:]):
            total = total + dot(pack[...], value)
        return total.astype(BF)

    @pl.when(step < blocks)
    def _():
        if first is None:
            out_ref[...] = packed([ref[...] for ref in second])
        else:
            product = first[0][...].astype(F32) * second[0][...].astype(F32)
            out_ref[...] = packed([product.astype(BF)])

    @pl.when(step >= blocks)
    def _():
        out_ref[...] = packed([ref[...] for ref in q_refs])


def pack_arrivals(pair, slots, early, late):
    wide = step_width(pair)
    width = early[0].shape[1]
    blocks = width // wide
    halves = len(late)
    sent = SHARDS * pair
    return pl.pallas_call(
        functools.partial(pack_kernel, halves, blocks),
        grid=(2 * blocks,),
        in_specs=[RESIDENT]
        + [cols(SLOTS, wide, last=blocks - 1)] * len(early)
        + [pl.BlockSpec((SLOTS, wide), lambda j: (0, jnp.maximum(j - blocks, 0)))] * halves,
        out_specs=cols(sent, wide),
        out_shape=sds((sent, 2 * width), BF),
        scratch_shapes=[pltpu.VMEM((sent, SLOTS), BF)] * halves,
        compiler_params=params(),
        cost_estimate=cost(4 * sent * SLOTS * width * halves, 4 * width * (sent + SLOTS * 2)),
    )(*kept(slots), *early, *late)


def product_kernel(k_ref, v_ref, out_ref):
    out_ref[...] = (k_ref[...].astype(F32) * v_ref[...].astype(F32)).astype(BF)


def slot_product(k, v):
    width = k.shape[1]
    return pl.pallas_call(
        product_kernel,
        grid=(width // WIDE,),
        in_specs=[cols(SLOTS, WIDE)] * 2,
        out_specs=cols(SLOTS, WIDE),
        out_shape=sds((SLOTS, width), BF),
        compiler_params=params(),
        cost_estimate=cost(SLOTS * width, 6 * width * SLOTS),
    )(*hbm(k, v))


def place_tail_kernel(pos_row, recv_ref, tail_ref, place):
    @pl.when(pl.program_id(0) == 0)
    def _():
        place[...] = onehot(iota(place.shape, 0) + (ROWS - TAPS) == pos_row[...])

    tail_ref[...] = dot(place[...], recv_ref[...]).astype(BF)


def place_tail(wide, pos_row, received, width):
    sent = received.shape[0]
    return pl.pallas_call(
        place_tail_kernel,
        grid=(width // wide,),
        in_specs=[RESIDENT, cols(sent, wide)],
        out_specs=cols(TAPS, wide),
        out_shape=sds((TAPS, width), BF),
        scratch_shapes=[pltpu.VMEM((TAPS, sent), BF)],
        compiler_params=params(),
        cost_estimate=cost(2 * sent * TAPS * width, 2 * width * (sent + TAPS)),
    )(*kept(pos_row), received)


def wave_of(turns):
    square = (turns * turns) * (4.0 * math.pi * math.pi)

    def series(first):
        total = jnp.zeros_like(square)
        for power in range(first + 18, first - 1, -2):
            term = (-1.0) ** ((power - first) // 2) / math.factorial(power)
            total = total * square + term
        return total

    return series(0), series(1) * (turns * (-2.0 * math.pi))


def segment_dft(docs_window):
    place = jnp.arange(WIN, dtype=I32)
    docs = jnp.where(place >= 1, docs_window, -1)
    ids = jnp.arange(NDOCS, dtype=I32)
    inside = docs[None, :] == ids[:, None]
    span = jnp.sum(inside.astype(I32), axis=1)
    own = jnp.sum((inside & (place >= TAPS)[None, :]).astype(I32), axis=1)
    first = jnp.min(jnp.where(inside, place[None, :], 2 * WIN), axis=1)
    taps = jnp.minimum(TAPS, span)
    length = jnp.maximum(span, own + taps - 1)
    length = length + 1 - length % 2
    slots = jnp.where(own > 0, (length + 1) // 2, 0)
    start = jnp.sum(jnp.where(ids[None, :] < ids[:, None], slots[None, :], 0), axis=1)
    slot = jnp.arange(FREQ, dtype=I32)[:, None]
    member = (slot >= start[None, :]) & (slot < (start + slots)[None, :])

    def pick(value):
        return jnp.sum(jnp.where(member, value[None, :], 0), axis=1, keepdims=True)

    live = pick(jnp.ones_like(ids)) > 0
    doc = jnp.where(live, pick(ids), -9)
    wave = slot - pick(start)
    size = jnp.where(live, pick(length), 1)
    size_f = size.astype(F32)
    inverse = 1.0 / size_f

    def waves(steps):
        turns = (wave * steps).astype(F32)
        turns = turns - jnp.round(turns * inverse) * size_f
        return wave_of(turns * inverse)

    real, imag = waves(place[None, :] - pick(first))
    mask = docs[None, :] == doc
    spectrum = jnp.where(
        jnp.concatenate([mask, mask], axis=0), jnp.concatenate([real, imag], axis=0), 0.0
    )
    lag = jnp.arange(TAPS, dtype=I32)[None, :]
    real, imag = waves(lag)
    weight = jnp.where(
        live & (lag < pick(taps)), jnp.where(wave == 0, inverse, 2.0 * inverse), 0.0
    )
    taps_spectrum = jnp.concatenate([weight * real, weight * imag], axis=0)
    return spectrum, taps_spectrum


CROSS = TAPS + ROWS - 1
CROSS_FREQ = (CROSS + 1) // 2


def crossing_dft(own_docs, next_docs):
    wave = jnp.arange(CROSS_FREQ, dtype=I32)[:, None]
    place = jnp.arange(TAPS, dtype=I32)[None, :]

    def waves(steps):
        turns = (wave * steps).astype(F32)
        turns = turns - jnp.round(turns * (1.0 / CROSS)) * CROSS
        return jnp.concatenate(wave_of(turns * (1.0 / CROSS)), axis=0)

    document = own_docs[ROWS - 1]
    head = jnp.where((next_docs == document)[None, :], waves(place + TAPS), 0.0)
    tail = jnp.where((own_docs[ROWS - TAPS :] == document)[None, :], waves(place), 0.0)
    weight = jnp.where(wave == 0, 1.0, 2.0) / CROSS
    taps = jnp.concatenate([weight, weight], axis=0) * waves(place)
    return head, tail, taps


def spectra_product(xr, xi, fr, fi):
    return jnp.concatenate(
        [(xr * fr - xi * fi).astype(BF), (xr * fi + xi * fr).astype(BF)], axis=0
    )


def conj_product(gr, gi, fr, fi):
    return jnp.concatenate(
        [(gr * fr + gi * fi).astype(BF), (gi * fr - gr * fi).astype(BF)], axis=0
    )


def sums_of(summed, scaled):
    squares = jnp.sum(summed * summed, axis=1, keepdims=True)
    dots = jnp.sum(scaled * summed, axis=1, keepdims=True)
    lane = iota((summed.shape[0], 128), 1)
    return jnp.where(lane == 0, squares, jnp.where(lane == 1, dots, 0.0))


def conv_kernel(
    pos_row, cc_own, cc_own_t, bb, recv_p, recv_q, filt, residual, cot, gain,
    q_ref, mix_ref, x_ref, f_ref, sums_ref,
    place, acc,
):
    step = pl.program_id(0)

    @pl.when(step == 0)
    def _():
        place[...] = onehot(iota(place.shape, 0) == pos_row[...])
        acc[...] = jnp.zeros_like(acc)

    at = block_of(step, recv_p.shape[1])
    product = dot(place[...], recv_p[...]).astype(BF)
    q = dot(place[...], recv_q[...])
    q_ref[:, at] = q.astype(BF)
    x = dot(cc_own[...], product)
    f = dot(bb[...], filt[...].astype(BF))
    x_ref[:, at] = x.astype(BF)
    f_ref[:, at] = f.astype(BF)
    mix = dot(cc_own_t[...], spectra_product(x[:FREQ], x[FREQ:], f[:FREQ], f[FREQ:]))
    mix_ref[:, at] = mix
    late = slice(TAPS, ROWS)
    summed = residual[late].astype(F32) + q[late] * mix[late]
    acc[...] += sums_of(summed, cot[late].astype(F32) * gain[...])

    @pl.when(step == pl.num_programs(0) - 1)
    def _():
        sums_ref[...] = jnp.transpose(acc[...])[:8]


def forward(wide, pos_row, cc_own, cc_own_t, bb, received, filt, residual, cot, gain):
    sent = received.shape[0]
    width = received.shape[1] // 2
    blocks = width // wide
    return pl.pallas_call(
        conv_kernel,
        grid=(blocks,),
        in_specs=[
            RESIDENT,
            RESIDENT,
            RESIDENT,
            RESIDENT,
            cols(sent, wide),
            pl.BlockSpec((sent, wide), lambda j: (0, blocks + j)),
            cols(TAPS, wide),
            cols(ROWS, wide),
            cols(ROWS, wide),
            cols(1, wide),
        ],
        out_specs=[RESIDENT] * 4 + [whole((8, TAPS))],
        out_shape=[
            pltpu.VMEM((ROWS, width), BF),
            pltpu.VMEM((ROWS, width), F32),
            pltpu.VMEM((2 * FREQ, width), BF),
            pltpu.VMEM((2 * FREQ, width), BF),
            jax.ShapeDtypeStruct((8, TAPS), F32),
        ],
        scratch_shapes=[pltpu.VMEM((ROWS, sent), BF), pltpu.VMEM((TAPS, 128), F32)],
        compiler_params=params(),
        cost_estimate=cost(4e9, width * 6000),
    )(*kept(pos_row, cc_own, cc_own_t, bb), received, received, *hbm(filt, residual, cot), gain)


def crossing(value):
    return value[:CROSS_FREQ], value[FREQ : FREQ + CROSS_FREQ]


def head_kernel(
    cc_halo, cc_head_t, halo, f_ref, q_ref, mix_ref, residual, cot, gain, sums_ref,
    mix_head_ref, out_sums_ref,
    acc,
):
    step = pl.program_id(0)

    @pl.when(step == 0)
    def _():
        acc[...] = jnp.zeros_like(acc)

    at = block_of(step, halo.shape[1])
    x = dot(cc_halo[...], halo[...])
    fr, fi = crossing(f_ref[:, at].astype(F32))
    y = spectra_product(x[:CROSS_FREQ], x[CROSS_FREQ:], fr, fi)
    mix = mix_ref[:TAPS, at] + dot(cc_head_t[...], y)
    mix_head_ref[:, at] = mix
    summed = residual[...].astype(F32) + q_ref[:TAPS, at].astype(F32) * mix
    acc[...] += sums_of(summed, cot[...].astype(F32) * gain[...])

    @pl.when(step == pl.num_programs(0) - 1)
    def _():
        out_sums_ref[:, :TAPS] = jnp.transpose(acc[...])[:8]
        out_sums_ref[:, TAPS:] = sums_ref[...]


def forward_head(wide, cc_halo, cc_head_t, halo, f, q, mix, residual, cot, gain, sums):
    width = q.shape[1]
    return pl.pallas_call(
        head_kernel,
        grid=(width // wide,),
        in_specs=[
            RESIDENT,
            RESIDENT,
            cols(TAPS, wide),
            RESIDENT,
            RESIDENT,
            RESIDENT,
            cols(TAPS, wide),
            cols(TAPS, wide),
            cols(1, wide),
            RESIDENT,
        ],
        out_specs=[RESIDENT, whole((8, ROWS))],
        out_shape=[pltpu.VMEM((TAPS, width), F32), jax.ShapeDtypeStruct((8, ROWS), F32)],
        scratch_shapes=[pltpu.VMEM((TAPS, 128), F32)],
        compiler_params=params(),
        cost_estimate=cost(6e8, width * 3000),
    )(*kept(cc_halo, cc_head_t), halo, *kept(f, q, mix), *hbm(residual, cot), gain, *kept(sums))


def prepare_kernel(
    cc_ref, bb_ref, head_ref, tail_ref, taps_ref,
    own, own_t, halo, head_t, bb, bb_t, onward_head, onward_tail_t, onward_taps,
):
    own[...] = cc_ref[:, TAPS:].astype(BF)
    own_t[...] = jnp.transpose(cc_ref[:, TAPS:]).astype(BF)
    bb[...] = bb_ref[...].astype(BF)
    bb_t[...] = jnp.transpose(bb_ref[...]).astype(BF)
    real, imag = crossing(cc_ref)
    halo[:CROSS_FREQ] = real[:, :TAPS].astype(BF)
    halo[CROSS_FREQ:] = imag[:, :TAPS].astype(BF)
    head = jnp.concatenate([real[:, TAPS : 2 * TAPS], imag[:, TAPS : 2 * TAPS]], axis=0)
    head_t[...] = jnp.transpose(head).astype(BF)
    onward_head[...] = head_ref[...].astype(BF)
    onward_tail_t[...] = jnp.transpose(tail_ref[...]).astype(BF)
    onward_taps[...] = taps_ref[...].astype(BF)


def prepare(cc, bb, head, tail, taps):
    shapes = [
        (2 * FREQ, ROWS),
        (ROWS, 2 * FREQ),
        (2 * CROSS_FREQ, TAPS),
        (TAPS, 2 * CROSS_FREQ),
        (2 * FREQ, TAPS),
        (TAPS, 2 * FREQ),
        (2 * CROSS_FREQ, TAPS),
        (TAPS, 2 * CROSS_FREQ),
        (2 * CROSS_FREQ, TAPS),
    ]
    return pl.pallas_call(
        prepare_kernel, out_shape=[pltpu.VMEM(shape, BF) for shape in shapes], compiler_params=params(False)
    )(cc, bb, head, tail, taps)


def tap_rows(pair, shape, tap_dim, step):
    tap = iota(shape, tap_dim)
    return (tap // 4) * pair + tap % 4 + 4 * (step % (pair // 4))


def extra_cols(pair, width):
    return (width // CB) * 4 // pair * CB, width // pair


def row_stats(s0, s1, s2, s3, stats):
    sums = s0[...] + s1[...] + s2[...] + s3[...]
    sums = jnp.transpose(jnp.concatenate([sums, jnp.zeros((120, ROWS), F32)], axis=0))
    inv = lax.rsqrt(sums[:, 0:1] / D + NORM_EPS)
    stats[...] = jnp.where(iota((ROWS, 128), 1) == 0, inv, sums)


def d_summed_of(stats, summed, scaled):
    inv = stats[:, 0:1]
    return inv * scaled - summed * (inv * inv * inv) * stats[:, 1:2] / D


def head_grad_kernel(
    s0, s1, s2, s3, q_ref, mix_head_ref, res_ref, cot_ref, gain_ref, head_ref, stats
):
    step = pl.program_id(0)

    @pl.when(step == 0)
    def _():
        row_stats(s0, s1, s2, s3, stats)

    at = block_of(step, res_ref.shape[1])
    q = q_ref[:TAPS, at].astype(F32)
    summed = res_ref[...].astype(F32) + q * mix_head_ref[:, at]
    d_summed = d_summed_of(stats[:TAPS], summed, cot_ref[...].astype(F32) * gain_ref[...])
    head_ref[...] = (d_summed * q).astype(BF)


def head_grad(wide, sums, q, mix_head, residual, cot, gain):
    width = q.shape[1]
    return pl.pallas_call(
        head_grad_kernel,
        grid=(width // wide,),
        in_specs=[RESIDENT] * 4
        + [RESIDENT, RESIDENT, cols(TAPS, wide), cols(TAPS, wide), cols(1, wide)],
        out_specs=cols(TAPS, wide),
        out_shape=sds((TAPS, width), BF),
        scratch_shapes=[pltpu.VMEM((ROWS, 128), F32)],
        compiler_params=params(),
        cost_estimate=cost(width * TAPS * 10, width * TAPS * 6),
    )(*kept(*sums, q, mix_head), *hbm(residual, cot), gain)


def mixture_block(mix_ref, mix_head_ref, at):
    return jnp.concatenate([mix_head_ref[:, at], mix_ref[TAPS:, at]], axis=0)


def backward_kernel(
    pair, blocks,
    s0, s1, s2, s3, pos_row, cc_own, cc_halo, bb_t, q_ref, mix_ref, mix_head_ref, x_ref,
    halo_ref, res_ref, cot_ref, gain_ref,
    dmix_ref, out_ref,
    give, stats, taps_acc, gain_acc,
):
    step = pl.program_id(0)
    per = pair // 4
    span = res_ref.shape[1]
    parts = taps_acc.shape[0]
    sent = SHARDS * pair

    @pl.when(step == 0)
    def _():
        give[...] = onehot(as_column(pos_row[...]) == iota(give.shape, 1))
        row_stats(s0, s1, s2, s3, stats)
        taps_acc[...] = jnp.zeros_like(taps_acc)
        gain_acc[...] = jnp.zeros_like(gain_acc)

    @pl.when(step < blocks)
    def _():
        at = block_of(jnp.minimum(step, blocks - 1), span)
        q = q_ref[:, at].astype(F32)
        mix = mixture_block(mix_ref, mix_head_ref, at)
        summed = res_ref[...].astype(F32) + q * mix
        cot = cot_ref[...].astype(F32)
        gain_part = jnp.sum(cot * summed * stats[:, 0:1], axis=0, keepdims=True)
        d_summed = d_summed_of(stats, summed, cot * gain_ref[...])
        out_ref[...] = dot(give[...], (d_summed * mix).astype(BF)).astype(BF)
        d_mix = (d_summed * q).astype(BF)
        dmix_ref[...] = d_mix
        g = dot(cc_own[...], d_mix)
        x = x_ref[:, at].astype(F32)
        reach = dot(cc_halo[...], halo_ref[...])
        xr = jnp.concatenate([x[:CROSS_FREQ] + reach[:CROSS_FREQ], x[CROSS_FREQ:FREQ]], axis=0)
        xi = jnp.concatenate(
            [x[FREQ : FREQ + CROSS_FREQ] + reach[CROSS_FREQ:], x[FREQ + CROSS_FREQ :]], axis=0
        )
        taps = dot(bb_t[...], conj_product(g[:FREQ], g[FREQ:], xr, xi)).astype(BF)
        for i in range(span // CB):
            block = jnp.minimum(step, blocks - 1) * (span // CB) + i
            spread = onehot(iota((sent, TAPS), 0) == tap_rows(pair, (sent, TAPS), 1, block))
            taps_acc[block // per] += dot(spread, taps[:, CB * i : CB * (i + 1)])
        wide = gain_acc.shape[1]
        for i in range(span // wide):
            row = iota(gain_acc.shape, 0) == step * (span // wide) + i
            gain_acc[...] += jnp.where(row, gain_part[:, wide * i : wide * (i + 1)], 0.0)

    def extra(at):
        if at < CB * parts:
            return taps_acc[at // CB]
        wide = gain_acc.shape[1]
        return jnp.broadcast_to(gain_acc[...][None], (SHARDS, pair, wide)).reshape(sent, wide)

    starts = [CB * part for part in range(parts + 1)]
    for late in range(pl.cdiv(starts[-1] + 1, span)):

        @pl.when(step == blocks + late)
        def _(late=late):
            for at in starts:
                if at // span == late:
                    value = extra(at).astype(BF)
                    out_ref[:, at % span : at % span + value.shape[1]] = value


def backward(pair, sums, pos_row, cc_own, cc_halo, bb_t, q, mix, mix_head, x, halo, residual, cot, gain):
    wide = max(CB, step_width(pair))
    width = q.shape[1]
    blocks = width // wide
    last = blocks - 1
    sent = SHARDS * pair
    part_cols, gain_cols = extra_cols(pair, width)
    parts = part_cols // CB
    return pl.pallas_call(
        functools.partial(backward_kernel, pair, blocks),
        grid=(blocks + pl.cdiv(part_cols + gain_cols, wide),),
        in_specs=[RESIDENT] * 4
        + [
            RESIDENT,
            RESIDENT,
            RESIDENT,
            RESIDENT,
        ]
        + [RESIDENT] * 4
        + [
            cols(TAPS, wide, last=last),
            cols(ROWS, wide, last=last),
            cols(ROWS, wide, last=last),
            cols(1, wide, last=last),
        ],
        out_specs=[cols(ROWS, wide, last=last), cols(sent, wide)],
        out_shape=[
            sds((ROWS, width), BF),
            sds((sent, width + part_cols + gain_cols), BF),
        ],
        scratch_shapes=[
            pltpu.VMEM((sent, ROWS), BF),
            pltpu.VMEM((ROWS, 128), F32),
            pltpu.VMEM((parts, sent, CB), F32),
            pltpu.VMEM((pair, gain_cols), F32),
        ],
        compiler_params=params(),
        cost_estimate=cost(2e9, width * 6000),
    )(
        *kept(*sums, pos_row, cc_own, cc_halo, bb_t, q, mix, mix_head, x), halo,
        *hbm(residual, cot), gain,
    )


def finish_kernel(
    s0, s1, s2, s3, cc_own, cc_own_t, q_ref, mix_ref, mix_head_ref, f_ref, res_ref, cot_ref,
    gain_ref, dmix_ref,
    normed_ref, dres_ref, own_ref,
    stats,
):
    step = pl.program_id(0)

    @pl.when(step == 0)
    def _():
        row_stats(s0, s1, s2, s3, stats)

    at = block_of(step, res_ref.shape[1])
    gain = gain_ref[...]
    mix = mixture_block(mix_ref, mix_head_ref, at)
    summed = res_ref[...].astype(F32) + q_ref[:, at].astype(F32) * mix
    normed_ref[...] = (summed * stats[:, 0:1] * gain).astype(BF)
    dres_ref[...] = d_summed_of(stats, summed, cot_ref[...].astype(F32) * gain).astype(BF)
    g = dot(cc_own[...], dmix_ref[...])
    f = f_ref[:, at].astype(F32)
    own_ref[...] = dot(cc_own_t[...], conj_product(g[:FREQ], g[FREQ:], f[:FREQ], f[FREQ:]))


def finish(wide, sums, cc_own, cc_own_t, q, mix, mix_head, f, residual, cot, gain, d_mix):
    width = q.shape[1]
    return pl.pallas_call(
        finish_kernel,
        grid=(width // wide,),
        in_specs=[RESIDENT] * 4
        + [RESIDENT, RESIDENT]
        + [RESIDENT] * 4
        + [cols(ROWS, wide), cols(ROWS, wide), cols(1, wide), cols(ROWS, wide)],
        out_specs=[cols(ROWS, wide)] * 3,
        out_shape=[sds((ROWS, width), BF), sds((ROWS, width), BF), sds((ROWS, width), F32)],
        scratch_shapes=[pltpu.VMEM((ROWS, 128), F32)],
        compiler_params=params(),
        cost_estimate=cost(2 * 2 * 2 * FREQ * ROWS * width, width * 6000),
    )(
        *kept(*sums, cc_own, cc_own_t, q, mix, mix_head, f), *hbm(residual, cot), gain,
        *hbm(d_mix),
    )


def give_back_kernel(pos_row, head, tail_t, taps, own_ref, next_ref, filt, out_ref, give):
    @pl.when(pl.program_id(0) == 0)
    def _():
        give[...] = onehot(as_column(pos_row[...]) == iota(give.shape, 1))

    g = dot(head[...], next_ref[...])
    f = dot(taps[...], filt[...].astype(BF))
    gr, gi, fr, fi = g[:CROSS_FREQ], g[CROSS_FREQ:], f[:CROSS_FREQ], f[CROSS_FREQ:]
    z = conj_product(gr, gi, fr, fi)
    own = own_ref[...]
    grad = jnp.concatenate(
        [own[: ROWS - TAPS], own[ROWS - TAPS :] + dot(tail_t[...], z)], axis=0
    )
    out_ref[...] = dot(give[...], grad.astype(BF)).astype(BF)


def give_back(pair, pos_row, onward, own, from_next, filt):
    wide = step_width(pair)
    width = own.shape[1]
    sent = SHARDS * pair
    return pl.pallas_call(
        give_back_kernel,
        grid=(width // wide,),
        in_specs=[
            RESIDENT,
            RESIDENT,
            RESIDENT,
            RESIDENT,
            cols(ROWS, wide),
            cols(TAPS, wide),
            cols(TAPS, wide),
        ],
        out_specs=cols(sent, wide),
        out_shape=sds((sent, width + extra_cols(pair, width)[0]), BF),
        scratch_shapes=[pltpu.VMEM((sent, ROWS), BF)],
        compiler_params=params(),
        cost_estimate=cost(2 * sent * ROWS * width, width * 2400),
    )(*kept(pos_row, *onward), *hbm(own), from_next, *hbm(filt))


def reduce_kernel(pair, taps_ref, gain_ref, rows_ref, out_ref, d_gain_ref):
    def over_sources(ref):
        value = ref[...].astype(F32)
        return jnp.sum(value.reshape(SHARDS, pair, value.shape[1]), axis=0)

    total = over_sources(taps_ref)
    out_ref[...] = (
        jnp.broadcast_to(total[None], (SHARDS, pair, CB)).reshape(SHARDS * pair, CB).astype(BF)
    )
    d_gain_ref[...] = over_sources(gain_ref)


def reduce_parts(pair, received, rows, width):
    part_cols, gain_cols = extra_cols(pair, width)
    blocks = width // CB
    sent = SHARDS * pair
    return pl.pallas_call(
        functools.partial(reduce_kernel, pair),
        grid=(part_cols // CB,),
        in_specs=[
            pl.BlockSpec((sent, CB), lambda j: (0, blocks + j)),
            pl.BlockSpec((sent, gain_cols), lambda j: (0, (width + part_cols) // gain_cols)),
            pl.BlockSpec(memory_space=pl.ANY),
        ],
        out_specs=[
            pl.BlockSpec((sent, CB), lambda j: (0, blocks + j)),
            whole((pair, gain_cols)),
        ],
        out_shape=[sds(rows.shape, BF), jax.ShapeDtypeStruct((pair, gain_cols), F32)],
        input_output_aliases={2: 0},
        compiler_params=params(),
        cost_estimate=cost(sent * part_cols, sent * part_cols * 4),
    )(received, received, *hbm(rows))


def build_home(pair, slots_ref, homes):
    for half, home in enumerate(homes):
        slot = as_column(slots_ref[2 * half : 2 * half + 1, :])
        home[...] = onehot(iota(home.shape, 1) == slot)


def homecoming(backs, homes):
    total = dot(homes[0][...], backs[0][...])
    for back, home in zip(backs[1:], homes[1:]):
        total = total + dot(home[...], back[...])
    return total


def home_rows_kernel(pair, halves, slots_ref, *refs):
    backs, out_ref, homes = refs[:halves], refs[halves], refs[halves + 1 :]

    @pl.when(pl.program_id(0) == 0)
    def _():
        build_home(pair, slots_ref, homes)

    out_ref[...] = homecoming(backs, homes).astype(BF)


def home_rows(pair, slots, backs, width):
    wide = step_width(pair)
    sent = SHARDS * pair
    halves = len(backs)
    return pl.pallas_call(
        functools.partial(home_rows_kernel, pair, halves),
        grid=(width // wide,),
        in_specs=[RESIDENT] + [cols(sent, wide)] * halves,
        out_specs=cols(SLOTS, wide),
        out_shape=sds((SLOTS, width), BF),
        scratch_shapes=[pltpu.VMEM((SLOTS, sent), BF)] * halves,
        compiler_params=params(),
        cost_estimate=cost(
            2 * sent * SLOTS * width * halves, 2 * width * (sent * halves + SLOTS)
        ),
    )(*kept(slots), *backs)


def home_product_kernel(pair, halves, slots_ref, taps_ref, k_ref, v_ref, *refs):
    backs, (dk_ref, dv_ref, filt_ref), homes = refs[:halves], refs[halves : halves + 3], refs[halves + 3 :]
    step = pl.program_id(0)

    @pl.when(step == 0)
    def _():
        build_home(pair, slots_ref, homes)

    grad = homecoming(backs, homes)
    dk_ref[...] = (grad * v_ref[...].astype(F32)).astype(BF)
    dv_ref[...] = (grad * k_ref[...].astype(F32)).astype(BF)
    shape = (TAPS, SHARDS * pair)
    for i in range(k_ref.shape[1] // CB):
        block = step * (k_ref.shape[1] // CB) + i
        gather = onehot(iota(shape, 1) == tap_rows(pair, shape, 0, block))
        part = taps_ref[:, block_of(block // (pair // 4))]
        filt_ref[:, CB * i : CB * (i + 1)] = dot(gather, part)


def home_product(pair, slots, back, backs, k, v):
    wide = max(CB, step_width(pair))
    width = k.shape[1]
    part_cols = extra_cols(pair, width)[0]
    sent = SHARDS * pair
    halves = len(backs)
    return pl.pallas_call(
        functools.partial(home_product_kernel, pair, halves),
        grid=(width // wide,),
        in_specs=[
            RESIDENT,
            pl.BlockSpec((sent, part_cols), lambda j: (0, width // part_cols)),
            cols(SLOTS, wide),
            cols(SLOTS, wide),
        ]
        + [cols(sent, wide)] * halves,
        out_specs=[cols(SLOTS, wide), cols(SLOTS, wide), cols(TAPS, wide)],
        out_shape=[sds((SLOTS, width), BF), sds((SLOTS, width), BF), sds((TAPS, width), F32)],
        scratch_shapes=[pltpu.VMEM((SLOTS, sent), BF)] * halves,
        compiler_params=params(),
        cost_estimate=cost(2 * sent * SLOTS * width, 2 * width * (sent + 5 * SLOTS)),
    )(*kept(slots), back, *hbm(k, v), *backs)


def exchange(pair, rows):
    shards = rows.reshape(SHARDS, pair, rows.shape[1])
    return lax.all_to_all(shards, "seq", split_axis=0, concat_axis=0, tiled=True).reshape(
        rows.shape
    )


def shift(value, steps):
    pairs = [(i, i + steps) for i in range(SHARDS) if 0 <= i + steps < SHARDS]
    return lax.ppermute(value, "seq", pairs)


def swap(value):
    return lax.ppermute(value, "seq", [(i, i ^ 1) for i in range(SHARDS)])


def slot_positions(pair, dest_pos, my_index):
    holders = SHARDS * pair // PAIR
    table = dest_pos.reshape(holders, -1)
    arriving = (table >= 0) & (table // ROWS == my_index)
    row = jnp.arange(table.shape[1], dtype=I32)
    before = (row[:, None] < row[None, :]).astype(BF)
    rank = jnp.dot(arriving.astype(BF), before, preferred_element_type=F32).astype(I32)
    rank = jnp.where(arriving, rank, -1)
    target = table - my_index * ROWS + 1
    order = jnp.arange(PAIR, dtype=I32)
    if pair != PAIR:
        order = (order % pair) * 2 + order // pair
    hit = rank[:, None, :] == order[None, :, None]
    return (jnp.sum(jnp.where(hit, target[:, None, :], 0), axis=2) - 1).reshape(SHARDS * pair)


def layer(pair, others, q_in, k_in, v_in, dest_pos, doc_ids, mr_filter, norm_gain, residual, cotangent):
    my_index = lax.axis_index("seq")
    width = q_in.shape[1]
    wide = step_width(pair)
    gain = norm_gain[None, :]
    shared = pair != PAIR

    slots = send_plan(pair, my_index, dest_pos)
    if shared:
        product_in, product_other, q_other = others
        early, late = [*hbm(product_in), product_other], [*hbm(q_in), q_other]
    else:
        early, late = hbm(k_in, v_in), hbm(q_in)
    sent_rows = pack_arrivals(pair, slots, early, late)
    sent_rows, dest_later, docs_later, slots = lax.optimization_barrier(
        (sent_rows, dest_pos, doc_ids, slots)
    )
    received = exchange(pair, sent_rows)

    pos = slot_positions(pair, dest_later, my_index)
    pos_row = pos[None, :]
    docs_all = jnp.concatenate(
        [jnp.full((TAPS,), -1, I32), docs_later, jnp.full((TAPS,), -2, I32)]
    )
    docs = lax.dynamic_slice_in_dim(docs_all, my_index * ROWS, WIN + TAPS)
    cc, bb = segment_dft(docs[:WIN])
    onward = crossing_dft(docs[TAPS:WIN], docs[WIN:])
    prepared = prepare(cc, bb, *onward)
    received, pos_row, prepared = lax.optimization_barrier((received, pos_row, prepared))
    cc_own, cc_own_t, cc_halo, cc_head_t, bb, bb_t, *onward = prepared

    halo = shift(place_tail(wide, pos_row, received, width), 1)
    q, mix, x, f, sums = forward(
        wide, pos_row, cc_own, cc_own_t, bb, received, mr_filter, residual, cotangent, gain
    )
    mix_head, sums = forward_head(
        wide, cc_halo, cc_head_t, halo, f, q, mix, residual, cotangent, gain, sums
    )
    all_sums = [sums] + [
        lax.ppermute(sums, "mp", [(i, (i + k) % 4) for i in range(4)]) for k in (1, 2, 3)
    ]
    head = head_grad(wide, all_sums, q, mix_head, residual, cotangent, gain)
    d_mix, sent_dq = backward(
        pair, all_sums, pos_row, cc_own, cc_halo, bb_t, q, mix, mix_head, x, halo,
        residual, cotangent, gain,
    )
    sent_dq, from_next = lax.optimization_barrier((sent_dq, shift(head, -1)))
    back_q = exchange(pair, sent_dq)
    normed, d_residual, own_grad = finish(
        wide, all_sums, cc_own, cc_own_t, q, mix, mix_head, f, residual, cotangent, gain, d_mix
    )
    rows = give_back(pair, pos_row, onward, own_grad, from_next, mr_filter)
    sent_dp, d_gain = reduce_parts(pair, back_q, rows, width)
    back_p = exchange(pair, sent_dp)
    backs_q, backs_p = [back_q], [back_p]
    if shared:
        backs_q.append(swap(back_q[:, :width]))
        backs_p.append(swap(back_p[:, :width]))
    d_q_in = home_rows(pair, slots, backs_q, width)
    d_k_in, d_v_in, d_filter = home_product(pair, slots, back_p, backs_p, k_in, v_in)
    return (normed, d_residual, d_q_in, d_k_in, d_v_in, d_filter, d_gain.reshape(width))


def fits_shared(dest_pos):
    chips = dest_pos.reshape(SHARDS // 2, 2 * SLOTS)
    owner = jnp.where(chips >= 0, chips // ROWS, -1)
    load = jnp.sum(
        (owner[:, None, :] == jnp.arange(SHARDS, dtype=I32)[None, :, None]).astype(I32), axis=2
    )
    return jnp.max(load) <= PAIR


def body(q_in, k_in, v_in, dest_pos, *rest):
    product_in = slot_product(k_in, v_in)
    others = (product_in, swap(product_in), swap(q_in))
    return lax.cond(
        fits_shared(dest_pos),
        functools.partial(layer, PAIR // 2),
        functools.partial(layer, PAIR),
        others, q_in, k_in, v_in, dest_pos, *rest,
    )


def solution(mesh):
    return jax.shard_map(
        body,
        mesh=mesh,
        in_specs=(
            P("seq", "mp"),
            P("seq", "mp"),
            P("seq", "mp"),
            P(),
            P(),
            P(None, "mp"),
            P("mp"),
            P("seq", "mp"),
            P("seq", "mp"),
        ),
        out_specs=(
            P("seq", "mp"),
            P("seq", "mp"),
            P("seq", "mp"),
            P("seq", "mp"),
            P("seq", "mp"),
            P(None, "mp"),
            P("mp"),
        ),
        check_vma=False,
    )
```

```python
import functools
import math

import jax
import jax.numpy as jnp
from jax import lax
from jax.experimental import pallas as pl
from jax.experimental.pallas import tpu as pltpu
from jax.sharding import PartitionSpec as P

D = 8192
NORM_EPS = 1e-06
NDOCS = 64
BF = jnp.bfloat16
F32 = jnp.float32
I32 = jnp.int32

ROWS = 256
SLOTS = 384
TAPS = 128
SHARDS = 32
PAIR = 16
WIN = TAPS + ROWS
FREQ = 320
CB = 512
WIDE, NARROW = 1024, 128


def step_width(pair):
    return NARROW if pair == PAIR else WIDE


def dot(a, b):
    return jnp.dot(a, b, preferred_element_type=F32)


def iota(shape, dim):
    return lax.broadcasted_iota(I32, shape, dim)


def onehot(match):
    return jnp.where(match, 1.0, 0.0).astype(BF)


def params(grid=True):
    return pltpu.CompilerParams(
        dimension_semantics=("arbitrary",) if grid else None, vmem_limit_bytes=36 * 1024 * 1024
    )


def cols(rows, width=CB, last=None):
    if last is None:
        return pl.BlockSpec((rows, width), lambda j: (0, j))
    return pl.BlockSpec((rows, width), lambda j: (0, jnp.minimum(j, last)))


RESIDENT = pl.BlockSpec(memory_space=pltpu.VMEM)


def block_of(step, width=CB):
    return pl.ds(pl.multiple_of(step * width, width), width)


def whole(shape):
    return pl.BlockSpec(shape, lambda j: (0,) * len(shape))


def cost(flops, nbytes):
    return pl.CostEstimate(flops=int(flops), transcendentals=0, bytes_accessed=int(nbytes))


def hbm(*values):
    return [pltpu.with_memory_space_constraint(v, pltpu.HBM) for v in values]


def kept(*values):
    return [pltpu.with_memory_space_constraint(v, pltpu.VMEM) for v in values]


def sds(shape, dtype):
    return pltpu.HBM(shape, dtype)


def owners_of(table_ref, index):
    rows = [table_ref[pl.ds(3 * index + i, 1), :] for i in range(3)]
    plan = jnp.concatenate(rows, axis=1)
    return jnp.where(plan >= 0, plan // ROWS, -1)


def as_column(row):
    return jnp.transpose(jnp.broadcast_to(row, (128, row.shape[1])))[:, 0:1]


def slots_of(pair, core, half, owner, owner_col, sibling_col):
    early = iota((SLOTS, SLOTS), 0) < iota((SLOTS, SLOTS), 1)
    same = jnp.where((owner_col == owner) & early, 1, 0)
    rank = jnp.sum(same, axis=0, keepdims=True)
    if pair == PAIR:
        return jnp.where(owner >= 0, owner * pair + rank, -1)
    before = jnp.sum(jnp.where(sibling_col == owner, 1, 0), axis=0, keepdims=True)
    mine = core if half == 0 else 1 - core
    rank = rank + mine * before
    return jnp.where((owner >= 0) & (rank % 2 == core), owner * pair + rank // 2, -1)


def plan_kernel(pair, index_ref, table_ref, slots_ref):
    index = index_ref[0]
    core = index % 2
    own = owners_of(table_ref, index)
    own_col = as_column(own)
    if pair == PAIR:
        slots_ref[...] = jnp.broadcast_to(
            slots_of(pair, core, 0, own, own_col, None), (8, SLOTS)
        )
        return
    other = owners_of(table_ref, index + 1 - 2 * core)
    other_col = as_column(other)
    first = slots_of(pair, core, 0, own, own_col, other_col)
    second = slots_of(pair, core, 1, other, other_col, own_col)
    theirs = slots_of(pair, 1 - core, 1, own, own_col, other_col)
    slots_ref[...] = jnp.concatenate(
        [first, second, theirs, jnp.full((5, SLOTS), -1, I32)], axis=0
    )


def send_plan(pair, my_index, dest_pos):
    return pl.pallas_call(
        functools.partial(plan_kernel, pair),
        grid_spec=pltpu.PrefetchScalarGridSpec(
            num_scalar_prefetch=1,
            grid=(1,),
            in_specs=[pl.BlockSpec((SHARDS * SLOTS // 128, 128), lambda j, ref: (0, 0))],
            out_specs=pl.BlockSpec((8, SLOTS), lambda j, ref: (0, 0)),
        ),
        out_shape=jax.ShapeDtypeStruct((8, SLOTS), I32),
        compiler_params=params(),
    )(my_index.reshape(1), dest_pos.reshape(SHARDS * SLOTS // 128, 128))


def build_pack(slots_ref, packs):
    for half, pack in enumerate(packs):
        pack[...] = onehot(iota(pack.shape, 0) == slots_ref[half : half + 1, :])


def pack_kernel(halves, blocks, slots_ref, *refs):
    first, second = refs[: 2 * halves : 2], refs[1 : 2 * halves : 2]
    q_refs, out_ref, packs = refs[2:3], refs[3], refs[4:]
    if halves == 2:
        first, second, q_refs, out_ref, packs = None, refs[:2], refs[2:4], refs[4], refs[5:]
    step = pl.program_id(0)
    wide = out_ref.shape[1]

    @pl.when(step == 0)
    def _():
        build_pack(slots_ref, packs)

    def packed(values):
        total = dot(packs[0][...], values[0])
        for value, pack in zip(values[1:], packs[1:]):
            total = total + dot(pack[...], value)
        return total.astype(BF)

    @pl.when(step < blocks)
    def _():
        if first is None:
            out_ref[...] = packed([second[0][...], second[1][:, block_of(step, wide)]])
        else:
            product = first[0][...].astype(F32) * second[0][...].astype(F32)
            out_ref[...] = packed([product.astype(BF)])

    @pl.when(step >= blocks)
    def _():
        rows = [q_refs[0][...]]
        if halves == 2:
            rows.append(q_refs[1][:, block_of(step - blocks, wide)])
        out_ref[...] = packed(rows)


def pack_arrivals(pair, slots, early, late):
    wide = step_width(pair)
    width = early[0].shape[1]
    blocks = width // wide
    halves = len(late)
    sent = SHARDS * pair
    return pl.pallas_call(
        functools.partial(pack_kernel, halves, blocks),
        grid=(2 * blocks,),
        in_specs=[RESIDENT]
        + [cols(SLOTS, wide, last=blocks - 1)]
        + [RESIDENT if halves == 2 else cols(SLOTS, wide, last=blocks - 1)]
        + [pl.BlockSpec((SLOTS, wide), lambda j: (0, jnp.maximum(j - blocks, 0)))]
        + [RESIDENT] * (halves - 1),
        out_specs=cols(sent, wide),
        out_shape=sds((sent, 2 * width), BF),
        scratch_shapes=[pltpu.VMEM((sent, SLOTS), BF)] * halves,
        compiler_params=params(),
        cost_estimate=cost(4 * sent * SLOTS * width * halves, 4 * width * (sent + SLOTS * 2)),
    )(*kept(slots), *early, *late)


def product_kernel(k_ref, v_ref, out_ref):
    out_ref[...] = (k_ref[...].astype(F32) * v_ref[...].astype(F32)).astype(BF)


def slot_product(k, v):
    width = k.shape[1]
    return pl.pallas_call(
        product_kernel,
        grid=(width // WIDE,),
        in_specs=[cols(SLOTS, WIDE)] * 2,
        out_specs=cols(SLOTS, WIDE),
        out_shape=sds((SLOTS, width), BF),
        compiler_params=params(),
        cost_estimate=cost(SLOTS * width, 6 * width * SLOTS),
    )(*hbm(k, v))


def place_tail_kernel(pos_row, recv_ref, tail_ref, place):
    @pl.when(pl.program_id(0) == 0)
    def _():
        place[...] = onehot(iota(place.shape, 0) + (ROWS - TAPS) == pos_row[...])

    tail_ref[...] = dot(place[...], recv_ref[:, block_of(pl.program_id(0), tail_ref.shape[1])]).astype(BF)


def place_tail(wide, pos_row, received, width):
    sent = received.shape[0]
    return pl.pallas_call(
        place_tail_kernel,
        grid=(width // wide,),
        in_specs=[RESIDENT, RESIDENT],
        out_specs=cols(TAPS, wide),
        out_shape=sds((TAPS, width), BF),
        scratch_shapes=[pltpu.VMEM((TAPS, sent), BF)],
        compiler_params=params(),
        cost_estimate=cost(2 * sent * TAPS * width, 2 * width * (sent + TAPS)),
    )(*kept(pos_row, received))


def wave_of(turns):
    square = (turns * turns) * (4.0 * math.pi * math.pi)

    def series(first):
        total = jnp.zeros_like(square)
        for power in range(first + 16, first - 1, -2):
            term = (-1.0) ** ((power - first) // 2) / math.factorial(power)
            total = total * square + term
        return total

    return series(0), series(1) * (turns * (-2.0 * math.pi))


def segment_dft(docs_window):
    place = jnp.arange(WIN, dtype=I32)
    docs = jnp.where(place >= 1, docs_window, -1)
    ids = jnp.arange(NDOCS, dtype=I32)
    inside = docs[None, :] == ids[:, None]
    span = jnp.sum(inside.astype(I32), axis=1)
    own = jnp.sum((inside & (place >= TAPS)[None, :]).astype(I32), axis=1)
    first = jnp.min(jnp.where(inside, place[None, :], 2 * WIN), axis=1)
    taps = jnp.minimum(TAPS, span)
    length = jnp.maximum(span, own + taps - 1)
    length = length + 1 - length % 2
    slots = jnp.where(own > 0, (length + 1) // 2, 0)
    start = jnp.sum(jnp.where(ids[None, :] < ids[:, None], slots[None, :], 0), axis=1)
    slot = jnp.arange(FREQ, dtype=I32)[:, None]
    member = (slot >= start[None, :]) & (slot < (start + slots)[None, :])

    def pick(value):
        return jnp.sum(jnp.where(member, value[None, :], 0), axis=1, keepdims=True)

    live = pick(jnp.ones_like(ids)) > 0
    doc = jnp.where(live, pick(ids), -9)
    wave = slot - pick(start)
    size = jnp.where(live, pick(length), 1)
    size_f = size.astype(F32)
    inverse = 1.0 / size_f

    def waves(steps):
        turns = (wave * steps).astype(F32)
        turns = turns - jnp.round(turns * inverse) * size_f
        return wave_of(turns * inverse)

    real, imag = waves(place[None, :] - pick(first))
    mask = docs[None, :] == doc
    spectrum = jnp.where(
        jnp.concatenate([mask, mask], axis=0), jnp.concatenate([real, imag], axis=0), 0.0
    )
    lag = jnp.arange(TAPS, dtype=I32)[None, :]
    real, imag = waves(lag)
    weight = jnp.where(
        live & (lag < pick(taps)), jnp.where(wave == 0, inverse, 2.0 * inverse), 0.0
    )
    taps_spectrum = jnp.concatenate([weight * real, weight * imag], axis=0)
    return spectrum, taps_spectrum


CROSS = TAPS + ROWS - 1
CROSS_FREQ = (CROSS + 1) // 2


def crossing_dft(own_docs, next_docs):
    wave = jnp.arange(CROSS_FREQ, dtype=I32)[:, None]
    place = jnp.arange(TAPS, dtype=I32)[None, :]

    def waves(steps):
        turns = (wave * steps).astype(F32)
        turns = turns - jnp.round(turns * (1.0 / CROSS)) * CROSS
        return jnp.concatenate(wave_of(turns * (1.0 / CROSS)), axis=0)

    document = own_docs[ROWS - 1]
    head = jnp.where((next_docs == document)[None, :], waves(place + TAPS), 0.0)
    tail = jnp.where((own_docs[ROWS - TAPS :] == document)[None, :], waves(place), 0.0)
    weight = jnp.where(wave == 0, 1.0, 2.0) / CROSS
    taps = jnp.concatenate([weight, weight], axis=0) * waves(place)
    return head, tail, taps


def spectra_product(xr, xi, fr, fi):
    return jnp.concatenate(
        [(xr * fr - xi * fi).astype(BF), (xr * fi + xi * fr).astype(BF)], axis=0
    )


def conj_product(gr, gi, fr, fi):
    return jnp.concatenate(
        [(gr * fr + gi * fi).astype(BF), (gi * fr - gr * fi).astype(BF)], axis=0
    )


def sums_of(summed, scaled):
    squares = jnp.sum(summed * summed, axis=1, keepdims=True)
    dots = jnp.sum(scaled * summed, axis=1, keepdims=True)
    lane = iota((summed.shape[0], 128), 1)
    return jnp.where(lane == 0, squares, jnp.where(lane == 1, dots, 0.0))


def conv_kernel(
    pos_row, cc_own, cc_own_t, bb, recv, filt, residual, cot, gain,
    q_ref, mix_ref, x_ref, f_ref, sums_ref,
    place, acc,
):
    step = pl.program_id(0)

    @pl.when(step == 0)
    def _():
        place[...] = onehot(iota(place.shape, 0) == pos_row[...])
        acc[...] = jnp.zeros_like(acc)

    at = block_of(step, filt.shape[1])
    product = dot(place[...], recv[:, at]).astype(BF)
    q = dot(place[...], recv[:, block_of(step + pl.num_programs(0), filt.shape[1])])
    q_ref[:, at] = q.astype(BF)
    x = dot(cc_own[...], product)
    f = dot(bb[...], filt[...].astype(BF))
    x_ref[:, at] = x.astype(BF)
    f_ref[:, at] = f.astype(BF)
    mix = dot(cc_own_t[...], spectra_product(x[:FREQ], x[FREQ:], f[:FREQ], f[FREQ:]))
    mix_ref[:, at] = mix
    late = slice(TAPS, ROWS)
    summed = residual[late].astype(F32) + q[late] * mix[late]
    acc[...] += sums_of(summed, cot[late].astype(F32) * gain[...])

    @pl.when(step == pl.num_programs(0) - 1)
    def _():
        sums_ref[...] = jnp.transpose(acc[...])[:8]


def forward(wide, pos_row, cc_own, cc_own_t, bb, received, filt, residual, cot, gain):
    sent = received.shape[0]
    width = received.shape[1] // 2
    blocks = width // wide
    return pl.pallas_call(
        conv_kernel,
        grid=(blocks,),
        in_specs=[
            RESIDENT,
            RESIDENT,
            RESIDENT,
            RESIDENT,
            RESIDENT,
            cols(TAPS, wide),
            cols(ROWS, wide),
            cols(ROWS, wide),
            cols(1, wide),
        ],
        out_specs=[RESIDENT] * 4 + [whole((8, TAPS))],
        out_shape=[
            pltpu.VMEM((ROWS, width), BF),
            pltpu.VMEM((ROWS, width), F32),
            pltpu.VMEM((2 * FREQ, width), BF),
            pltpu.VMEM((2 * FREQ, width), BF),
            jax.ShapeDtypeStruct((8, TAPS), F32),
        ],
        scratch_shapes=[pltpu.VMEM((ROWS, sent), BF), pltpu.VMEM((TAPS, 128), F32)],
        compiler_params=params(),
        cost_estimate=cost(4e9, width * 6000),
    )(*kept(pos_row, cc_own, cc_own_t, bb, received), *hbm(filt, residual, cot), gain)


def crossing(value):
    return value[:CROSS_FREQ], value[FREQ : FREQ + CROSS_FREQ]


def head_kernel(
    cc_halo, cc_head_t, halo, f_ref, q_ref, mix_ref, residual, cot, gain, sums_ref,
    mix_head_ref, summed_ref, scaled_ref, out_sums_ref,
    acc,
):
    step = pl.program_id(0)

    @pl.when(step == 0)
    def _():
        acc[...] = jnp.zeros_like(acc)

    at = block_of(step, halo.shape[1])
    x = dot(cc_halo[...], halo[...])
    fr, fi = crossing(f_ref[:, at].astype(F32))
    y = spectra_product(x[:CROSS_FREQ], x[CROSS_FREQ:], fr, fi)
    mix = mix_ref[:TAPS, at] + dot(cc_head_t[...], y)
    mix_head_ref[:, at] = mix
    summed = residual[...].astype(F32) + q_ref[:TAPS, at].astype(F32) * mix
    scaled = cot[...].astype(F32) * gain[...]
    summed_ref[:, at] = summed
    scaled_ref[:, at] = scaled
    acc[...] += sums_of(summed, scaled)

    @pl.when(step == pl.num_programs(0) - 1)
    def _():
        out_sums_ref[:, :TAPS] = jnp.transpose(acc[...])[:8]
        out_sums_ref[:, TAPS:] = sums_ref[...]


def forward_head(wide, cc_halo, cc_head_t, halo, f, q, mix, residual, cot, gain, sums):
    width = q.shape[1]
    return pl.pallas_call(
        head_kernel,
        grid=(width // wide,),
        in_specs=[
            RESIDENT,
            RESIDENT,
            cols(TAPS, wide),
            RESIDENT,
            RESIDENT,
            RESIDENT,
            cols(TAPS, wide),
            cols(TAPS, wide),
            cols(1, wide),
            RESIDENT,
        ],
        out_specs=[RESIDENT] * 3 + [whole((8, ROWS))],
        out_shape=[pltpu.VMEM((TAPS, width), F32)] * 3 + [jax.ShapeDtypeStruct((8, ROWS), F32)],
        scratch_shapes=[pltpu.VMEM((TAPS, 128), F32)],
        compiler_params=params(),
        cost_estimate=cost(6e8, width * 3000),
    )(*kept(cc_halo, cc_head_t), halo, *kept(f, q, mix), *hbm(residual, cot), gain, *kept(sums))


def prepare_kernel(
    cc_ref, bb_ref, head_ref, tail_ref, taps_ref,
    own, own_t, halo, head_t, bb, bb_t, onward_head, onward_tail_t, onward_taps,
):
    own[...] = cc_ref[:, TAPS:].astype(BF)
    own_t[...] = jnp.transpose(cc_ref[:, TAPS:]).astype(BF)
    bb[...] = bb_ref[...].astype(BF)
    bb_t[...] = jnp.transpose(bb_ref[...]).astype(BF)
    real, imag = crossing(cc_ref)
    halo[:CROSS_FREQ] = real[:, :TAPS].astype(BF)
    halo[CROSS_FREQ:] = imag[:, :TAPS].astype(BF)
    head = jnp.concatenate([real[:, TAPS : 2 * TAPS], imag[:, TAPS : 2 * TAPS]], axis=0)
    head_t[...] = jnp.transpose(head).astype(BF)
    onward_head[...] = head_ref[...].astype(BF)
    onward_tail_t[...] = jnp.transpose(tail_ref[...]).astype(BF)
    onward_taps[...] = taps_ref[...].astype(BF)


def prepare(cc, bb, head, tail, taps):
    shapes = [
        (2 * FREQ, ROWS),
        (ROWS, 2 * FREQ),
        (2 * CROSS_FREQ, TAPS),
        (TAPS, 2 * CROSS_FREQ),
        (2 * FREQ, TAPS),
        (TAPS, 2 * FREQ),
        (2 * CROSS_FREQ, TAPS),
        (TAPS, 2 * CROSS_FREQ),
        (2 * CROSS_FREQ, TAPS),
    ]
    return pl.pallas_call(
        prepare_kernel, out_shape=[pltpu.VMEM(shape, BF) for shape in shapes], compiler_params=params(False)
    )(cc, bb, head, tail, taps)


def tap_rows(pair, shape, tap_dim, block):
    tap = iota(shape, tap_dim)
    return (tap // 4) * pair + tap % 4 + 4 * block


def part_cols(pair):
    return 4 * WIDE // pair


def piece_cols(pair):
    return WIDE + part_cols(pair) + 128


def row_stats(s0, s1, s2, s3, stats):
    sums = s0[...] + s1[...] + s2[...] + s3[...]
    sums = jnp.transpose(jnp.concatenate([sums, jnp.zeros((120, ROWS), F32)], axis=0))
    inv = lax.rsqrt(sums[:, 0:1] / D + NORM_EPS)
    stats[...] = jnp.where(iota((ROWS, 128), 1) == 0, inv, sums)


def d_summed_of(stats, summed, scaled):
    inv = stats[:, 0:1]
    return inv * scaled - summed * (inv * inv * inv) * stats[:, 1:2] / D


def head_grad_kernel(s0, s1, s2, s3, q_ref, summed_ref, scaled_ref, head_ref, stats):
    step = pl.program_id(0)

    @pl.when(step == 0)
    def _():
        row_stats(s0, s1, s2, s3, stats)

    at = block_of(step, head_ref.shape[1])
    d_summed = d_summed_of(stats[:TAPS], summed_ref[:, at], scaled_ref[:, at])
    head_ref[...] = (d_summed * q_ref[:TAPS, at].astype(F32)).astype(BF)


def head_grad(wide, sums, q, summed_head, scaled_head):
    width = q.shape[1]
    return pl.pallas_call(
        head_grad_kernel,
        grid=(width // wide,),
        in_specs=[RESIDENT] * 7,
        out_specs=cols(TAPS, wide),
        out_shape=sds((TAPS, width), BF),
        scratch_shapes=[pltpu.VMEM((ROWS, 128), F32)],
        compiler_params=params(),
        cost_estimate=cost(width * TAPS * 10, width * TAPS * 6),
    )(*kept(*sums, q, summed_head, scaled_head))


def mixture_block(mix_ref, mix_head_ref, at):
    return jnp.concatenate([mix_head_ref[:, at], mix_ref[TAPS:, at]], axis=0)


def backward_kernel(
    pair,
    s0, s1, s2, s3, pos_row, cc_own, cc_halo, bb_t, q_ref, mix_ref, mix_head_ref, x_ref,
    halo_ref, res_ref, cot_ref, gain_ref,
    dmix_ref, out_ref,
    give, stats,
):
    step = pl.program_id(0)
    part = part_cols(pair)
    sent = SHARDS * pair

    @pl.when(step == 0)
    def _():
        give[...] = onehot(as_column(pos_row[...]) == iota(give.shape, 1))
        row_stats(s0, s1, s2, s3, stats)

    at = block_of(step, WIDE)
    q = q_ref[:, at].astype(F32)
    mix = mixture_block(mix_ref, mix_head_ref, at)
    summed = res_ref[...].astype(F32) + q * mix
    cot = cot_ref[...].astype(F32)
    gain_part = jnp.sum(cot * summed * stats[:, 0:1], axis=0, keepdims=True)
    d_summed = d_summed_of(stats, summed, cot * gain_ref[...])
    out_ref[:, :WIDE] = dot(give[...], (d_summed * mix).astype(BF)).astype(BF)
    d_mix = (d_summed * q).astype(BF)
    dmix_ref[...] = d_mix
    g = dot(cc_own[...], d_mix)
    x = x_ref[:, at].astype(F32)
    reach = dot(cc_halo[...], halo_ref[...])
    xr = jnp.concatenate([x[:CROSS_FREQ] + reach[:CROSS_FREQ], x[CROSS_FREQ:FREQ]], axis=0)
    xi = jnp.concatenate(
        [x[FREQ : FREQ + CROSS_FREQ] + reach[CROSS_FREQ:], x[FREQ + CROSS_FREQ :]], axis=0
    )
    taps = dot(bb_t[...], conj_product(g[:FREQ], g[FREQ:], xr, xi)).astype(BF)
    total = jnp.zeros((sent, part), F32)
    for block in range(WIDE // part):
        spread = onehot(iota((sent, TAPS), 0) == tap_rows(pair, (sent, TAPS), 1, block))
        total = total + dot(spread, taps[:, part * block : part * (block + 1)])
    out_ref[:, WIDE : WIDE + part] = total.astype(BF)
    rows = [gain_part[:, 128 * r : 128 * (r + 1)] for r in range(WIDE // 128)]
    rows = jnp.concatenate(rows + [jnp.zeros((pair - len(rows), 128), F32)] * (pair > len(rows)), axis=0)
    rows = jnp.broadcast_to(rows[None], (SHARDS, pair, 128)).reshape(sent, 128)
    out_ref[:, WIDE + part :] = rows.astype(BF)


def backward(pair, sums, pos_row, cc_own, cc_halo, bb_t, q, mix, mix_head, x, halo, residual, cot, gain):
    width = q.shape[1]
    steps = width // WIDE
    sent = SHARDS * pair
    return pl.pallas_call(
        functools.partial(backward_kernel, pair),
        grid=(steps,),
        in_specs=[RESIDENT] * 12
        + [cols(TAPS, WIDE), cols(ROWS, WIDE), cols(ROWS, WIDE), cols(1, WIDE)],
        out_specs=[cols(ROWS, WIDE), cols(sent, piece_cols(pair))],
        out_shape=[sds((ROWS, width), BF), sds((sent, steps * piece_cols(pair)), BF)],
        scratch_shapes=[pltpu.VMEM((sent, ROWS), BF), pltpu.VMEM((ROWS, 128), F32)],
        compiler_params=params(),
        cost_estimate=cost(2e9, width * 6000),
    )(
        *kept(*sums, pos_row, cc_own, cc_halo, bb_t, q, mix, mix_head, x), halo,
        *hbm(residual, cot), gain,
    )


def finish_kernel(
    s0, s1, s2, s3, cc_own, cc_own_t, q_ref, mix_ref, mix_head_ref, f_ref, res_ref, cot_ref,
    gain_ref, dmix_ref,
    normed_ref, dres_ref, own_ref,
    stats,
):
    step = pl.program_id(0)

    @pl.when(step == 0)
    def _():
        row_stats(s0, s1, s2, s3, stats)

    at = block_of(step, res_ref.shape[1])
    gain = gain_ref[...]
    mix = mixture_block(mix_ref, mix_head_ref, at)
    summed = res_ref[...].astype(F32) + q_ref[:, at].astype(F32) * mix
    normed_ref[...] = (summed * stats[:, 0:1] * gain).astype(BF)
    dres_ref[...] = d_summed_of(stats, summed, cot_ref[...].astype(F32) * gain).astype(BF)
    g = dot(cc_own[...], dmix_ref[...])
    f = f_ref[:, at].astype(F32)
    own_ref[...] = dot(cc_own_t[...], conj_product(g[:FREQ], g[FREQ:], f[:FREQ], f[FREQ:]))


def finish(wide, sums, cc_own, cc_own_t, q, mix, mix_head, f, residual, cot, gain, d_mix):
    width = q.shape[1]
    return pl.pallas_call(
        finish_kernel,
        grid=(width // wide,),
        in_specs=[RESIDENT] * 4
        + [RESIDENT, RESIDENT]
        + [RESIDENT] * 4
        + [cols(ROWS, wide), cols(ROWS, wide), cols(1, wide), cols(ROWS, wide)],
        out_specs=[cols(ROWS, wide)] * 3,
        out_shape=[sds((ROWS, width), BF), sds((ROWS, width), BF), sds((ROWS, width), F32)],
        scratch_shapes=[pltpu.VMEM((ROWS, 128), F32)],
        compiler_params=params(),
        cost_estimate=cost(2 * 2 * 2 * FREQ * ROWS * width, width * 6000),
    )(
        *kept(*sums, cc_own, cc_own_t, q, mix, mix_head, f), *hbm(residual, cot), gain,
        *hbm(d_mix),
    )


def give_back_kernel(pos_row, head, tail_t, taps, own_ref, next_ref, filt, out_ref, give):
    @pl.when(pl.program_id(0) == 0)
    def _():
        give[...] = onehot(as_column(pos_row[...]) == iota(give.shape, 1))

    g = dot(head[...], next_ref[...])
    f = dot(taps[...], filt[...].astype(BF))
    gr, gi, fr, fi = g[:CROSS_FREQ], g[CROSS_FREQ:], f[:CROSS_FREQ], f[CROSS_FREQ:]
    z = conj_product(gr, gi, fr, fi)
    own = own_ref[...]
    grad = jnp.concatenate(
        [own[: ROWS - TAPS], own[ROWS - TAPS :] + dot(tail_t[...], z)], axis=0
    )
    out_ref[...] = dot(give[...], grad.astype(BF)).astype(BF)


def give_back(pair, pos_row, onward, own, from_next, filt):
    wide = step_width(pair)
    width = own.shape[1]
    sent = SHARDS * pair
    return pl.pallas_call(
        give_back_kernel,
        grid=(width // wide,),
        in_specs=[
            RESIDENT,
            RESIDENT,
            RESIDENT,
            RESIDENT,
            cols(ROWS, wide),
            cols(TAPS, wide),
            cols(TAPS, wide),
        ],
        out_specs=cols(sent, wide),
        out_shape=sds((sent, width + CB), BF),
        scratch_shapes=[pltpu.VMEM((sent, ROWS), BF)],
        compiler_params=params(),
        cost_estimate=cost(2 * sent * ROWS * width, width * 2400),
    )(*kept(pos_row, *onward), *hbm(own), from_next, *hbm(filt))


def reduce_kernel(pair, pieces, received_ref, rows_ref, out_ref, d_gain_ref):
    def over_sources(at, size):
        value = received_ref[:, at : at + size].astype(F32)
        return jnp.sum(value.reshape(SHARDS, pair, size), axis=0)

    part = part_cols(pair)
    starts = [piece_cols(pair) * piece + WIDE for piece in range(pieces)]
    totals = [over_sources(at, part) for at in starts]
    if pair == PAIR:
        both = jnp.broadcast_to(jnp.concatenate(totals, axis=1)[None], (SHARDS, pair, CB))
    else:
        both = jnp.broadcast_to(
            jnp.concatenate(totals, axis=0)[None], (SHARDS // 2, 2 * pair, CB)
        )
    out_ref[...] = both.reshape(SHARDS * pair, CB).astype(BF)
    for piece, at in enumerate(starts):
        d_gain_ref[piece] = over_sources(at + part, 128)[:8]


def reduce_parts(pair, received, rows, width):
    sent = SHARDS * pair
    pieces = width // WIDE
    return pl.pallas_call(
        functools.partial(reduce_kernel, pair, pieces),
        grid=(1,),
        in_specs=[RESIDENT, pl.BlockSpec(memory_space=pl.ANY)],
        out_specs=[
            pl.BlockSpec((sent, CB), lambda j: (0, width // CB)),
            whole((pieces, 8, 128)),
        ],
        out_shape=[sds(rows.shape, BF), jax.ShapeDtypeStruct((pieces, 8, 128), F32)],
        input_output_aliases={1: 0},
        compiler_params=params(),
        cost_estimate=cost(sent * CB, sent * CB * 4),
    )(*kept(received), *hbm(rows))


def build_home(pair, slots_ref, homes):
    for half, home in enumerate(homes):
        slot = as_column(slots_ref[2 * half : 2 * half + 1, :])
        home[...] = onehot(iota(home.shape, 1) == slot)


def homecoming(backs, homes):
    total = dot(homes[0][...], backs[0][...])
    for back, home in zip(backs[1:], homes[1:]):
        total = total + dot(home[...], back[...])
    return total


def home_rows_kernel(pair, halves, slots_ref, *refs):
    backs, out_ref, homes = refs[:halves], refs[halves], refs[halves + 1 :]

    @pl.when(pl.program_id(0) == 0)
    def _():
        build_home(pair, slots_ref, homes)

    piece = piece_cols(pair)
    at = pl.ds(pl.multiple_of(pl.program_id(0) * piece, 128), WIDE)
    rows = [ref.at[:, at] for ref in backs]
    out_ref[...] = homecoming(rows, homes).astype(BF)


def home_rows(pair, slots, backs, width):
    sent = SHARDS * pair
    halves = len(backs)
    return pl.pallas_call(
        functools.partial(home_rows_kernel, pair, halves),
        grid=(width // WIDE,),
        in_specs=[RESIDENT] + [RESIDENT] * halves,
        out_specs=cols(SLOTS, WIDE),
        out_shape=sds((SLOTS, width), BF),
        scratch_shapes=[pltpu.VMEM((SLOTS, sent), BF)] * halves,
        compiler_params=params(),
        cost_estimate=cost(
            2 * sent * SLOTS * width * halves, 2 * width * (sent * halves + SLOTS)
        ),
    )(*kept(slots, *backs))


def home_product_kernel(pair, halves, index_ref, slots_ref, k_ref, v_ref, *refs):
    backs, refs = refs[:halves], refs[halves:]
    (dk_ref, dv_ref, filt_ref), homes = refs[:3], refs[3:]
    step = pl.program_id(0)

    @pl.when(step == 0)
    def _():
        build_home(pair, slots_ref, homes)

    grad = homecoming([ref.at[:, block_of(step, WIDE)] for ref in backs], homes)
    dk_ref[...] = (grad * v_ref[...].astype(F32)).astype(BF)
    dv_ref[...] = (grad * k_ref[...].astype(F32)).astype(BF)
    part = part_cols(pair)
    width = backs[0].shape[1] - CB
    taps_refs = [ref.at[:, width:] for ref in backs]
    if pair == PAIR:
        taps = taps_refs[0][:, block_of(step, part)]
    else:
        core = lax.rem(index_ref[0], 2)
        taps = jnp.where(core == step, taps_refs[0][...], taps_refs[1][...])
    shape = (TAPS, SHARDS * pair)
    for block in range(WIDE // part):
        gather = onehot(iota(shape, 1) == tap_rows(pair, shape, 0, block))
        filt_ref[:, part * block : part * (block + 1)] = dot(gather, taps)


def home_product(pair, my_index, slots, backs, k, v):
    width = k.shape[1]
    sent = SHARDS * pair
    halves = len(backs)
    return pl.pallas_call(
        functools.partial(home_product_kernel, pair, halves),
        grid=(width // WIDE,),
        in_specs=[
            pl.BlockSpec(memory_space=pltpu.SMEM),
            RESIDENT,
            cols(SLOTS, WIDE),
            cols(SLOTS, WIDE),
        ]
        + [RESIDENT] * halves,
        out_specs=[cols(SLOTS, WIDE), cols(SLOTS, WIDE), cols(TAPS, WIDE)],
        out_shape=[sds((SLOTS, width), BF), sds((SLOTS, width), BF), sds((TAPS, width), F32)],
        scratch_shapes=[pltpu.VMEM((SLOTS, sent), BF)] * halves,
        compiler_params=params(),
        cost_estimate=cost(2 * sent * SLOTS * width, 2 * width * (sent + 5 * SLOTS)),
    )(my_index.reshape(1), *kept(slots), *hbm(k, v), *kept(*backs))


def exchange(pair, rows):
    shards = rows.reshape(SHARDS, pair, rows.shape[1])
    return lax.all_to_all(shards, "seq", split_axis=0, concat_axis=0, tiled=True).reshape(
        rows.shape
    )


def shift(value, steps):
    pairs = [(i, i + steps) for i in range(SHARDS) if 0 <= i + steps < SHARDS]
    return lax.ppermute(value, "seq", pairs)


def swap(value):
    return lax.ppermute(value, "seq", [(i, i ^ 1) for i in range(SHARDS)])


def slot_positions(pair, dest_pos, my_index):
    holders = SHARDS * pair // PAIR
    table = dest_pos.reshape(holders, -1)
    arriving = (table >= 0) & (table // ROWS == my_index)
    row = jnp.arange(table.shape[1], dtype=I32)
    before = (row[:, None] < row[None, :]).astype(BF)
    rank = jnp.dot(arriving.astype(BF), before, preferred_element_type=F32).astype(I32)
    rank = jnp.where(arriving, rank, -1)
    target = table - my_index * ROWS + 1
    order = jnp.arange(PAIR, dtype=I32)
    if pair != PAIR:
        order = (order % pair) * 2 + order // pair
    hit = rank[:, None, :] == order[None, :, None]
    return (jnp.sum(jnp.where(hit, target[:, None, :], 0), axis=2) - 1).reshape(SHARDS * pair)


def layer(pair, others, q_in, k_in, v_in, dest_pos, doc_ids, mr_filter, norm_gain, residual, cotangent):
    my_index = lax.axis_index("seq")
    width = q_in.shape[1]
    wide = step_width(pair)
    gain = norm_gain[None, :]
    shared = pair != PAIR

    slots = send_plan(pair, my_index, dest_pos)
    if shared:
        product_in, product_other, q_other = others
        early = [*hbm(product_in), *kept(product_other)]
        late = [*hbm(q_in), *kept(q_other)]
    else:
        early, late = hbm(k_in, v_in), hbm(q_in)
    sent_rows = pack_arrivals(pair, slots, early, late)
    sent_rows, dest_later, docs_later, slots = lax.optimization_barrier(
        (sent_rows, dest_pos, doc_ids, slots)
    )
    received = exchange(pair, sent_rows)

    pos = slot_positions(pair, dest_later, my_index)
    pos_row = pos[None, :]
    docs_all = jnp.concatenate(
        [jnp.full((TAPS,), -1, I32), docs_later, jnp.full((TAPS,), -2, I32)]
    )
    docs = lax.dynamic_slice_in_dim(docs_all, my_index * ROWS, WIN + TAPS)
    cc, bb = segment_dft(docs[:WIN])
    onward = crossing_dft(docs[TAPS:WIN], docs[WIN:])
    prepared = prepare(cc, bb, *onward)
    received, pos_row, prepared = lax.optimization_barrier((received, pos_row, prepared))
    cc_own, cc_own_t, cc_halo, cc_head_t, bb, bb_t, *onward = prepared

    halo = shift(place_tail(wide, pos_row, received, width), 1)
    q, mix, x, f, sums = forward(
        wide, pos_row, cc_own, cc_own_t, bb, received, mr_filter, residual, cotangent, gain
    )
    mix_head, summed_head, scaled_head, sums = forward_head(
        wide, cc_halo, cc_head_t, halo, f, q, mix, residual, cotangent, gain, sums
    )
    all_sums = [sums] + [
        lax.ppermute(sums, "mp", [(i, (i + k) % 4) for i in range(4)]) for k in (1, 2, 3)
    ]
    head = head_grad(wide, all_sums, q, summed_head, scaled_head)
    d_mix, sent_dq = backward(
        pair, all_sums, pos_row, cc_own, cc_halo, bb_t, q, mix, mix_head, x, halo,
        residual, cotangent, gain,
    )
    sent_dq, from_next = lax.optimization_barrier((sent_dq, shift(head, -1)))
    back_q = exchange(pair, sent_dq)
    normed, d_residual, own_grad = finish(
        wide, all_sums, cc_own, cc_own_t, q, mix, mix_head, f, residual, cotangent, gain, d_mix
    )
    rows = give_back(pair, pos_row, onward, own_grad, from_next, mr_filter)
    sent_dp, d_gain = reduce_parts(pair, back_q, rows, width)
    back_p = exchange(pair, sent_dp)
    backs_q, backs_p = [back_q], [back_p]
    if shared:
        backs_q.append(swap(back_q))
        backs_p.append(swap(back_p))
    d_q_in = home_rows(pair, slots, backs_q, width)
    d_k_in, d_v_in, d_filter = home_product(pair, my_index, slots, backs_p, k_in, v_in)
    return (normed, d_residual, d_q_in, d_k_in, d_v_in, d_filter, d_gain.reshape(width))


def fits_shared(dest_pos):
    chips = dest_pos.reshape(SHARDS // 2, 2 * SLOTS)
    owner = jnp.where(chips >= 0, chips // ROWS, -1)
    load = jnp.sum(
        (owner[:, None, :] == jnp.arange(SHARDS, dtype=I32)[None, :, None]).astype(I32), axis=2
    )
    return jnp.max(load) <= PAIR


def body(q_in, k_in, v_in, dest_pos, *rest):
    product_in = slot_product(k_in, v_in)
    others = (product_in, swap(product_in), swap(q_in))
    return lax.cond(
        fits_shared(dest_pos),
        functools.partial(layer, PAIR // 2),
        functools.partial(layer, PAIR),
        others, q_in, k_in, v_in, dest_pos, *rest,
    )


def solution(mesh):
    return jax.shard_map(
        body,
        mesh=mesh,
        in_specs=(
            P("seq", "mp"),
            P("seq", "mp"),
            P("seq", "mp"),
            P(),
            P(),
            P(None, "mp"),
            P("mp"),
            P("seq", "mp"),
            P("seq", "mp"),
        ),
        out_specs=(
            P("seq", "mp"),
            P("seq", "mp"),
            P("seq", "mp"),
            P("seq", "mp"),
            P("seq", "mp"),
            P(None, "mp"),
            P("mp"),
        ),
        check_vma=False,
    )
```

```python
import functools
import math

import jax
import jax.numpy as jnp
from jax import lax
from jax.experimental import pallas as pl
from jax.experimental.pallas import tpu as pltpu
from jax.sharding import PartitionSpec as P

D = 8192
NORM_EPS = 1e-06
NDOCS = 64
BF = jnp.bfloat16
F32 = jnp.float32
I32 = jnp.int32

ROWS = 256
SLOTS = 384
TAPS = 128
SHARDS = 32
PAIR = 16
WIN = TAPS + ROWS
FREQ = 320
CB = 512
WIDE, NARROW = 1024, 128


def step_width(pair):
    return NARROW if pair == PAIR else WIDE


def dot(a, b):
    return jnp.dot(a, b, preferred_element_type=F32)


def iota(shape, dim):
    return lax.broadcasted_iota(I32, shape, dim)


def onehot(match):
    return jnp.where(match, 1.0, 0.0).astype(BF)


def params(grid=True):
    return pltpu.CompilerParams(
        dimension_semantics=("arbitrary",) if grid else None, vmem_limit_bytes=36 * 1024 * 1024
    )


def cols(rows, width=CB, last=None):
    if last is None:
        return pl.BlockSpec((rows, width), lambda j: (0, j))
    return pl.BlockSpec((rows, width), lambda j: (0, jnp.minimum(j, last)))


RESIDENT = pl.BlockSpec(memory_space=pltpu.VMEM)


def block_of(step, width=CB):
    return pl.ds(pl.multiple_of(step * width, width), width)


def whole(shape):
    return pl.BlockSpec(shape, lambda j: (0,) * len(shape))


def cost(flops, nbytes):
    return pl.CostEstimate(flops=int(flops), transcendentals=0, bytes_accessed=int(nbytes))


def hbm(*values):
    return [pltpu.with_memory_space_constraint(v, pltpu.HBM) for v in values]


def kept(*values):
    return [pltpu.with_memory_space_constraint(v, pltpu.VMEM) for v in values]


def sds(shape, dtype):
    return pltpu.HBM(shape, dtype)


def owners_of(table_ref, index):
    rows = [table_ref[pl.ds(3 * index + i, 1), :] for i in range(3)]
    plan = jnp.concatenate(rows, axis=1)
    return jnp.where(plan >= 0, plan // ROWS, -1)


def as_column(row):
    return jnp.transpose(jnp.broadcast_to(row, (128, row.shape[1])))[:, 0:1]


def slots_of(pair, core, half, owner, owner_col, sibling_col):
    early = iota((SLOTS, SLOTS), 0) < iota((SLOTS, SLOTS), 1)
    same = jnp.where((owner_col == owner) & early, 1, 0)
    rank = jnp.sum(same, axis=0, keepdims=True)
    if pair == PAIR:
        return jnp.where(owner >= 0, owner * pair + rank, -1)
    before = jnp.sum(jnp.where(sibling_col == owner, 1, 0), axis=0, keepdims=True)
    mine = core if half == 0 else 1 - core
    rank = rank + mine * before
    return jnp.where((owner >= 0) & (rank % 2 == core), owner * pair + rank // 2, -1)


def plan_kernel(pair, index_ref, table_ref, slots_ref):
    index = index_ref[0]
    core = index % 2
    own = owners_of(table_ref, index)
    own_col = as_column(own)
    if pair == PAIR:
        slots_ref[...] = jnp.broadcast_to(
            slots_of(pair, core, 0, own, own_col, None), (8, SLOTS)
        )
        return
    other = owners_of(table_ref, index + 1 - 2 * core)
    other_col = as_column(other)
    first = slots_of(pair, core, 0, own, own_col, other_col)
    second = slots_of(pair, core, 1, other, other_col, own_col)
    theirs = slots_of(pair, 1 - core, 1, own, own_col, other_col)
    slots_ref[...] = jnp.concatenate(
        [first, second, theirs, jnp.full((5, SLOTS), -1, I32)], axis=0
    )


def send_plan(pair, my_index, dest_pos):
    return pl.pallas_call(
        functools.partial(plan_kernel, pair),
        grid_spec=pltpu.PrefetchScalarGridSpec(
            num_scalar_prefetch=1,
            grid=(1,),
            in_specs=[pl.BlockSpec((SHARDS * SLOTS // 128, 128), lambda j, ref: (0, 0))],
            out_specs=pl.BlockSpec((8, SLOTS), lambda j, ref: (0, 0)),
        ),
        out_shape=jax.ShapeDtypeStruct((8, SLOTS), I32),
        compiler_params=params(),
    )(my_index.reshape(1), dest_pos.reshape(SHARDS * SLOTS // 128, 128))


def build_pack(slots_ref, packs):
    for half, pack in enumerate(packs):
        pack[...] = onehot(iota(pack.shape, 0) == slots_ref[half : half + 1, :])


def pack_kernel(halves, blocks, slots_ref, *refs):
    first, second = refs[: 2 * halves : 2], refs[1 : 2 * halves : 2]
    q_refs, out_ref, packs = refs[2:3], refs[3], refs[4:]
    if halves == 2:
        first, second, q_refs, out_ref, packs = None, refs[:2], refs[2:4], refs[4], refs[5:]
    step = pl.program_id(0)
    wide = out_ref.shape[1]

    @pl.when(step == 0)
    def _():
        build_pack(slots_ref, packs)

    def packed(values):
        total = dot(packs[0][...], values[0])
        for value, pack in zip(values[1:], packs[1:]):
            total = total + dot(pack[...], value)
        return total.astype(BF)

    @pl.when(step < blocks)
    def _():
        if first is None:
            out_ref[...] = packed([second[0][...], second[1][:, block_of(step, wide)]])
        else:
            product = first[0][...].astype(F32) * second[0][...].astype(F32)
            out_ref[...] = packed([product.astype(BF)])

    @pl.when(step >= blocks)
    def _():
        rows = [q_refs[0][...]]
        if halves == 2:
            rows.append(q_refs[1][:, block_of(step - blocks, wide)])
        out_ref[...] = packed(rows)


def pack_arrivals(pair, slots, early, late):
    wide = step_width(pair)
    width = early[0].shape[1]
    blocks = width // wide
    halves = len(late)
    sent = SHARDS * pair
    return pl.pallas_call(
        functools.partial(pack_kernel, halves, blocks),
        grid=(2 * blocks,),
        in_specs=[RESIDENT]
        + [cols(SLOTS, wide, last=blocks - 1)]
        + [RESIDENT if halves == 2 else cols(SLOTS, wide, last=blocks - 1)]
        + [pl.BlockSpec((SLOTS, wide), lambda j: (0, jnp.maximum(j - blocks, 0)))]
        + [RESIDENT] * (halves - 1),
        out_specs=cols(sent, wide),
        out_shape=sds((sent, 2 * width), BF),
        scratch_shapes=[pltpu.VMEM((sent, SLOTS), BF)] * halves,
        compiler_params=params(),
        cost_estimate=cost(4 * sent * SLOTS * width * halves, 4 * width * (sent + SLOTS * 2)),
    )(*kept(slots), *early, *late)


def product_kernel(k_ref, v_ref, out_ref):
    out_ref[...] = (k_ref[...].astype(F32) * v_ref[...].astype(F32)).astype(BF)


def slot_product(k, v):
    width = k.shape[1]
    return pl.pallas_call(
        product_kernel,
        grid=(width // WIDE,),
        in_specs=[cols(SLOTS, WIDE)] * 2,
        out_specs=cols(SLOTS, WIDE),
        out_shape=sds((SLOTS, width), BF),
        compiler_params=params(),
        cost_estimate=cost(SLOTS * width, 6 * width * SLOTS),
    )(*hbm(k, v))


def place_tail_kernel(pos_row, recv_ref, tail_ref, place):
    @pl.when(pl.program_id(0) == 0)
    def _():
        place[...] = onehot(iota(place.shape, 0) + (ROWS - TAPS) == pos_row[...])

    tail_ref[...] = dot(place[...], recv_ref[:, block_of(pl.program_id(0), tail_ref.shape[1])]).astype(BF)


def place_tail(wide, pos_row, received, width):
    sent = received.shape[0]
    return pl.pallas_call(
        place_tail_kernel,
        grid=(width // wide,),
        in_specs=[RESIDENT, RESIDENT],
        out_specs=cols(TAPS, wide),
        out_shape=sds((TAPS, width), BF),
        scratch_shapes=[pltpu.VMEM((TAPS, sent), BF)],
        compiler_params=params(),
        cost_estimate=cost(2 * sent * TAPS * width, 2 * width * (sent + TAPS)),
    )(*kept(pos_row, received))


def wave_of(turns):
    square = (turns * turns) * (4.0 * math.pi * math.pi)

    def series(first):
        total = jnp.zeros_like(square)
        for power in range(first + 16, first - 1, -2):
            term = (-1.0) ** ((power - first) // 2) / math.factorial(power)
            total = total * square + term
        return total

    return series(0), series(1) * (turns * (-2.0 * math.pi))


def segment_dft(docs_window):
    place = jnp.arange(WIN, dtype=I32)
    docs = jnp.where(place >= 1, docs_window, -1)
    ids = jnp.arange(NDOCS, dtype=I32)
    inside = docs[None, :] == ids[:, None]
    span = jnp.sum(inside.astype(I32), axis=1)
    own = jnp.sum((inside & (place >= TAPS)[None, :]).astype(I32), axis=1)
    first = jnp.min(jnp.where(inside, place[None, :], 2 * WIN), axis=1)
    taps = jnp.minimum(TAPS, span)
    length = jnp.maximum(span, own + taps - 1)
    length = length + 1 - length % 2
    slots = jnp.where(own > 0, (length + 1) // 2, 0)
    start = jnp.sum(jnp.where(ids[None, :] < ids[:, None], slots[None, :], 0), axis=1)
    slot = jnp.arange(FREQ, dtype=I32)[:, None]
    member = (slot >= start[None, :]) & (slot < (start + slots)[None, :])

    def pick(value):
        return jnp.sum(jnp.where(member, value[None, :], 0), axis=1, keepdims=True)

    live = pick(jnp.ones_like(ids)) > 0
    doc = jnp.where(live, pick(ids), -9)
    wave = slot - pick(start)
    size = jnp.where(live, pick(length), 1)
    size_f = size.astype(F32)
    inverse = 1.0 / size_f

    def waves(steps):
        turns = (wave * steps).astype(F32)
        turns = turns - jnp.round(turns * inverse) * size_f
        return wave_of(turns * inverse)

    real, imag = waves(place[None, :] - pick(first))
    mask = docs[None, :] == doc
    spectrum = jnp.where(
        jnp.concatenate([mask, mask], axis=0), jnp.concatenate([real, imag], axis=0), 0.0
    )
    lag = jnp.arange(TAPS, dtype=I32)[None, :]
    real, imag = waves(lag)
    weight = jnp.where(
        live & (lag < pick(taps)), jnp.where(wave == 0, inverse, 2.0 * inverse), 0.0
    )
    taps_spectrum = jnp.concatenate([weight * real, weight * imag], axis=0)
    return spectrum, taps_spectrum


CROSS = TAPS + ROWS - 1
CROSS_FREQ = (CROSS + 1) // 2


def crossing_dft(own_docs, next_docs):
    wave = jnp.arange(CROSS_FREQ, dtype=I32)[:, None]
    place = jnp.arange(TAPS, dtype=I32)[None, :]

    def waves(steps):
        turns = (wave * steps).astype(F32)
        turns = turns - jnp.round(turns * (1.0 / CROSS)) * CROSS
        return jnp.concatenate(wave_of(turns * (1.0 / CROSS)), axis=0)

    document = own_docs[ROWS - 1]
    head = jnp.where((next_docs == document)[None, :], waves(place + TAPS), 0.0)
    tail = jnp.where((own_docs[ROWS - TAPS :] == document)[None, :], waves(place), 0.0)
    weight = jnp.where(wave == 0, 1.0, 2.0) / CROSS
    taps = jnp.concatenate([weight, weight], axis=0) * waves(place)
    return head, tail, taps


def spectra_product(xr, xi, fr, fi):
    return jnp.concatenate(
        [(xr * fr - xi * fi).astype(BF), (xr * fi + xi * fr).astype(BF)], axis=0
    )


def conj_product(gr, gi, fr, fi):
    return jnp.concatenate(
        [(gr * fr + gi * fi).astype(BF), (gi * fr - gr * fi).astype(BF)], axis=0
    )


def sums_of(summed, scaled):
    squares = jnp.sum(summed * summed, axis=1, keepdims=True)
    dots = jnp.sum(scaled * summed, axis=1, keepdims=True)
    lane = iota((summed.shape[0], 128), 1)
    return jnp.where(lane == 0, squares, jnp.where(lane == 1, dots, 0.0))


def conv_kernel(
    pos_row, cc_own, cc_own_t, bb, recv, filt, residual, cot, gain,
    q_ref, mix_ref, x_ref, f_ref, sums_ref,
    place, acc,
):
    step = pl.program_id(0)

    @pl.when(step == 0)
    def _():
        place[...] = onehot(iota(place.shape, 0) == pos_row[...])
        acc[...] = jnp.zeros_like(acc)

    at = block_of(step, filt.shape[1])
    product = dot(place[...], recv[:, at]).astype(BF)
    q = dot(place[...], recv[:, block_of(step + pl.num_programs(0), filt.shape[1])])
    q_ref[:, at] = q.astype(BF)
    x = dot(cc_own[...], product)
    f = dot(bb[...], filt[...].astype(BF))
    x_ref[:, at] = x.astype(BF)
    f_ref[:, at] = f.astype(BF)
    mix = dot(cc_own_t[...], spectra_product(x[:FREQ], x[FREQ:], f[:FREQ], f[FREQ:]))
    mix_ref[:, at] = mix
    late = slice(TAPS, ROWS)
    summed = residual[late].astype(F32) + q[late] * mix[late]
    acc[...] += sums_of(summed, cot[late].astype(F32) * gain[...])

    @pl.when(step == pl.num_programs(0) - 1)
    def _():
        sums_ref[...] = jnp.transpose(acc[...])[:8]


def forward(wide, pos_row, cc_own, cc_own_t, bb, received, filt, residual, cot, gain):
    sent = received.shape[0]
    width = received.shape[1] // 2
    blocks = width // wide
    return pl.pallas_call(
        conv_kernel,
        grid=(blocks,),
        in_specs=[
            RESIDENT,
            RESIDENT,
            RESIDENT,
            RESIDENT,
            RESIDENT,
            cols(TAPS, wide),
            cols(ROWS, wide),
            cols(ROWS, wide),
            cols(1, wide),
        ],
        out_specs=[RESIDENT] * 4 + [whole((8, TAPS))],
        out_shape=[
            pltpu.VMEM((ROWS, width), BF),
            pltpu.VMEM((ROWS, width), F32),
            pltpu.VMEM((2 * FREQ, width), BF),
            pltpu.VMEM((2 * FREQ, width), BF),
            jax.ShapeDtypeStruct((8, TAPS), F32),
        ],
        scratch_shapes=[pltpu.VMEM((ROWS, sent), BF), pltpu.VMEM((TAPS, 128), F32)],
        compiler_params=params(),
        cost_estimate=cost(4e9, width * 6000),
    )(*kept(pos_row, cc_own, cc_own_t, bb, received), *hbm(filt, residual, cot), gain)


def crossing(value):
    return value[:CROSS_FREQ], value[FREQ : FREQ + CROSS_FREQ]


def head_kernel(
    cc_halo, cc_head_t, halo, f_ref, q_ref, mix_ref, residual, cot, gain, sums_ref,
    mix_head_ref, summed_ref, scaled_ref, out_sums_ref,
    acc,
):
    step = pl.program_id(0)

    @pl.when(step == 0)
    def _():
        acc[...] = jnp.zeros_like(acc)

    at = block_of(step, halo.shape[1])
    x = dot(cc_halo[...], halo[...])
    fr, fi = crossing(f_ref[:, at].astype(F32))
    y = spectra_product(x[:CROSS_FREQ], x[CROSS_FREQ:], fr, fi)
    mix = mix_ref[:TAPS, at] + dot(cc_head_t[...], y)
    mix_head_ref[:, at] = mix
    summed = residual[...].astype(F32) + q_ref[:TAPS, at].astype(F32) * mix
    scaled = cot[...].astype(F32) * gain[...]
    summed_ref[:, at] = summed
    scaled_ref[:, at] = scaled
    acc[...] += sums_of(summed, scaled)

    @pl.when(step == pl.num_programs(0) - 1)
    def _():
        out_sums_ref[:, :TAPS] = jnp.transpose(acc[...])[:8]
        out_sums_ref[:, TAPS:] = sums_ref[...]


def forward_head(wide, cc_halo, cc_head_t, halo, f, q, mix, residual, cot, gain, sums):
    width = q.shape[1]
    return pl.pallas_call(
        head_kernel,
        grid=(width // wide,),
        in_specs=[
            RESIDENT,
            RESIDENT,
            cols(TAPS, wide),
            RESIDENT,
            RESIDENT,
            RESIDENT,
            cols(TAPS, wide),
            cols(TAPS, wide),
            cols(1, wide),
            RESIDENT,
        ],
        out_specs=[RESIDENT] * 3 + [whole((8, ROWS))],
        out_shape=[pltpu.VMEM((TAPS, width), F32)] * 3 + [jax.ShapeDtypeStruct((8, ROWS), F32)],
        scratch_shapes=[pltpu.VMEM((TAPS, 128), F32)],
        compiler_params=params(),
        cost_estimate=cost(6e8, width * 3000),
    )(*kept(cc_halo, cc_head_t), halo, *kept(f, q, mix), *hbm(residual, cot), gain, *kept(sums))


def prepare_kernel(
    cc_ref, bb_ref, head_ref, tail_ref, taps_ref,
    own, own_t, halo, head_t, bb, bb_t, onward_head, onward_tail_t, onward_taps,
):
    own[...] = cc_ref[:, TAPS:].astype(BF)
    own_t[...] = jnp.transpose(cc_ref[:, TAPS:]).astype(BF)
    bb[...] = bb_ref[...].astype(BF)
    bb_t[...] = jnp.transpose(bb_ref[...]).astype(BF)
    real, imag = crossing(cc_ref)
    halo[:CROSS_FREQ] = real[:, :TAPS].astype(BF)
    halo[CROSS_FREQ:] = imag[:, :TAPS].astype(BF)
    head = jnp.concatenate([real[:, TAPS : 2 * TAPS], imag[:, TAPS : 2 * TAPS]], axis=0)
    head_t[...] = jnp.transpose(head).astype(BF)
    onward_head[...] = head_ref[...].astype(BF)
    onward_tail_t[...] = jnp.transpose(tail_ref[...]).astype(BF)
    onward_taps[...] = taps_ref[...].astype(BF)


def prepare(cc, bb, head, tail, taps):
    shapes = [
        (2 * FREQ, ROWS),
        (ROWS, 2 * FREQ),
        (2 * CROSS_FREQ, TAPS),
        (TAPS, 2 * CROSS_FREQ),
        (2 * FREQ, TAPS),
        (TAPS, 2 * FREQ),
        (2 * CROSS_FREQ, TAPS),
        (TAPS, 2 * CROSS_FREQ),
        (2 * CROSS_FREQ, TAPS),
    ]
    return pl.pallas_call(
        prepare_kernel, out_shape=[pltpu.VMEM(shape, BF) for shape in shapes], compiler_params=params(False)
    )(cc, bb, head, tail, taps)


def tap_rows(pair, shape, tap_dim, block):
    tap = iota(shape, tap_dim)
    return (tap // 4) * pair + tap % 4 + 4 * block


def part_cols(pair):
    return 4 * WIDE // pair


def piece_cols(pair):
    return WIDE + part_cols(pair) + 128


def row_stats(s0, s1, s2, s3, stats):
    sums = s0[...] + s1[...] + s2[...] + s3[...]
    sums = jnp.transpose(jnp.concatenate([sums, jnp.zeros((120, ROWS), F32)], axis=0))
    inv = lax.rsqrt(sums[:, 0:1] / D + NORM_EPS)
    stats[...] = jnp.where(iota((ROWS, 128), 1) == 0, inv, sums)


def d_summed_of(stats, summed, scaled):
    inv = stats[:, 0:1]
    return inv * scaled - summed * (inv * inv * inv) * stats[:, 1:2] / D


def head_grad_kernel(s0, s1, s2, s3, q_ref, summed_ref, scaled_ref, head_ref, stats):
    step = pl.program_id(0)

    @pl.when(step == 0)
    def _():
        row_stats(s0, s1, s2, s3, stats)

    at = block_of(step, head_ref.shape[1])
    d_summed = d_summed_of(stats[:TAPS], summed_ref[:, at], scaled_ref[:, at])
    head_ref[...] = (d_summed * q_ref[:TAPS, at].astype(F32)).astype(BF)


def head_grad(wide, sums, q, summed_head, scaled_head):
    width = q.shape[1]
    return pl.pallas_call(
        head_grad_kernel,
        grid=(width // wide,),
        in_specs=[RESIDENT] * 7,
        out_specs=cols(TAPS, wide),
        out_shape=sds((TAPS, width), BF),
        scratch_shapes=[pltpu.VMEM((ROWS, 128), F32)],
        compiler_params=params(),
        cost_estimate=cost(width * TAPS * 10, width * TAPS * 6),
    )(*kept(*sums, q, summed_head, scaled_head))


def mixture_block(mix_ref, mix_head_ref, at):
    return jnp.concatenate([mix_head_ref[:, at], mix_ref[TAPS:, at]], axis=0)


def backward_kernel(
    pair,
    s0, s1, s2, s3, pos_row, cc_own, cc_halo, bb_t, q_ref, mix_ref, mix_head_ref, x_ref,
    halo_ref, res_ref, cot_ref, gain_ref,
    dmix_ref, out_ref,
    give, stats,
):
    step = pl.program_id(0)
    part = part_cols(pair)
    sent = SHARDS * pair

    @pl.when(step == 0)
    def _():
        give[...] = onehot(as_column(pos_row[...]) == iota(give.shape, 1))
        row_stats(s0, s1, s2, s3, stats)

    at = block_of(step, WIDE)
    q = q_ref[:, at].astype(F32)
    mix = mixture_block(mix_ref, mix_head_ref, at)
    summed = res_ref[...].astype(F32) + q * mix
    cot = cot_ref[...].astype(F32)
    gain_part = jnp.sum(cot * summed * stats[:, 0:1], axis=0, keepdims=True)
    d_summed = d_summed_of(stats, summed, cot * gain_ref[...])
    out_ref[:, :WIDE] = dot(give[...], (d_summed * mix).astype(BF)).astype(BF)
    d_mix = (d_summed * q).astype(BF)
    dmix_ref[...] = d_mix
    g = dot(cc_own[...], d_mix)
    x = x_ref[:, at].astype(F32)
    reach = dot(cc_halo[...], halo_ref[...])
    xr = jnp.concatenate([x[:CROSS_FREQ] + reach[:CROSS_FREQ], x[CROSS_FREQ:FREQ]], axis=0)
    xi = jnp.concatenate(
        [x[FREQ : FREQ + CROSS_FREQ] + reach[CROSS_FREQ:], x[FREQ + CROSS_FREQ :]], axis=0
    )
    taps = dot(bb_t[...], conj_product(g[:FREQ], g[FREQ:], xr, xi)).astype(BF)
    total = jnp.zeros((sent, part), F32)
    for block in range(WIDE // part):
        spread = onehot(iota((sent, TAPS), 0) == tap_rows(pair, (sent, TAPS), 1, block))
        total = total + dot(spread, taps[:, part * block : part * (block + 1)])
    out_ref[:, WIDE : WIDE + part] = total.astype(BF)
    rows = [gain_part[:, 128 * r : 128 * (r + 1)] for r in range(WIDE // 128)]
    rows = jnp.concatenate(rows + [jnp.zeros((pair - len(rows), 128), F32)] * (pair > len(rows)), axis=0)
    rows = jnp.broadcast_to(rows[None], (SHARDS, pair, 128)).reshape(sent, 128)
    out_ref[:, WIDE + part :] = rows.astype(BF)


def backward(pair, sums, pos_row, cc_own, cc_halo, bb_t, q, mix, mix_head, x, halo, residual, cot, gain):
    width = q.shape[1]
    steps = width // WIDE
    sent = SHARDS * pair
    return pl.pallas_call(
        functools.partial(backward_kernel, pair),
        grid=(steps,),
        in_specs=[RESIDENT] * 12
        + [cols(TAPS, WIDE), cols(ROWS, WIDE), cols(ROWS, WIDE), cols(1, WIDE)],
        out_specs=[cols(ROWS, WIDE), cols(sent, piece_cols(pair))],
        out_shape=[sds((ROWS, width), BF), sds((sent, steps * piece_cols(pair)), BF)],
        scratch_shapes=[pltpu.VMEM((sent, ROWS), BF), pltpu.VMEM((ROWS, 128), F32)],
        compiler_params=params(),
        cost_estimate=cost(2e9, width * 6000),
    )(
        *kept(*sums, pos_row, cc_own, cc_halo, bb_t, q, mix, mix_head, x), halo,
        *hbm(residual, cot), gain,
    )


def finish_kernel(
    s0, s1, s2, s3, cc_own, cc_own_t, q_ref, mix_ref, mix_head_ref, f_ref, res_ref, cot_ref,
    gain_ref, dmix_ref,
    normed_ref, dres_ref, own_ref,
    stats,
):
    step = pl.program_id(0)

    @pl.when(step == 0)
    def _():
        row_stats(s0, s1, s2, s3, stats)

    at = block_of(step, res_ref.shape[1])
    gain = gain_ref[...]
    mix = mixture_block(mix_ref, mix_head_ref, at)
    summed = res_ref[...].astype(F32) + q_ref[:, at].astype(F32) * mix
    normed_ref[...] = (summed * stats[:, 0:1] * gain).astype(BF)
    dres_ref[...] = d_summed_of(stats, summed, cot_ref[...].astype(F32) * gain).astype(BF)
    g = dot(cc_own[...], dmix_ref[...])
    f = f_ref[:, at].astype(F32)
    own_ref[...] = dot(cc_own_t[...], conj_product(g[:FREQ], g[FREQ:], f[:FREQ], f[FREQ:]))


def finish(wide, sums, cc_own, cc_own_t, q, mix, mix_head, f, residual, cot, gain, d_mix):
    width = q.shape[1]
    return pl.pallas_call(
        finish_kernel,
        grid=(width // wide,),
        in_specs=[RESIDENT] * 4
        + [RESIDENT, RESIDENT]
        + [RESIDENT] * 4
        + [cols(ROWS, wide), cols(ROWS, wide), cols(1, wide), cols(ROWS, wide)],
        out_specs=[cols(ROWS, wide)] * 3,
        out_shape=[sds((ROWS, width), BF), sds((ROWS, width), BF), sds((ROWS, width), F32)],
        scratch_shapes=[pltpu.VMEM((ROWS, 128), F32)],
        compiler_params=params(),
        cost_estimate=cost(2 * 2 * 2 * FREQ * ROWS * width, width * 6000),
    )(
        *kept(*sums, cc_own, cc_own_t, q, mix, mix_head, f), *hbm(residual, cot), gain,
        *hbm(d_mix),
    )


def give_back_kernel(pos_row, head, tail_t, taps, own_ref, next_ref, filt, out_ref, give):
    @pl.when(pl.program_id(0) == 0)
    def _():
        give[...] = onehot(as_column(pos_row[...]) == iota(give.shape, 1))

    g = dot(head[...], next_ref[...])
    f = dot(taps[...], filt[...].astype(BF))
    gr, gi, fr, fi = g[:CROSS_FREQ], g[CROSS_FREQ:], f[:CROSS_FREQ], f[CROSS_FREQ:]
    z = conj_product(gr, gi, fr, fi)
    own = own_ref[...]
    grad = jnp.concatenate(
        [own[: ROWS - TAPS], own[ROWS - TAPS :] + dot(tail_t[...], z)], axis=0
    )
    out_ref[...] = dot(give[...], grad.astype(BF)).astype(BF)


def give_back(pair, pos_row, onward, own, from_next, filt):
    wide = step_width(pair)
    width = own.shape[1]
    sent = SHARDS * pair
    return pl.pallas_call(
        give_back_kernel,
        grid=(width // wide,),
        in_specs=[
            RESIDENT,
            RESIDENT,
            RESIDENT,
            RESIDENT,
            cols(ROWS, wide),
            cols(TAPS, wide),
            cols(TAPS, wide),
        ],
        out_specs=cols(sent, wide),
        out_shape=sds((sent, width + CB), BF),
        scratch_shapes=[pltpu.VMEM((sent, ROWS), BF)],
        compiler_params=params(),
        cost_estimate=cost(2 * sent * ROWS * width, width * 2400),
    )(*kept(pos_row, *onward), *hbm(own), from_next, *hbm(filt))


def reduce_kernel(pair, pieces, received_ref, rows_ref, out_ref, d_gain_ref):
    def over_sources(at, size):
        value = received_ref[:, at : at + size].astype(F32)
        return jnp.sum(value.reshape(SHARDS, pair, size), axis=0)

    part = part_cols(pair)
    starts = [piece_cols(pair) * piece + WIDE for piece in range(pieces)]
    totals = [over_sources(at, part) for at in starts]
    if pair == PAIR:
        both = jnp.broadcast_to(jnp.concatenate(totals, axis=1)[None], (SHARDS, pair, CB))
    else:
        both = jnp.broadcast_to(
            jnp.concatenate(totals, axis=0)[None], (SHARDS // 2, 2 * pair, CB)
        )
    out_ref[...] = both.reshape(SHARDS * pair, CB).astype(BF)
    for piece, at in enumerate(starts):
        d_gain_ref[piece] = over_sources(at + part, 128)[:8]


def reduce_parts(pair, received, rows, width):
    sent = SHARDS * pair
    pieces = width // WIDE
    return pl.pallas_call(
        functools.partial(reduce_kernel, pair, pieces),
        grid=(1,),
        in_specs=[RESIDENT, pl.BlockSpec(memory_space=pl.ANY)],
        out_specs=[
            pl.BlockSpec((sent, CB), lambda j: (0, width // CB)),
            whole((pieces, 8, 128)),
        ],
        out_shape=[sds(rows.shape, BF), jax.ShapeDtypeStruct((pieces, 8, 128), F32)],
        input_output_aliases={1: 0},
        compiler_params=params(),
        cost_estimate=cost(sent * CB, sent * CB * 4),
    )(*kept(received), *hbm(rows))


def build_home(pair, slots_ref, homes):
    for half, home in enumerate(homes):
        slot = as_column(slots_ref[2 * half : 2 * half + 1, :])
        home[...] = onehot(iota(home.shape, 1) == slot)


def homecoming(backs, homes):
    total = dot(homes[0][...], backs[0][...])
    for back, home in zip(backs[1:], homes[1:]):
        total = total + dot(home[...], back[...])
    return total


def home_rows_kernel(pair, halves, slots_ref, *refs):
    backs, out_ref, homes = refs[:halves], refs[halves], refs[halves + 1 :]

    @pl.when(pl.program_id(0) == 0)
    def _():
        build_home(pair, slots_ref, homes)

    step = pl.program_id(0)
    at = pl.ds(pl.multiple_of(step * piece_cols(pair), 128), WIDE)
    rows = [backs[0].at[:, at]] + [ref.at[:, block_of(step, WIDE)] for ref in backs[1:]]
    out_ref[...] = homecoming(rows, homes).astype(BF)


def home_rows(pair, slots, backs, width):
    sent = SHARDS * pair
    halves = len(backs)
    return pl.pallas_call(
        functools.partial(home_rows_kernel, pair, halves),
        grid=(width // WIDE,),
        in_specs=[RESIDENT] + [RESIDENT] * halves,
        out_specs=cols(SLOTS, WIDE),
        out_shape=sds((SLOTS, width), BF),
        scratch_shapes=[pltpu.VMEM((SLOTS, sent), BF)] * halves,
        compiler_params=params(),
        cost_estimate=cost(
            2 * sent * SLOTS * width * halves, 2 * width * (sent * halves + SLOTS)
        ),
    )(*kept(slots, *backs))


def home_product_kernel(pair, halves, index_ref, slots_ref, k_ref, v_ref, *refs):
    backs, refs = refs[:halves], refs[halves:]
    (dk_ref, dv_ref, filt_ref), homes = refs[:3], refs[3:]
    step = pl.program_id(0)

    @pl.when(step == 0)
    def _():
        build_home(pair, slots_ref, homes)

    grad = homecoming([ref.at[:, block_of(step, WIDE)] for ref in backs], homes)
    dk_ref[...] = (grad * v_ref[...].astype(F32)).astype(BF)
    dv_ref[...] = (grad * k_ref[...].astype(F32)).astype(BF)
    part = part_cols(pair)
    width = backs[0].shape[1] - CB
    taps_refs = [ref.at[:, width:] for ref in backs]
    if pair == PAIR:
        taps = taps_refs[0][:, block_of(step, part)]
    else:
        core = lax.rem(index_ref[0], 2)
        taps = jnp.where(core == step, taps_refs[0][...], taps_refs[1][...])
    shape = (TAPS, SHARDS * pair)
    for block in range(WIDE // part):
        gather = onehot(iota(shape, 1) == tap_rows(pair, shape, 0, block))
        filt_ref[:, part * block : part * (block + 1)] = dot(gather, taps)


def home_product(pair, my_index, slots, backs, k, v):
    width = k.shape[1]
    sent = SHARDS * pair
    halves = len(backs)
    return pl.pallas_call(
        functools.partial(home_product_kernel, pair, halves),
        grid=(width // WIDE,),
        in_specs=[
            pl.BlockSpec(memory_space=pltpu.SMEM),
            RESIDENT,
            cols(SLOTS, WIDE),
            cols(SLOTS, WIDE),
        ]
        + [RESIDENT] * halves,
        out_specs=[cols(SLOTS, WIDE), cols(SLOTS, WIDE), cols(TAPS, WIDE)],
        out_shape=[sds((SLOTS, width), BF), sds((SLOTS, width), BF), sds((TAPS, width), F32)],
        scratch_shapes=[pltpu.VMEM((SLOTS, sent), BF)] * halves,
        compiler_params=params(),
        cost_estimate=cost(2 * sent * SLOTS * width, 2 * width * (sent + 5 * SLOTS)),
    )(my_index.reshape(1), *kept(slots), *hbm(k, v), *kept(*backs))


def exchange(pair, rows):
    shards = rows.reshape(SHARDS, pair, rows.shape[1])
    return lax.all_to_all(shards, "seq", split_axis=0, concat_axis=0, tiled=True).reshape(
        rows.shape
    )


def shift(value, steps):
    pairs = [(i, i + steps) for i in range(SHARDS) if 0 <= i + steps < SHARDS]
    return lax.ppermute(value, "seq", pairs)


def swap(value):
    return lax.ppermute(value, "seq", [(i, i ^ 1) for i in range(SHARDS)])


def slot_positions(pair, dest_pos, my_index):
    holders = SHARDS * pair // PAIR
    table = dest_pos.reshape(holders, -1)
    arriving = (table >= 0) & (table // ROWS == my_index)
    row = jnp.arange(table.shape[1], dtype=I32)
    before = (row[:, None] < row[None, :]).astype(BF)
    rank = jnp.dot(arriving.astype(BF), before, preferred_element_type=F32).astype(I32)
    rank = jnp.where(arriving, rank, -1)
    target = table - my_index * ROWS + 1
    order = jnp.arange(PAIR, dtype=I32)
    if pair != PAIR:
        order = (order % pair) * 2 + order // pair
    hit = rank[:, None, :] == order[None, :, None]
    return (jnp.sum(jnp.where(hit, target[:, None, :], 0), axis=2) - 1).reshape(SHARDS * pair)


def layer(pair, others, q_in, k_in, v_in, dest_pos, doc_ids, mr_filter, norm_gain, residual, cotangent):
    my_index = lax.axis_index("seq")
    width = q_in.shape[1]
    wide = step_width(pair)
    gain = norm_gain[None, :]
    shared = pair != PAIR

    slots = send_plan(pair, my_index, dest_pos)
    if shared:
        product_in, product_other, q_other = others
        early = [*hbm(product_in), *kept(product_other)]
        late = [*hbm(q_in), *kept(q_other)]
    else:
        early, late = hbm(k_in, v_in), hbm(q_in)
    sent_rows = pack_arrivals(pair, slots, early, late)
    sent_rows, dest_later, docs_later, slots = lax.optimization_barrier(
        (sent_rows, dest_pos, doc_ids, slots)
    )
    received = exchange(pair, sent_rows)

    pos = slot_positions(pair, dest_later, my_index)
    pos_row = pos[None, :]
    docs_all = jnp.concatenate(
        [jnp.full((TAPS,), -1, I32), docs_later, jnp.full((TAPS,), -2, I32)]
    )
    docs = lax.dynamic_slice_in_dim(docs_all, my_index * ROWS, WIN + TAPS)
    cc, bb = segment_dft(docs[:WIN])
    onward = crossing_dft(docs[TAPS:WIN], docs[WIN:])
    prepared = prepare(cc, bb, *onward)
    received, pos_row, prepared = lax.optimization_barrier((received, pos_row, prepared))
    cc_own, cc_own_t, cc_halo, cc_head_t, bb, bb_t, *onward = prepared

    halo = shift(place_tail(wide, pos_row, received, width), 1)
    q, mix, x, f, sums = forward(
        wide, pos_row, cc_own, cc_own_t, bb, received, mr_filter, residual, cotangent, gain
    )
    mix_head, summed_head, scaled_head, sums = forward_head(
        wide, cc_halo, cc_head_t, halo, f, q, mix, residual, cotangent, gain, sums
    )
    all_sums = [sums] + [
        lax.ppermute(sums, "mp", [(i, (i + k) % 4) for i in range(4)]) for k in (1, 2, 3)
    ]
    head = head_grad(wide, all_sums, q, summed_head, scaled_head)
    d_mix, sent_dq = backward(
        pair, all_sums, pos_row, cc_own, cc_halo, bb_t, q, mix, mix_head, x, halo,
        residual, cotangent, gain,
    )
    sent_dq, from_next = lax.optimization_barrier((sent_dq, shift(head, -1)))
    back_q = exchange(pair, sent_dq)
    normed, d_residual, own_grad = finish(
        wide, all_sums, cc_own, cc_own_t, q, mix, mix_head, f, residual, cotangent, gain, d_mix
    )
    rows = give_back(pair, pos_row, onward, own_grad, from_next, mr_filter)
    sent_dp, d_gain = reduce_parts(pair, back_q, rows, width)
    sent_dp, back_q = lax.optimization_barrier((sent_dp, back_q))
    back_p = exchange(pair, sent_dp)
    backs_q, backs_p = [back_q], [back_p]
    if shared:
        pieces = range(0, back_q.shape[1], piece_cols(pair))
        rows = jnp.concatenate([back_q[:, at : at + WIDE] for at in pieces], axis=1)
        back_p, rows = lax.optimization_barrier((back_p, swap(rows)))
        backs_p = [back_p]
        backs_q.append(rows)
        backs_p.append(swap(back_p))
    d_q_in = home_rows(pair, slots, backs_q, width)
    d_k_in, d_v_in, d_filter = home_product(pair, my_index, slots, backs_p, k_in, v_in)
    return (normed, d_residual, d_q_in, d_k_in, d_v_in, d_filter, d_gain.reshape(width))


def fits_shared(dest_pos):
    chips = dest_pos.reshape(SHARDS // 2, 2 * SLOTS)
    owner = jnp.where(chips >= 0, chips // ROWS, -1)
    load = jnp.sum(
        (owner[:, None, :] == jnp.arange(SHARDS, dtype=I32)[None, :, None]).astype(I32), axis=2
    )
    return jnp.max(load) <= PAIR


def body(q_in, k_in, v_in, dest_pos, *rest):
    product_in = slot_product(k_in, v_in)
    others = (product_in, swap(product_in), swap(q_in))
    return lax.cond(
        fits_shared(dest_pos),
        functools.partial(layer, PAIR // 2),
        functools.partial(layer, PAIR),
        others, q_in, k_in, v_in, dest_pos, *rest,
    )


def solution(mesh):
    return jax.shard_map(
        body,
        mesh=mesh,
        in_specs=(
            P("seq", "mp"),
            P("seq", "mp"),
            P("seq", "mp"),
            P(),
            P(),
            P(None, "mp"),
            P("mp"),
            P("seq", "mp"),
            P("seq", "mp"),
        ),
        out_specs=(
            P("seq", "mp"),
            P("seq", "mp"),
            P("seq", "mp"),
            P("seq", "mp"),
            P("seq", "mp"),
            P(None, "mp"),
            P("mp"),
        ),
        check_vma=False,
    )
```

```python
import functools
import math

import jax
import jax.numpy as jnp
from jax import lax
from jax.experimental import pallas as pl
from jax.experimental.pallas import tpu as pltpu
from jax.sharding import PartitionSpec as P

D = 8192
NORM_EPS = 1e-06
NDOCS = 64
BF = jnp.bfloat16
F32 = jnp.float32
I32 = jnp.int32

ROWS = 256
SLOTS = 384
TAPS = 128
SHARDS = 32
PAIR = 16
WIN = TAPS + ROWS
FREQ = 320
CB = 512
WIDE, NARROW = 1024, 128


def step_width(pair):
    return NARROW if pair == PAIR else WIDE


def dot(a, b):
    return jnp.dot(a, b, preferred_element_type=F32)


def iota(shape, dim):
    return lax.broadcasted_iota(I32, shape, dim)


def onehot(match):
    return jnp.where(match, 1.0, 0.0).astype(BF)


def params(grid=True):
    return pltpu.CompilerParams(
        dimension_semantics=("arbitrary",) if grid else None, vmem_limit_bytes=36 * 1024 * 1024
    )


def cols(rows, width=CB, last=None):
    if last is None:
        return pl.BlockSpec((rows, width), lambda j: (0, j))
    return pl.BlockSpec((rows, width), lambda j: (0, jnp.minimum(j, last)))


RESIDENT = pl.BlockSpec(memory_space=pltpu.VMEM)


def block_of(step, width=CB):
    return pl.ds(pl.multiple_of(step * width, width), width)


def whole(shape):
    return pl.BlockSpec(shape, lambda j: (0,) * len(shape))


def cost(flops, nbytes):
    return pl.CostEstimate(flops=int(flops), transcendentals=0, bytes_accessed=int(nbytes))


def hbm(*values):
    return [pltpu.with_memory_space_constraint(v, pltpu.HBM) for v in values]


def kept(*values):
    return [pltpu.with_memory_space_constraint(v, pltpu.VMEM) for v in values]


def sds(shape, dtype):
    return pltpu.HBM(shape, dtype)


def owners_of(table_ref, index):
    rows = [table_ref[pl.ds(3 * index + i, 1), :] for i in range(3)]
    plan = jnp.concatenate(rows, axis=1)
    return jnp.where(plan >= 0, plan // ROWS, -1)


def as_column(row):
    return jnp.transpose(jnp.broadcast_to(row, (128, row.shape[1])))[:, 0:1]


def slots_of(pair, core, half, owner, owner_col, sibling_col):
    early = iota((SLOTS, SLOTS), 0) < iota((SLOTS, SLOTS), 1)
    same = jnp.where((owner_col == owner) & early, 1, 0)
    rank = jnp.sum(same, axis=0, keepdims=True)
    if pair == PAIR:
        return jnp.where(owner >= 0, owner * pair + rank, -1)
    before = jnp.sum(jnp.where(sibling_col == owner, 1, 0), axis=0, keepdims=True)
    mine = core if half == 0 else 1 - core
    rank = rank + mine * before
    return jnp.where((owner >= 0) & (rank % 2 == core), owner * pair + rank // 2, -1)


def plan_kernel(pair, index_ref, table_ref, slots_ref):
    index = index_ref[0]
    core = index % 2
    own = owners_of(table_ref, index)
    own_col = as_column(own)
    if pair == PAIR:
        slots_ref[...] = jnp.broadcast_to(
            slots_of(pair, core, 0, own, own_col, None), (8, SLOTS)
        )
        return
    other = owners_of(table_ref, index + 1 - 2 * core)
    other_col = as_column(other)
    first = slots_of(pair, core, 0, own, own_col, other_col)
    second = slots_of(pair, core, 1, other, other_col, own_col)
    theirs = slots_of(pair, 1 - core, 1, own, own_col, other_col)
    slots_ref[...] = jnp.concatenate(
        [first, second, theirs, jnp.full((5, SLOTS), -1, I32)], axis=0
    )


def send_plan(pair, my_index, dest_pos):
    return pl.pallas_call(
        functools.partial(plan_kernel, pair),
        grid_spec=pltpu.PrefetchScalarGridSpec(
            num_scalar_prefetch=1,
            grid=(1,),
            in_specs=[pl.BlockSpec((SHARDS * SLOTS // 128, 128), lambda j, ref: (0, 0))],
            out_specs=pl.BlockSpec((8, SLOTS), lambda j, ref: (0, 0)),
        ),
        out_shape=jax.ShapeDtypeStruct((8, SLOTS), I32),
        compiler_params=params(),
    )(my_index.reshape(1), dest_pos.reshape(SHARDS * SLOTS // 128, 128))


def build_pack(slots_ref, packs):
    for half, pack in enumerate(packs):
        pack[...] = onehot(iota(pack.shape, 0) == slots_ref[half : half + 1, :])


def pack_kernel(halves, blocks, slots_ref, *refs):
    first, second = refs[: 2 * halves : 2], refs[1 : 2 * halves : 2]
    q_refs, out_ref, packs = refs[2:3], refs[3], refs[4:]
    if halves == 2:
        first, second, q_refs, out_ref, packs = None, refs[:2], refs[2:4], refs[4], refs[5:]
    step = pl.program_id(0)
    wide = out_ref.shape[1]

    @pl.when(step == 0)
    def _():
        build_pack(slots_ref, packs)

    def packed(values):
        total = dot(packs[0][...], values[0])
        for value, pack in zip(values[1:], packs[1:]):
            total = total + dot(pack[...], value)
        return total.astype(BF)

    @pl.when(step < blocks)
    def _():
        if first is None:
            out_ref[...] = packed([second[0][...], second[1][:, block_of(step, wide)]])
        else:
            product = first[0][...].astype(F32) * second[0][...].astype(F32)
            out_ref[...] = packed([product.astype(BF)])

    @pl.when(step >= blocks)
    def _():
        rows = [q_refs[0][...]]
        if halves == 2:
            rows.append(q_refs[1][:, block_of(step - blocks, wide)])
        out_ref[...] = packed(rows)


def pack_arrivals(pair, slots, early, late):
    wide = step_width(pair)
    width = early[0].shape[1]
    blocks = width // wide
    halves = len(late)
    sent = SHARDS * pair
    return pl.pallas_call(
        functools.partial(pack_kernel, halves, blocks),
        grid=(2 * blocks,),
        in_specs=[RESIDENT]
        + [cols(SLOTS, wide, last=blocks - 1)]
        + [RESIDENT if halves == 2 else cols(SLOTS, wide, last=blocks - 1)]
        + [pl.BlockSpec((SLOTS, wide), lambda j: (0, jnp.maximum(j - blocks, 0)))]
        + [RESIDENT] * (halves - 1),
        out_specs=cols(sent, wide),
        out_shape=sds((sent, 2 * width), BF),
        scratch_shapes=[pltpu.VMEM((sent, SLOTS), BF)] * halves,
        compiler_params=params(),
        cost_estimate=cost(4 * sent * SLOTS * width * halves, 4 * width * (sent + SLOTS * 2)),
    )(*kept(slots), *early, *late)


def product_kernel(k_ref, v_ref, out_ref):
    out_ref[...] = (k_ref[...].astype(F32) * v_ref[...].astype(F32)).astype(BF)


def slot_product(k, v):
    width = k.shape[1]
    return pl.pallas_call(
        product_kernel,
        grid=(width // WIDE,),
        in_specs=[cols(SLOTS, WIDE)] * 2,
        out_specs=cols(SLOTS, WIDE),
        out_shape=sds((SLOTS, width), BF),
        compiler_params=params(),
        cost_estimate=cost(SLOTS * width, 6 * width * SLOTS),
    )(*hbm(k, v))


def place_tail_kernel(pos_row, recv_ref, tail_ref, place):
    @pl.when(pl.program_id(0) == 0)
    def _():
        place[...] = onehot(iota(place.shape, 0) + (ROWS - TAPS) == pos_row[...])

    tail_ref[...] = dot(place[...], recv_ref[:, block_of(pl.program_id(0), tail_ref.shape[1])]).astype(BF)


def place_tail(wide, pos_row, received, width):
    sent = received.shape[0]
    return pl.pallas_call(
        place_tail_kernel,
        grid=(width // wide,),
        in_specs=[RESIDENT, RESIDENT],
        out_specs=cols(TAPS, wide),
        out_shape=sds((TAPS, width), BF),
        scratch_shapes=[pltpu.VMEM((TAPS, sent), BF)],
        compiler_params=params(),
        cost_estimate=cost(2 * sent * TAPS * width, 2 * width * (sent + TAPS)),
    )(*kept(pos_row, received))


def wave_of(turns):
    square = (turns * turns) * (4.0 * math.pi * math.pi)

    def series(first):
        total = jnp.zeros_like(square)
        for power in range(first + 16, first - 1, -2):
            term = (-1.0) ** ((power - first) // 2) / math.factorial(power)
            total = total * square + term
        return total

    return series(0), series(1) * (turns * (-2.0 * math.pi))


def segment_dft(docs_window):
    place = jnp.arange(WIN, dtype=I32)
    docs = jnp.where(place >= 1, docs_window, -1)
    ids = jnp.arange(NDOCS, dtype=I32)
    inside = docs[None, :] == ids[:, None]
    span = jnp.sum(inside.astype(I32), axis=1)
    own = jnp.sum((inside & (place >= TAPS)[None, :]).astype(I32), axis=1)
    first = jnp.min(jnp.where(inside, place[None, :], 2 * WIN), axis=1)
    taps = jnp.minimum(TAPS, span)
    length = jnp.maximum(span, own + taps - 1)
    length = length + 1 - length % 2
    slots = jnp.where(own > 0, (length + 1) // 2, 0)
    start = jnp.sum(jnp.where(ids[None, :] < ids[:, None], slots[None, :], 0), axis=1)
    slot = jnp.arange(FREQ, dtype=I32)[:, None]
    member = (slot >= start[None, :]) & (slot < (start + slots)[None, :])

    def pick(value):
        return jnp.sum(jnp.where(member, value[None, :], 0), axis=1, keepdims=True)

    live = pick(jnp.ones_like(ids)) > 0
    doc = jnp.where(live, pick(ids), -9)
    wave = slot - pick(start)
    size = jnp.where(live, pick(length), 1)
    size_f = size.astype(F32)
    inverse = 1.0 / size_f

    def waves(steps):
        turns = (wave * steps).astype(F32)
        turns = turns - jnp.round(turns * inverse) * size_f
        return wave_of(turns * inverse)

    real, imag = waves(place[None, :] - pick(first))
    mask = docs[None, :] == doc
    spectrum = jnp.where(
        jnp.concatenate([mask, mask], axis=0), jnp.concatenate([real, imag], axis=0), 0.0
    )
    lag = jnp.arange(TAPS, dtype=I32)[None, :]
    real, imag = waves(lag)
    weight = jnp.where(
        live & (lag < pick(taps)), jnp.where(wave == 0, inverse, 2.0 * inverse), 0.0
    )
    taps_spectrum = jnp.concatenate([weight * real, weight * imag], axis=0)
    return spectrum, taps_spectrum


CROSS = TAPS + ROWS - 1
CROSS_FREQ = (CROSS + 1) // 2


def crossing_dft(own_docs, next_docs):
    wave = jnp.arange(CROSS_FREQ, dtype=I32)[:, None]
    place = jnp.arange(TAPS, dtype=I32)[None, :]

    def waves(steps):
        turns = (wave * steps).astype(F32)
        turns = turns - jnp.round(turns * (1.0 / CROSS)) * CROSS
        return jnp.concatenate(wave_of(turns * (1.0 / CROSS)), axis=0)

    document = own_docs[ROWS - 1]
    head = jnp.where((next_docs == document)[None, :], waves(place + TAPS), 0.0)
    tail = jnp.where((own_docs[ROWS - TAPS :] == document)[None, :], waves(place), 0.0)
    weight = jnp.where(wave == 0, 1.0, 2.0) / CROSS
    taps = jnp.concatenate([weight, weight], axis=0) * waves(place)
    return head, tail, taps


def spectra_product(xr, xi, fr, fi):
    return jnp.concatenate(
        [(xr * fr - xi * fi).astype(BF), (xr * fi + xi * fr).astype(BF)], axis=0
    )


def conj_product(gr, gi, fr, fi):
    return jnp.concatenate(
        [(gr * fr + gi * fi).astype(BF), (gi * fr - gr * fi).astype(BF)], axis=0
    )


def sums_of(summed, scaled):
    squares = jnp.sum(summed * summed, axis=1, keepdims=True)
    dots = jnp.sum(scaled * summed, axis=1, keepdims=True)
    lane = iota((summed.shape[0], 128), 1)
    return jnp.where(lane == 0, squares, jnp.where(lane == 1, dots, 0.0))


def conv_kernel(
    pos_row, cc_own, cc_own_t, bb, recv, filt, residual, cot, gain,
    q_ref, mix_ref, x_ref, f_ref, sums_ref,
    place, acc,
):
    step = pl.program_id(0)

    @pl.when(step == 0)
    def _():
        place[...] = onehot(iota(place.shape, 0) == pos_row[...])
        acc[...] = jnp.zeros_like(acc)

    at = block_of(step, filt.shape[1])
    product = dot(place[...], recv[:, at]).astype(BF)
    q = dot(place[...], recv[:, block_of(step + pl.num_programs(0), filt.shape[1])])
    q_ref[:, at] = q.astype(BF)
    x = dot(cc_own[...], product)
    f = dot(bb[...], filt[...].astype(BF))
    x_ref[:, at] = x.astype(BF)
    f_ref[:, at] = f.astype(BF)
    mix = dot(cc_own_t[...], spectra_product(x[:FREQ], x[FREQ:], f[:FREQ], f[FREQ:]))
    mix_ref[:, at] = mix
    late = slice(TAPS, ROWS)
    summed = residual[late].astype(F32) + q[late] * mix[late]
    acc[...] += sums_of(summed, cot[late].astype(F32) * gain[...])

    @pl.when(step == pl.num_programs(0) - 1)
    def _():
        sums_ref[...] = jnp.transpose(acc[...])[:8]


def forward(wide, pos_row, cc_own, cc_own_t, bb, received, filt, residual, cot, gain):
    sent = received.shape[0]
    width = received.shape[1] // 2
    blocks = width // wide
    return pl.pallas_call(
        conv_kernel,
        grid=(blocks,),
        in_specs=[
            RESIDENT,
            RESIDENT,
            RESIDENT,
            RESIDENT,
            RESIDENT,
            cols(TAPS, wide),
            cols(ROWS, wide),
            cols(ROWS, wide),
            cols(1, wide),
        ],
        out_specs=[RESIDENT] * 4 + [whole((8, TAPS))],
        out_shape=[
            pltpu.VMEM((ROWS, width), BF),
            pltpu.VMEM((ROWS, width), F32),
            pltpu.VMEM((2 * FREQ, width), BF),
            pltpu.VMEM((2 * FREQ, width), BF),
            jax.ShapeDtypeStruct((8, TAPS), F32),
        ],
        scratch_shapes=[pltpu.VMEM((ROWS, sent), BF), pltpu.VMEM((TAPS, 128), F32)],
        compiler_params=params(),
        cost_estimate=cost(4e9, width * 6000),
    )(*kept(pos_row, cc_own, cc_own_t, bb, received), *hbm(filt, residual, cot), gain)


def crossing(value):
    return value[:CROSS_FREQ], value[FREQ : FREQ + CROSS_FREQ]


def head_kernel(
    cc_halo, cc_head_t, halo, f_ref, q_ref, mix_ref, residual, cot, gain, sums_ref,
    mix_head_ref, summed_ref, scaled_ref, out_sums_ref,
    acc,
):
    step = pl.program_id(0)

    @pl.when(step == 0)
    def _():
        acc[...] = jnp.zeros_like(acc)

    at = block_of(step, halo.shape[1])
    x = dot(cc_halo[...], halo[...])
    fr, fi = crossing(f_ref[:, at].astype(F32))
    y = spectra_product(x[:CROSS_FREQ], x[CROSS_FREQ:], fr, fi)
    mix = mix_ref[:TAPS, at] + dot(cc_head_t[...], y)
    mix_head_ref[:, at] = mix
    summed = residual[...].astype(F32) + q_ref[:TAPS, at].astype(F32) * mix
    scaled = cot[...].astype(F32) * gain[...]
    summed_ref[:, at] = summed
    scaled_ref[:, at] = scaled
    acc[...] += sums_of(summed, scaled)

    @pl.when(step == pl.num_programs(0) - 1)
    def _():
        out_sums_ref[:, :TAPS] = jnp.transpose(acc[...])[:8]
        out_sums_ref[:, TAPS:] = sums_ref[...]


def forward_head(wide, cc_halo, cc_head_t, halo, f, q, mix, residual, cot, gain, sums):
    width = q.shape[1]
    return pl.pallas_call(
        head_kernel,
        grid=(width // wide,),
        in_specs=[
            RESIDENT,
            RESIDENT,
            cols(TAPS, wide),
            RESIDENT,
            RESIDENT,
            RESIDENT,
            cols(TAPS, wide),
            cols(TAPS, wide),
            cols(1, wide),
            RESIDENT,
        ],
        out_specs=[RESIDENT] * 3 + [whole((8, ROWS))],
        out_shape=[pltpu.VMEM((TAPS, width), F32)] * 3 + [jax.ShapeDtypeStruct((8, ROWS), F32)],
        scratch_shapes=[pltpu.VMEM((TAPS, 128), F32)],
        compiler_params=params(),
        cost_estimate=cost(6e8, width * 3000),
    )(*kept(cc_halo, cc_head_t), halo, *kept(f, q, mix), *hbm(residual, cot), gain, *kept(sums))


def prepare_kernel(
    cc_ref, bb_ref, head_ref, tail_ref, taps_ref,
    own, own_t, halo, head_t, bb, bb_t, onward_head, onward_tail_t, onward_taps,
):
    own[...] = cc_ref[:, TAPS:].astype(BF)
    own_t[...] = jnp.transpose(cc_ref[:, TAPS:]).astype(BF)
    bb[...] = bb_ref[...].astype(BF)
    bb_t[...] = jnp.transpose(bb_ref[...]).astype(BF)
    real, imag = crossing(cc_ref)
    halo[:CROSS_FREQ] = real[:, :TAPS].astype(BF)
    halo[CROSS_FREQ:] = imag[:, :TAPS].astype(BF)
    head = jnp.concatenate([real[:, TAPS : 2 * TAPS], imag[:, TAPS : 2 * TAPS]], axis=0)
    head_t[...] = jnp.transpose(head).astype(BF)
    onward_head[...] = head_ref[...].astype(BF)
    onward_tail_t[...] = jnp.transpose(tail_ref[...]).astype(BF)
    onward_taps[...] = taps_ref[...].astype(BF)


def prepare(cc, bb, head, tail, taps):
    shapes = [
        (2 * FREQ, ROWS),
        (ROWS, 2 * FREQ),
        (2 * CROSS_FREQ, TAPS),
        (TAPS, 2 * CROSS_FREQ),
        (2 * FREQ, TAPS),
        (TAPS, 2 * FREQ),
        (2 * CROSS_FREQ, TAPS),
        (TAPS, 2 * CROSS_FREQ),
        (2 * CROSS_FREQ, TAPS),
    ]
    return pl.pallas_call(
        prepare_kernel, out_shape=[pltpu.VMEM(shape, BF) for shape in shapes], compiler_params=params(False)
    )(cc, bb, head, tail, taps)


def tap_rows(pair, shape, tap_dim, block):
    tap = iota(shape, tap_dim)
    return (tap // 4) * pair + tap % 4 + 4 * block


def part_cols(pair):
    return 4 * WIDE // pair


def piece_cols(pair):
    return WIDE + part_cols(pair) + 128


def row_stats(s0, s1, s2, s3, stats):
    sums = s0[...] + s1[...] + s2[...] + s3[...]
    sums = jnp.transpose(jnp.concatenate([sums, jnp.zeros((120, ROWS), F32)], axis=0))
    inv = lax.rsqrt(sums[:, 0:1] / D + NORM_EPS)
    stats[...] = jnp.where(iota((ROWS, 128), 1) == 0, inv, sums)


def d_summed_of(stats, summed, scaled):
    inv = stats[:, 0:1]
    return inv * scaled - summed * (inv * inv * inv) * stats[:, 1:2] / D


def head_grad_kernel(s0, s1, s2, s3, q_ref, summed_ref, scaled_ref, head_ref, stats):
    step = pl.program_id(0)

    @pl.when(step == 0)
    def _():
        row_stats(s0, s1, s2, s3, stats)

    at = block_of(step, head_ref.shape[1])
    d_summed = d_summed_of(stats[:TAPS], summed_ref[:, at], scaled_ref[:, at])
    head_ref[...] = (d_summed * q_ref[:TAPS, at].astype(F32)).astype(BF)


def head_grad(wide, sums, q, summed_head, scaled_head):
    width = q.shape[1]
    return pl.pallas_call(
        head_grad_kernel,
        grid=(width // wide,),
        in_specs=[RESIDENT] * 7,
        out_specs=cols(TAPS, wide),
        out_shape=sds((TAPS, width), BF),
        scratch_shapes=[pltpu.VMEM((ROWS, 128), F32)],
        compiler_params=params(),
        cost_estimate=cost(width * TAPS * 10, width * TAPS * 6),
    )(*kept(*sums, q, summed_head, scaled_head))


def mixture_block(mix_ref, mix_head_ref, at):
    return jnp.concatenate([mix_head_ref[:, at], mix_ref[TAPS:, at]], axis=0)


def backward_kernel(
    pair,
    s0, s1, s2, s3, pos_row, cc_own, cc_halo, bb_t, q_ref, mix_ref, mix_head_ref, x_ref,
    halo_ref, res_ref, cot_ref, gain_ref,
    dmix_ref, out_ref,
    give, stats,
):
    step = pl.program_id(0)
    part = part_cols(pair)
    sent = SHARDS * pair

    @pl.when(step == 0)
    def _():
        give[...] = onehot(as_column(pos_row[...]) == iota(give.shape, 1))
        row_stats(s0, s1, s2, s3, stats)

    at = block_of(step, WIDE)
    q = q_ref[:, at].astype(F32)
    mix = mixture_block(mix_ref, mix_head_ref, at)
    summed = res_ref[...].astype(F32) + q * mix
    cot = cot_ref[...].astype(F32)
    gain_part = jnp.sum(cot * summed * stats[:, 0:1], axis=0, keepdims=True)
    d_summed = d_summed_of(stats, summed, cot * gain_ref[...])
    out_ref[:, :WIDE] = dot(give[...], (d_summed * mix).astype(BF)).astype(BF)
    d_mix = (d_summed * q).astype(BF)
    dmix_ref[...] = d_mix
    g = dot(cc_own[...], d_mix)
    x = x_ref[:, at].astype(F32)
    reach = dot(cc_halo[...], halo_ref[...])
    xr = jnp.concatenate([x[:CROSS_FREQ] + reach[:CROSS_FREQ], x[CROSS_FREQ:FREQ]], axis=0)
    xi = jnp.concatenate(
        [x[FREQ : FREQ + CROSS_FREQ] + reach[CROSS_FREQ:], x[FREQ + CROSS_FREQ :]], axis=0
    )
    taps = dot(bb_t[...], conj_product(g[:FREQ], g[FREQ:], xr, xi)).astype(BF)
    total = jnp.zeros((sent, part), F32)
    for block in range(WIDE // part):
        spread = onehot(iota((sent, TAPS), 0) == tap_rows(pair, (sent, TAPS), 1, block))
        total = total + dot(spread, taps[:, part * block : part * (block + 1)])
    out_ref[:, WIDE : WIDE + part] = total.astype(BF)
    rows = [gain_part[:, 128 * r : 128 * (r + 1)] for r in range(WIDE // 128)]
    rows = jnp.concatenate(rows + [jnp.zeros((pair - len(rows), 128), F32)] * (pair > len(rows)), axis=0)
    rows = jnp.broadcast_to(rows[None], (SHARDS, pair, 128)).reshape(sent, 128)
    out_ref[:, WIDE + part :] = rows.astype(BF)


def backward(pair, sums, pos_row, cc_own, cc_halo, bb_t, q, mix, mix_head, x, halo, residual, cot, gain):
    width = q.shape[1]
    steps = width // WIDE
    sent = SHARDS * pair
    return pl.pallas_call(
        functools.partial(backward_kernel, pair),
        grid=(steps,),
        in_specs=[RESIDENT] * 12
        + [cols(TAPS, WIDE), cols(ROWS, WIDE), cols(ROWS, WIDE), cols(1, WIDE)],
        out_specs=[cols(ROWS, WIDE), cols(sent, piece_cols(pair))],
        out_shape=[sds((ROWS, width), BF), sds((sent, steps * piece_cols(pair)), BF)],
        scratch_shapes=[pltpu.VMEM((sent, ROWS), BF), pltpu.VMEM((ROWS, 128), F32)],
        compiler_params=params(),
        cost_estimate=cost(2e9, width * 6000),
    )(
        *kept(*sums, pos_row, cc_own, cc_halo, bb_t, q, mix, mix_head, x), halo,
        *hbm(residual, cot), gain,
    )


def finish_kernel(
    s0, s1, s2, s3, cc_own, cc_own_t, q_ref, mix_ref, mix_head_ref, f_ref, res_ref, cot_ref,
    gain_ref, dmix_ref,
    normed_ref, dres_ref, own_ref,
    stats,
):
    step = pl.program_id(0)

    @pl.when(step == 0)
    def _():
        row_stats(s0, s1, s2, s3, stats)

    at = block_of(step, res_ref.shape[1])
    gain = gain_ref[...]
    mix = mixture_block(mix_ref, mix_head_ref, at)
    summed = res_ref[...].astype(F32) + q_ref[:, at].astype(F32) * mix
    normed_ref[...] = (summed * stats[:, 0:1] * gain).astype(BF)
    dres_ref[...] = d_summed_of(stats, summed, cot_ref[...].astype(F32) * gain).astype(BF)
    g = dot(cc_own[...], dmix_ref[...])
    f = f_ref[:, at].astype(F32)
    own_ref[...] = dot(cc_own_t[...], conj_product(g[:FREQ], g[FREQ:], f[:FREQ], f[FREQ:]))


def finish(wide, sums, cc_own, cc_own_t, q, mix, mix_head, f, residual, cot, gain, d_mix):
    width = q.shape[1]
    return pl.pallas_call(
        finish_kernel,
        grid=(width // wide,),
        in_specs=[RESIDENT] * 4
        + [RESIDENT, RESIDENT]
        + [RESIDENT] * 4
        + [cols(ROWS, wide), cols(ROWS, wide), cols(1, wide), cols(ROWS, wide)],
        out_specs=[cols(ROWS, wide)] * 3,
        out_shape=[sds((ROWS, width), BF), sds((ROWS, width), BF), sds((ROWS, width), F32)],
        scratch_shapes=[pltpu.VMEM((ROWS, 128), F32)],
        compiler_params=params(),
        cost_estimate=cost(2 * 2 * 2 * FREQ * ROWS * width, width * 6000),
    )(
        *kept(*sums, cc_own, cc_own_t, q, mix, mix_head, f), *hbm(residual, cot), gain,
        *hbm(d_mix),
    )


def give_back_kernel(pos_row, head, tail_t, taps, own_ref, next_ref, filt, out_ref, give):
    @pl.when(pl.program_id(0) == 0)
    def _():
        give[...] = onehot(as_column(pos_row[...]) == iota(give.shape, 1))

    g = dot(head[...], next_ref[...])
    f = dot(taps[...], filt[...].astype(BF))
    gr, gi, fr, fi = g[:CROSS_FREQ], g[CROSS_FREQ:], f[:CROSS_FREQ], f[CROSS_FREQ:]
    z = conj_product(gr, gi, fr, fi)
    own = own_ref[...]
    grad = jnp.concatenate(
        [own[: ROWS - TAPS], own[ROWS - TAPS :] + dot(tail_t[...], z)], axis=0
    )
    out_ref[...] = dot(give[...], grad.astype(BF)).astype(BF)


def give_back(pair, pos_row, onward, own, from_next, filt):
    wide = step_width(pair)
    width = own.shape[1]
    sent = SHARDS * pair
    return pl.pallas_call(
        give_back_kernel,
        grid=(width // wide,),
        in_specs=[
            RESIDENT,
            RESIDENT,
            RESIDENT,
            RESIDENT,
            cols(ROWS, wide),
            cols(TAPS, wide),
            cols(TAPS, wide),
        ],
        out_specs=cols(sent, wide),
        out_shape=sds((sent, width + CB), BF),
        scratch_shapes=[pltpu.VMEM((sent, ROWS), BF)],
        compiler_params=params(),
        cost_estimate=cost(2 * sent * ROWS * width, width * 2400),
    )(*kept(pos_row, *onward), *hbm(own), from_next, *hbm(filt))


def reduce_kernel(pair, pieces, received_ref, rows_ref, out_ref, d_gain_ref):
    def over_sources(at, size):
        value = received_ref[:, at : at + size].astype(F32)
        return jnp.sum(value.reshape(SHARDS, pair, size), axis=0)

    part = part_cols(pair)
    starts = [piece_cols(pair) * piece + WIDE for piece in range(pieces)]
    totals = [over_sources(at, part) for at in starts]
    if pair == PAIR:
        both = jnp.broadcast_to(jnp.concatenate(totals, axis=1)[None], (SHARDS, pair, CB))
    else:
        both = jnp.broadcast_to(
            jnp.concatenate(totals, axis=0)[None], (SHARDS // 2, 2 * pair, CB)
        )
    out_ref[...] = both.reshape(SHARDS * pair, CB).astype(BF)
    for piece, at in enumerate(starts):
        d_gain_ref[piece] = over_sources(at + part, 128)[:8]


def reduce_parts(pair, received, rows, width):
    sent = SHARDS * pair
    pieces = width // WIDE
    return pl.pallas_call(
        functools.partial(reduce_kernel, pair, pieces),
        grid=(1,),
        in_specs=[RESIDENT, pl.BlockSpec(memory_space=pl.ANY)],
        out_specs=[
            pl.BlockSpec((sent, CB), lambda j: (0, width // CB)),
            whole((pieces, 8, 128)),
        ],
        out_shape=[sds(rows.shape, BF), jax.ShapeDtypeStruct((pieces, 8, 128), F32)],
        input_output_aliases={1: 0},
        compiler_params=params(),
        cost_estimate=cost(sent * CB, sent * CB * 4),
    )(*kept(received), *hbm(rows))


def build_home(pair, slots_ref, homes):
    for half, home in enumerate(homes):
        slot = as_column(slots_ref[2 * half : 2 * half + 1, :])
        home[...] = onehot(iota(home.shape, 1) == slot)


def homecoming(backs, homes):
    total = dot(homes[0][...], backs[0][...])
    for back, home in zip(backs[1:], homes[1:]):
        total = total + dot(home[...], back[...])
    return total


def home_rows_kernel(pair, halves, slots_ref, *refs):
    backs, out_ref, homes = refs[:halves], refs[halves], refs[halves + 1 :]

    @pl.when(pl.program_id(0) == 0)
    def _():
        build_home(pair, slots_ref, homes)

    step = pl.program_id(0)
    at = pl.ds(pl.multiple_of(step * piece_cols(pair), 128), WIDE)
    rows = [backs[0].at[:, at]] + [ref.at[:, block_of(step, WIDE)] for ref in backs[1:]]
    out_ref[...] = homecoming(rows, homes).astype(BF)


def home_rows(pair, slots, backs, width):
    sent = SHARDS * pair
    halves = len(backs)
    return pl.pallas_call(
        functools.partial(home_rows_kernel, pair, halves),
        grid=(width // WIDE,),
        in_specs=[RESIDENT] + [RESIDENT] * halves,
        out_specs=cols(SLOTS, WIDE),
        out_shape=sds((SLOTS, width), BF),
        scratch_shapes=[pltpu.VMEM((SLOTS, sent), BF)] * halves,
        compiler_params=params(),
        cost_estimate=cost(
            2 * sent * SLOTS * width * halves, 2 * width * (sent * halves + SLOTS)
        ),
    )(*kept(slots, *backs))


def home_product_kernel(pair, halves, index_ref, slots_ref, k_ref, v_ref, *refs):
    backs, refs = refs[:halves], refs[halves:]
    (dk_ref, dv_ref, filt_ref), homes = refs[:3], refs[3:]
    step = pl.program_id(0)

    @pl.when(step == 0)
    def _():
        build_home(pair, slots_ref, homes)

    grad = homecoming([ref.at[:, block_of(step, WIDE)] for ref in backs], homes)
    dk_ref[...] = (grad * v_ref[...].astype(F32)).astype(BF)
    dv_ref[...] = (grad * k_ref[...].astype(F32)).astype(BF)
    part = part_cols(pair)
    width = backs[0].shape[1] - CB
    taps_refs = [ref.at[:, width:] for ref in backs]
    if pair == PAIR:
        taps = taps_refs[0][:, block_of(step, part)]
    else:
        core = lax.rem(index_ref[0], 2)
        taps = jnp.where(core == step, taps_refs[0][...], taps_refs[1][...])
    shape = (TAPS, SHARDS * pair)
    for block in range(WIDE // part):
        gather = onehot(iota(shape, 1) == tap_rows(pair, shape, 0, block))
        filt_ref[:, part * block : part * (block + 1)] = dot(gather, taps)


def home_product(pair, my_index, slots, backs, k, v):
    width = k.shape[1]
    sent = SHARDS * pair
    halves = len(backs)
    return pl.pallas_call(
        functools.partial(home_product_kernel, pair, halves),
        grid=(width // WIDE,),
        in_specs=[
            pl.BlockSpec(memory_space=pltpu.SMEM),
            RESIDENT,
            cols(SLOTS, WIDE),
            cols(SLOTS, WIDE),
        ]
        + [RESIDENT] * halves,
        out_specs=[cols(SLOTS, WIDE), cols(SLOTS, WIDE), cols(TAPS, WIDE)],
        out_shape=[sds((SLOTS, width), BF), sds((SLOTS, width), BF), sds((TAPS, width), F32)],
        scratch_shapes=[pltpu.VMEM((SLOTS, sent), BF)] * halves,
        compiler_params=params(),
        cost_estimate=cost(2 * sent * SLOTS * width, 2 * width * (sent + 5 * SLOTS)),
    )(my_index.reshape(1), *kept(slots), *hbm(k, v), *kept(*backs))


def exchange(pair, rows):
    shards = rows.reshape(SHARDS, pair, rows.shape[1])
    return lax.all_to_all(shards, "seq", split_axis=0, concat_axis=0, tiled=True).reshape(
        rows.shape
    )


def shift(value, steps):
    pairs = [(i, i + steps) for i in range(SHARDS) if 0 <= i + steps < SHARDS]
    return lax.ppermute(value, "seq", pairs)


def swap(value):
    return lax.ppermute(value, "seq", [(i, i ^ 1) for i in range(SHARDS)])


def slot_positions(pair, dest_pos, my_index):
    holders = SHARDS * pair // PAIR
    table = dest_pos.reshape(holders, -1)
    arriving = (table >= 0) & (table // ROWS == my_index)
    row = jnp.arange(table.shape[1], dtype=I32)
    before = (row[:, None] < row[None, :]).astype(BF)
    rank = jnp.dot(arriving.astype(BF), before, preferred_element_type=F32).astype(I32)
    rank = jnp.where(arriving, rank, -1)
    target = table - my_index * ROWS + 1
    order = jnp.arange(PAIR, dtype=I32)
    if pair != PAIR:
        order = (order % pair) * 2 + order // pair
    hit = rank[:, None, :] == order[None, :, None]
    return (jnp.sum(jnp.where(hit, target[:, None, :], 0), axis=2) - 1).reshape(SHARDS * pair)


def layer(pair, others, q_in, k_in, v_in, dest_pos, doc_ids, mr_filter, norm_gain, residual, cotangent):
    my_index = lax.axis_index("seq")
    width = q_in.shape[1]
    wide = step_width(pair)
    gain = norm_gain[None, :]
    shared = pair != PAIR

    slots = send_plan(pair, my_index, dest_pos)
    if shared:
        product_in, product_other, q_other = others
        early = [*hbm(product_in), *kept(product_other)]
        late = [*hbm(q_in), *kept(q_other)]
    else:
        early, late = hbm(k_in, v_in), hbm(q_in)
    sent_rows = pack_arrivals(pair, slots, early, late)
    sent_rows, dest_later, docs_later, slots = lax.optimization_barrier(
        (sent_rows, dest_pos, doc_ids, slots)
    )
    received = exchange(pair, sent_rows)

    pos = slot_positions(pair, dest_later, my_index)
    pos_row = pos[None, :]
    docs_all = jnp.concatenate(
        [jnp.full((TAPS,), -1, I32), docs_later, jnp.full((TAPS,), -2, I32)]
    )
    docs = lax.dynamic_slice_in_dim(docs_all, my_index * ROWS, WIN + TAPS)
    cc, bb = segment_dft(docs[:WIN])
    onward = crossing_dft(docs[TAPS:WIN], docs[WIN:])
    prepared = prepare(cc, bb, *onward)
    received, pos_row, prepared = lax.optimization_barrier((received, pos_row, prepared))
    cc_own, cc_own_t, cc_halo, cc_head_t, bb, bb_t, *onward = prepared

    halo = shift(place_tail(2 * wide, pos_row, received, width), 1)
    q, mix, x, f, sums = forward(
        wide, pos_row, cc_own, cc_own_t, bb, received, mr_filter, residual, cotangent, gain
    )
    mix_head, summed_head, scaled_head, sums = forward_head(
        wide, cc_halo, cc_head_t, halo, f, q, mix, residual, cotangent, gain, sums
    )
    all_sums = [sums] + [
        lax.ppermute(sums, "mp", [(i, (i + k) % 4) for i in range(4)]) for k in (1, 2, 3)
    ]
    head = head_grad(2 * wide, all_sums, q, summed_head, scaled_head)
    d_mix, sent_dq = backward(
        pair, all_sums, pos_row, cc_own, cc_halo, bb_t, q, mix, mix_head, x, halo,
        residual, cotangent, gain,
    )
    sent_dq, from_next = lax.optimization_barrier((sent_dq, shift(head, -1)))
    back_q = exchange(pair, sent_dq)
    normed, d_residual, own_grad = finish(
        wide, all_sums, cc_own, cc_own_t, q, mix, mix_head, f, residual, cotangent, gain, d_mix
    )
    rows = give_back(pair, pos_row, onward, own_grad, from_next, mr_filter)
    sent_dp, d_gain = reduce_parts(pair, back_q, rows, width)
    sent_dp, back_q = lax.optimization_barrier((sent_dp, back_q))
    back_p = exchange(pair, sent_dp)
    backs_q, backs_p = [back_q], [back_p]
    if shared:
        pieces = range(0, back_q.shape[1], piece_cols(pair))
        rows = jnp.concatenate([back_q[:, at : at + WIDE] for at in pieces], axis=1)
        back_p, rows = lax.optimization_barrier((back_p, swap(rows)))
        backs_p = [back_p]
        backs_q.append(rows)
        backs_p.append(swap(back_p))
    d_q_in = home_rows(pair, slots, backs_q, width)
    d_k_in, d_v_in, d_filter = home_product(pair, my_index, slots, backs_p, k_in, v_in)
    return (normed, d_residual, d_q_in, d_k_in, d_v_in, d_filter, d_gain.reshape(width))


def fits_shared(dest_pos):
    chips = dest_pos.reshape(SHARDS // 2, 2 * SLOTS)
    owner = jnp.where(chips >= 0, chips // ROWS, -1)
    load = jnp.sum(
        (owner[:, None, :] == jnp.arange(SHARDS, dtype=I32)[None, :, None]).astype(I32), axis=2
    )
    return jnp.max(load) <= PAIR


def body(q_in, k_in, v_in, dest_pos, *rest):
    product_in = slot_product(k_in, v_in)
    others = (product_in, swap(product_in), swap(q_in))
    return lax.cond(
        fits_shared(dest_pos),
        functools.partial(layer, PAIR // 2),
        functools.partial(layer, PAIR),
        others, q_in, k_in, v_in, dest_pos, *rest,
    )


def solution(mesh):
    return jax.shard_map(
        body,
        mesh=mesh,
        in_specs=(
            P("seq", "mp"),
            P("seq", "mp"),
            P("seq", "mp"),
            P(),
            P(),
            P(None, "mp"),
            P("mp"),
            P("seq", "mp"),
            P("seq", "mp"),
        ),
        out_specs=(
            P("seq", "mp"),
            P("seq", "mp"),
            P("seq", "mp"),
            P("seq", "mp"),
            P("seq", "mp"),
            P(None, "mp"),
            P("mp"),
        ),
        check_vma=False,
    )
```
